32 devices in a mesh: dp: 16 (over z, y, core), ctx: 2 (over x).
Axes of the slice: x: 2, y: 2, z: 4, core: 2. Of those that a mesh axis runs over, the one named last changes fastest.
Arguments:
- tokens: bfloat16 [32, 1024, 1024], P('dp', 'ctx'), may hold values from -6 to 6
- segments: int32 [32, 1024], P('dp'), may hold values from 0 to 7, never falling along the last dimension, each value on 1 to 512 neighbouring positions
- cotangent: float32 [32, 1024, 1024], P('dp', 'ctx'), may hold values from -6 to 6
- w_q: bfloat16 [1024, 1024], P(('dp', 'ctx')), may hold values from -0.1875 to 0.1875
- w_k: bfloat16 [1024, 512], P(('dp', 'ctx')), may hold values from -0.1875 to 0.1875
- w_v: bfloat16 [1024, 512], P(('dp', 'ctx')), may hold values from -0.1875 to 0.1875
- w_o: bfloat16 [1024, 1024], P(('dp', 'ctx')), may hold values from -0.75 to 0.75
- w_gate: bfloat16 [1024, 4608], P(('dp', 'ctx')), may hold values from -0.1875 to 0.1875
- w_up: bfloat16 [1024, 4608], P(('dp', 'ctx')), may hold values from -0.1875 to 0.1875
- w_down: bfloat16 [4608, 1024], P(('dp', 'ctx')), may hold values from -0.09375 to 0.09375
- g_attn: float32 [1024], replicated, may hold values from 0.5 to 1.5
- g_q: float32 [64], replicated, may hold values from 0.5 to 1.5
- g_k: float32 [64], replicated, may hold values from 0.5 to 1.5
- g_ffn: float32 [1024], replicated, may hold values from 0.5 to 1.5
Outputs:
- output: bfloat16 [32, 1024, 1024], P('dp', 'ctx')
- input_grad: float32 [32, 1024, 1024], P('dp', 'ctx')
- grad_w_q: float32 [1024, 1024], P(('dp', 'ctx'))
- grad_w_k: float32 [1024, 512], P(('dp', 'ctx'))
- grad_w_v: float32 [1024, 512], P(('dp', 'ctx'))
- grad_w_o: float32 [1024, 1024], P(('dp', 'ctx'))
- grad_w_gate: float32 [1024, 4608], P(('dp', 'ctx'))
- grad_w_up: float32 [1024, 4608], P(('dp', 'ctx'))
- grad_w_down: float32 [4608, 1024], P(('dp', 'ctx'))
- grad_g_attn: float32 [1024], replicated
- grad_g_q: float32 [64], replicated
- grad_g_k: float32 [64], replicated
- grad_g_ffn: float32 [1024], replicated
The draws below stay inside these ranges and needn't reach their ends.
Inputs may be any that keep to these rules, and one draw needn't show every extreme that they name: `segments`: segment numbers never fall along a sequence; each document has 1 to 512 tokens, and some document has exactly 512.
All inputs are finite; a program needn't handle non-finite values.
Results may differ from the reference program's by a relative error of at most 0.018.
Values may be sent and summed in bfloat16 or wider, within the bound.
A program may use at most 216 MiB of HBM per device.

```python
import math
import jax
import jax.numpy as jnp
import numpy as np
from jax import lax

D = 1024
H = 16
KVH = 8
HD = 64
FF = 4608
LENGTH = 1024
DOCS = 8
QW = 1024
KW = 512
SEQS = 32


def block_levels(stream_key, dims, pieces, low, high):
    loudness = 1.0
    for dim, blocks in pieces:
        draws = jax.random.uniform(jax.random.fold_in(jax.random.fold_in(stream_key, 6), dim), (blocks,), jnp.float32, low / len(pieces), high / len(pieces))
        loudness = loudness * jnp.repeat(jnp.exp(draws), dims[dim] // blocks).reshape((-1,) + (1,) * (len(dims) - 1 - dim))
    return loudness


def length_profile(count, total, limit, lean):
    loads = [(1 << 20) // math.isqrt(standing ** lean) + 1 for standing in range(2, count + 1)]
    rest, given = total - limit - (count - 1), [1] * (count - 1)
    while rest > 0:
        movable = [i for i in range(count - 1) if given[i] < limit]
        whole, remaining = sum([loads[i] for i in movable]), rest
        for i in movable:
            addition = min(limit - given[i], max(1, remaining * loads[i] // whole), rest)
            given[i] = given[i] + addition
            rest = rest - addition
    return np.array([limit] + given)


def ragged(key, amount, total, reach, skew):
    if amount == 2:
        one = jax.random.randint(key, (), max(1, total - reach), min(reach, total - 1) + 1)
        return jnp.stack([one, total - one])
    tallies = jnp.asarray(length_profile(amount, total, reach, skew), jnp.int32)
    twos = (amount - 1) // 2
    donor, sink = tallies[1:1 + 2 * twos:2], tallies[2:2 + 2 * twos:2]
    room = jnp.minimum(donor - 1, reach - sink)
    shifted = jax.random.randint(jax.random.fold_in(key, 1), (twos,), 0, 1 << 20) % (room + 1)
    tallies = tallies.at[1:1 + 2 * twos:2].set(donor - shifted).at[2:2 + 2 * twos:2].set(sink + shifted)
    return tallies[jax.random.permutation(jax.random.fold_in(key, 2), amount)]


def noise(rng, shape, scale, limit, cuts=(), kind=jnp.bfloat16):
    loudness = block_levels(rng, shape, cuts, -0.22, 0.18) if cuts else 1.0
    entries = jax.random.normal(rng, shape, jnp.float32) * scale * loudness
    return jnp.minimum(jnp.maximum(entries, -limit), limit).astype(kind)


def setup_inputs(seed: int = 0) -> dict:
    arg_keys = jax.random.split(jax.random.key(seed), 15)
    return {
        "tokens": noise(arg_keys[0], (SEQS, LENGTH, D), 1.0, 6.0, ((0, 16), (1, 2))),
        "segments": jax.vmap(lambda own: jnp.searchsorted(jnp.cumsum(ragged(own, DOCS, LENGTH, LENGTH // 2, 2)), jnp.arange(LENGTH), side="right"))(jax.random.split(arg_keys[1], SEQS)).reshape((SEQS, LENGTH)).astype(jnp.int32),
        "cotangent": noise(arg_keys[2], (SEQS, LENGTH, D), 1.0, 6.0, ((0, 16), (1, 2)), jnp.float32),
        "w_q": noise(arg_keys[3], (D, QW), D ** -0.5, 0.1875, ((0, 32),)),
        "w_k": noise(arg_keys[4], (D, KW), D ** -0.5, 0.1875, ((0, 32),)),
        "w_v": noise(arg_keys[5], (D, KW), D ** -0.5, 0.1875, ((0, 32),)),
        "w_o": noise(arg_keys[6], (QW, D), (QW // 16) ** -0.5, 0.75, ((0, 32),)),
        "w_gate": noise(arg_keys[7], (D, FF), D ** -0.5, 0.1875, ((0, 32),)),
        "w_up": noise(arg_keys[8], (D, FF), D ** -0.5, 0.1875, ((0, 32),)),
        "w_down": noise(arg_keys[9], (FF, D), FF ** -0.5, 0.09375, ((0, 32),)),
        "g_attn": jnp.clip(1.0 + 0.1 * jax.random.normal(arg_keys[10], (D,), jnp.float32), 0.5, 1.5),
        "g_q": jnp.clip(1.0 + 0.1 * jax.random.normal(arg_keys[11], (HD,), jnp.float32), 0.5, 1.5),
        "g_k": jnp.clip(1.0 + 0.1 * jax.random.normal(arg_keys[12], (HD,), jnp.float32), 0.5, 1.5),
        "g_ffn": jnp.clip(1.0 + 0.1 * jax.random.normal(arg_keys[13], (D,), jnp.float32), 0.5, 1.5),
    }


HIGH = lax.Precision.HIGHEST
epsilon = 1e-05
rope_base = 1000000.0

@jax.custom_vjp
def low(v):
    return lax.optimization_barrier(v.astype(jnp.bfloat16)).astype(jnp.float32)

@jax.custom_vjp
def low_back(v):
    return v

def low_keep(v):
    return (low(v), None)

def low_pass(kept, grad):
    return (grad,)

def back_keep(v):
    return (v, None)

def back_low(kept, grad):
    return (low(grad),)
low.defvjp(low_keep, low_pass)
low_back.defvjp(back_keep, back_low)

def rms_norm(field, gain):
    return field * lax.rsqrt(lax.optimization_barrier(jnp.mean(field * field, axis=-1, keepdims=True)) + epsilon) * gain

def doc_positions(seg_ids):
    token_index = jnp.arange(seg_ids.shape[0], dtype=jnp.int32)
    new_doc = jnp.concatenate([jnp.ones((1,), dtype=jnp.bool_), seg_ids[1:] != seg_ids[:-1]])
    doc_start = lax.cummax(jnp.where(new_doc, token_index, jnp.zeros_like(token_index)), axis=0)
    return token_index - doc_start

def rope_tables(positions):
    frequency = rope_base ** (-jnp.arange(0, HD, 2, dtype=jnp.float32) / HD)
    angles = positions.astype(jnp.float32)[:, None] * frequency[None, :]
    angles = jnp.concatenate([angles, angles], axis=-1)
    return (jnp.cos(angles), jnp.sin(angles))

def rotate(field, cos_table, sin_table):
    half_dim = field.shape[-1] // 2
    turned = jnp.concatenate([-field[..., half_dim:], field[..., :half_dim]], axis=-1)
    return field * cos_table[:, None, :] + turned * sin_table[:, None, :]

def attention(queries, all_keys, all_values, seg_ids):
    seq_length = queries.shape[0]
    block_size = min(512, seq_length)
    group_size = H // KVH
    score_scale = HD ** (-0.5)
    key_pos = jnp.arange(seq_length, dtype=jnp.int32)

    def one_block(micro_item):
        q_block, block_start = micro_item
        query_pos = block_start + jnp.arange(block_size, dtype=jnp.int32)
        seg_rows = lax.dynamic_slice_in_dim(seg_ids, block_start, block_size, 0)
        live_mask = (key_pos[None, :] <= query_pos[:, None]) & (seg_rows[:, None] == seg_ids[None, :])
        grouped = q_block.reshape(block_size, KVH, group_size, HD)
        raw_scores = jnp.einsum('qkgd,tkd->kgqt', grouped, all_keys, precision=HIGH) * score_scale
        scores = low_back(jnp.where(live_mask, raw_scores, -1000000000.0))
        row_top = lax.optimization_barrier(jnp.max(scores, axis=-1, keepdims=True))
        expo = jnp.exp(scores - row_top)
        attn_probs = low(expo / lax.optimization_barrier(jnp.sum(expo, axis=-1, keepdims=True)))
        attn_mix = jnp.einsum('kgqt,tkd->qkgd', attn_probs, all_values, precision=HIGH)
        return attn_mix.reshape(block_size, H * HD)
    block_starts = jnp.arange(seq_length // block_size, dtype=jnp.int32) * block_size
    q_blocks = queries.reshape(seq_length // block_size, block_size, H, HD)
    result = lax.map(jax.checkpoint(one_block), (q_blocks, block_starts))
    return result.reshape(seq_length, H * HD)

def block_layer(x_float, params, seg_ids):
    w_q, w_k, w_v, w_o, w_gate, w_up, w_down, g_attn, g_q, g_k, g_ffn = params
    seq_length = x_float.shape[0]
    normed = low(rms_norm(x_float, g_attn))
    q_raw = low_back(jnp.dot(normed, w_q, precision=HIGH)).reshape(seq_length, H, HD)
    k_raw = low_back(jnp.dot(normed, w_k, precision=HIGH)).reshape(seq_length, KVH, HD)
    v_raw = low_back(jnp.dot(normed, w_v, precision=HIGH)).reshape(seq_length, KVH, HD)
    cos_table, sin_table = rope_tables(doc_positions(seg_ids))
    queries = low(rotate(rms_norm(q_raw, g_q), cos_table, sin_table))
    all_keys = low(rotate(rms_norm(k_raw, g_k), cos_table, sin_table))
    all_values = low(v_raw)
    attended = low_back(low(attention(queries, all_keys, all_values, seg_ids)))
    hidden = x_float + low_back(jnp.dot(attended, w_o, precision=HIGH))
    normed_two = low(rms_norm(hidden, g_ffn))
    gate_out = low_back(jnp.dot(normed_two, w_gate, precision=HIGH))
    up_out = low_back(jnp.dot(normed_two, w_up, precision=HIGH))
    hidden_act = low(jax.nn.silu(gate_out) * up_out)
    return hidden + low_back(jnp.dot(hidden_act, w_down, precision=HIGH))

def reference(tokens, segments, cotangent, w_q, w_k, w_v, w_o, w_gate, w_up, w_down, g_attn, g_q, g_k, g_ffn):
    params = (w_q.astype(jnp.float32), w_k.astype(jnp.float32), w_v.astype(jnp.float32), w_o.astype(jnp.float32), w_gate.astype(jnp.float32), w_up.astype(jnp.float32), w_down.astype(jnp.float32), g_attn.astype(jnp.float32), g_q.astype(jnp.float32), g_k.astype(jnp.float32), g_ffn.astype(jnp.float32))

    def seq_step(totals, micro_item):
        tok_seq, seg_ids, grad_seq = micro_item

        def layer_fn(x_float, param_set):
            return block_layer(x_float, param_set, seg_ids)
        block_out, pullback = jax.vjp(layer_fn, tok_seq.astype(jnp.float32), params)
        grad_in, grad_params = pullback(grad_seq.astype(jnp.float32))
        totals = tuple((left + right for left, right in zip(totals, grad_params)))
        return (totals, (block_out.astype(jnp.bfloat16), grad_in))
    start_totals = tuple((jnp.zeros(p.shape, jnp.float32) for p in params))
    gradients, (outputs, input_grads) = lax.scan(seq_step, start_totals, (tokens, segments, cotangent))
    return (outputs, input_grads, gradients[0], gradients[1], gradients[2], gradients[3], gradients[4], gradients[5], gradients[6], gradients[7], gradients[8], gradients[9], gradients[10])
```

```python
import functools

import jax
import jax.numpy as jnp
from jax import lax
from jax.experimental import pallas as pl
from jax.experimental.pallas import tpu as pltpu
from jax.sharding import PartitionSpec as P

epsilon = 1e-05
rope_base = 1000000.0
AXES = ("dp", "ctx")
BF = jnp.bfloat16
F32 = jnp.float32
LANES = 128
VMEM_LIMIT = 56 * 2**20
NN = (((1,), (0,)), ((), ()))
NT = (((1,), (1,)), ((), ()))
TN = (((0,), (0,)), ((), ()))


def mm(a, b, dims=NN):
    return lax.dot_general(a, b, dims, preferred_element_type=F32)


def params(semantics=None):
    return pltpu.CompilerParams(
        vmem_limit_bytes=VMEM_LIMIT,
        dimension_semantics=semantics,
    )


def resident(shape):
    zeros = (0,) * len(shape)
    return pl.BlockSpec(shape, lambda *_: zeros, pipeline_mode=pl.Buffered(1))


def largest_block(size, most):
    return max(b for b in range(1, min(size, most) + 1) if size % b == 0)


def head_sum(field, ones):
    wide = ones.shape[0]
    high = field.astype(BF)
    low = (field - high.astype(F32)).astype(BF)
    parts = [
        mm(high[:, c : c + wide], ones) + mm(low[:, c : c + wide], ones)
        for c in range(0, field.shape[1], wide)
    ]
    return jnp.concatenate(parts, axis=1)


def swap_halves(field, head):
    half = head // 2
    width = field.shape[1]
    lane = lax.broadcasted_iota(jnp.int32, field.shape, 1)
    return jnp.where(
        lane % head < half,
        pltpu.roll(field, width - half, 1),
        pltpu.roll(field, half, 1),
    )


def spread(table, width):
    return jnp.concatenate([table] * (width // table.shape[1]), axis=1)


def qkv_kernel(
    q_width, kv_width, head, scale,
    x_ref, w_ref, g_ref, gqk_ref, cos_ref, sin_ref, ones_ref,
    normed_ref, q_ref, kv_ref, raw_ref,
):
    x = x_ref[...].astype(F32)
    inverse = lax.rsqrt(jnp.mean(x * x, axis=-1, keepdims=True) + epsilon)
    normed = (x * inverse * g_ref[...]).astype(BF)
    normed_ref[...] = normed
    qk = q_width + kv_width
    ones = ones_ref[...]
    wide = ones.shape[0]
    cos = spread(cos_ref[...], wide)
    sin = spread(sin_ref[...], wide)
    for c in range(0, qk, wide):
        raw = mm(normed, w_ref[:, c : c + wide])
        raw_ref[:, c : c + wide] = raw
        inv = lax.rsqrt(head_sum(raw * raw, ones) * (1.0 / head) + epsilon)
        field = raw * inv * gqk_ref[:, c : c + wide]
        turned = (field * cos + swap_halves(field, head) * sin).astype(BF)
        if c < q_width:
            q_ref[:, c : c + wide] = turned * jnp.asarray(scale, BF)
        else:
            kv_ref[:, c - q_width : c - q_width + wide] = turned
    kv_ref[:, kv_width:] = mm(normed, w_ref[:, qk:]).astype(BF)


def qkv_call(x, w, g, gqk, cos, sin, ones, q_width, kv_width, head):
    total, width = x.shape
    block = largest_block(total, 256)
    qk = q_width + kv_width

    def rows(n):
        return pl.BlockSpec((block, n), lambda i: (i, 0))

    return pl.pallas_call(
        functools.partial(qkv_kernel, q_width, kv_width, head, head ** (-0.5)),
        grid=(total // block,),
        in_specs=[
            rows(width), resident(w.shape), resident(g.shape), resident(gqk.shape),
            rows(LANES), rows(LANES), resident(ones.shape),
        ],
        out_specs=[rows(width), rows(q_width), rows(2 * kv_width), rows(qk)],
        out_shape=[
            jax.ShapeDtypeStruct((total, width), BF),
            jax.ShapeDtypeStruct((total, q_width), BF),
            jax.ShapeDtypeStruct((total, 2 * kv_width), BF),
            jax.ShapeDtypeStruct((total, qk), F32),
        ],
        compiler_params=params(),
        name="qkv_rope",
    )(x, w, g, gqk, cos, sin, ones)


def pad_head(pair, odd, fill):
    lane = lax.broadcasted_iota(jnp.int32, pair.shape, 1)
    if odd:
        pair = pltpu.roll(pair, LANES // 2, 1)
    return jnp.where(lane < LANES // 2, pair, jnp.asarray(fill, pair.dtype))


def attend_kernel(
    block_q, block_k, heads,
    low_ref, start_ref, q_ref, k_ref, v_ref, first_ref,
    out_ref, total_ref, k_scr, v_scr,
):
    s = pl.program_id(0)
    rows = q_ref.shape[1]
    length = k_ref.shape[1]
    start = start_ref[0]
    half = LANES // 2
    for h in range(heads):
        c = h // 2 * LANES
        k_scr[h] = pad_head(k_ref[0, :, c : c + LANES].astype(F32), h % 2, 0).astype(BF)
        v_scr[h] = pad_head(v_ref[0, :, c : c + LANES].astype(F32), h % 2, 1).astype(BF)
    lane = lax.broadcasted_iota(jnp.int32, (block_q, LANES), 1)
    key_lane = lax.broadcasted_iota(jnp.int32, (2 * block_q, block_k), 1)
    row = lax.broadcasted_iota(jnp.int32, (2 * block_q, 1), 0) % block_q

    def q_step(i, carry):
        at = pl.multiple_of(i * block_q, block_q)
        first = first_ref[0, pl.ds(at, block_q), :]
        first = jnp.concatenate([first, first], axis=0)
        last = row + (start + at)
        queries = []
        for h in range(heads):
            pair = q_ref[0, pl.ds(at, block_q), h * LANES : (h + 1) * LANES].astype(F32)
            queries.append(
                jnp.concatenate([pad_head(pair, 0, 0), pad_head(pair, 1, 0)], axis=0).astype(BF)
            )

        def k_step(j, sums):
            key_at = pl.multiple_of(j * block_k, block_k)
            key = key_lane + key_at
            live = (key >= first) & (key <= last)
            new = []
            for h in range(heads):
                scores = mm(queries[h], k_scr[h, pl.ds(key_at, block_k), :], NT)
                expo = jnp.where(live, jnp.exp(scores), 0.0).astype(BF)
                new.append(sums[h] + mm(expo, v_scr[h, pl.ds(key_at, block_k), :]))
            return tuple(new)

        end = (start + at + block_q - 1) // block_k + 1
        sums = lax.fori_loop(
            low_ref[s, i], end, k_step,
            tuple(jnp.zeros((2 * block_q, LANES), F32) for _ in range(heads)),
        )
        for h in range(heads):
            even, odd = sums[h][:block_q], sums[h][block_q:]
            both = jnp.where(lane < half, even, pltpu.roll(odd, half, 1))
            tot = jnp.where(lane < half, pltpu.roll(even, half, 1), odd)
            cols = slice(h * LANES, (h + 1) * LANES)
            out_ref[0, pl.ds(at, block_q), cols] = both / tot
            total_ref[0, pl.ds(at, block_q), cols] = tot
        return carry

    lax.fori_loop(0, rows // block_q, q_step, 0)


def attend_call(q, kv, first, low, start, block_q, block_k):
    seqs, rows, q_width = q.shape
    length = kv.shape[1]
    kv_width = kv.shape[2] // 2
    kv_heads = q_width // LANES
    heads = largest_block(kv_heads, 4)
    steps = kv_heads // heads
    half = LANES // 2
    spec_q = pl.BlockSpec((1, rows, heads * LANES), lambda s, p, *_: (s, 0, p))
    return pl.pallas_call(
        functools.partial(attend_kernel, block_q, block_k, heads),
        grid_spec=pltpu.PrefetchScalarGridSpec(
            num_scalar_prefetch=2,
            grid=(seqs, steps),
            in_specs=[
                spec_q,
                pl.BlockSpec((1, length, heads * half), lambda s, p, *_: (s, 0, p)),
                pl.BlockSpec((1, length, heads * half), lambda s, p, *_: (s, 0, p + steps)),
                pl.BlockSpec((1, rows, 1), lambda s, p, *_: (s, 0, 0)),
            ],
            out_specs=[spec_q, spec_q],
            scratch_shapes=[
                pltpu.VMEM((heads, length, LANES), BF),
                pltpu.VMEM((heads, length, LANES), BF),
            ],
        ),
        out_shape=[jax.ShapeDtypeStruct(q.shape, F32)] * 2,
        compiler_params=params(),
        name="attend",
    )(low, start, q, kv, kv, first)


def attend_back_kernel(
    block_q, block_k, heads,
    low_ref, start_ref, q_ref, do_ref, de_ref, k_ref, v_ref, first_ref,
    dq_ref, dk_ref, dv_ref, k_scr, v_scr, dk_scr, dv_scr,
):
    s = pl.program_id(0)
    rows = q_ref.shape[1]
    length = k_ref.shape[1]
    start = start_ref[0]
    half = LANES // 2
    for h in range(heads):
        c = h // 2 * LANES
        k_scr[h] = pad_head(k_ref[0, :, c : c + LANES].astype(F32), h % 2, 0).astype(BF)
        v_scr[h] = pad_head(v_ref[0, :, c : c + LANES].astype(F32), h % 2, 1).astype(BF)
    dk_scr[...] = jnp.zeros_like(dk_scr)
    dv_scr[...] = jnp.zeros_like(dv_scr)
    lane = lax.broadcasted_iota(jnp.int32, (block_q, LANES), 1)
    key_row = lax.broadcasted_iota(jnp.int32, (block_k, 2 * block_q), 0)
    column = lax.broadcasted_iota(jnp.int32, (1, 2 * block_q), 1) % block_q

    def tail(pair, odd, delta):
        if odd:
            pair = pltpu.roll(pair, half, 1)
        else:
            delta = pltpu.roll(delta, half, 1)
        part0 = delta.astype(BF).astype(F32)
        part1 = (delta - part0).astype(BF).astype(F32)
        part2 = delta - part0 - part1
        rest = jnp.where(
            lane == half, part0, jnp.where(lane == half + 1, part1, jnp.where(lane == half + 2, part2, 0.0))
        )
        return jnp.where(lane < half, pair, -rest)

    def q_step(i, carry):
        at = pl.multiple_of(i * block_q, block_q)
        first = first_ref[0, :, pl.ds(at, block_q)]
        first = jnp.concatenate([first, first], axis=1)
        last = column + (start + at)
        queries, grads = [], []
        for h in range(heads):
            cols = slice(h * LANES, (h + 1) * LANES)
            pair = q_ref[0, pl.ds(at, block_q), cols].astype(F32)
            queries.append(
                jnp.concatenate([pad_head(pair, 0, 0), pad_head(pair, 1, 0)], axis=0).astype(BF)
            )
            pair = do_ref[0, pl.ds(at, block_q), cols].astype(F32)
            delta = de_ref[0, pl.ds(at, block_q), cols]
            grads.append(
                jnp.concatenate([tail(pair, 0, delta), tail(pair, 1, delta)], axis=0).astype(BF)
            )

        def k_step(j, sums):
            key_at = pl.multiple_of(j * block_k, block_k)
            key = key_row + key_at
            live = (key >= first) & (key <= last)
            new = []
            for h in range(heads):
                k = k_scr[h, pl.ds(key_at, block_k), :]
                v = v_scr[h, pl.ds(key_at, block_k), :]
                scores = mm(k, queries[h], NT)
                expo = jnp.where(live, jnp.exp(scores), 0.0)
                change = mm(v, grads[h], NT)
                d_scores = (expo * change).astype(BF)
                dv_scr[h, pl.ds(key_at, block_k), :] += mm(expo.astype(BF), grads[h])
                dk_scr[h, pl.ds(key_at, block_k), :] += mm(d_scores, queries[h])
                new.append(sums[h] + mm(d_scores, k, TN))
            return tuple(new)

        end = (start + at + block_q - 1) // block_k + 1
        sums = lax.fori_loop(
            low_ref[s, i], end, k_step,
            tuple(jnp.zeros((2 * block_q, LANES), F32) for _ in range(heads)),
        )
        for h in range(heads):
            even, odd = sums[h][:block_q], sums[h][block_q:]
            cols = slice(h * LANES, (h + 1) * LANES)
            dq_ref[0, pl.ds(at, block_q), cols] = jnp.where(
                lane < half, even, pltpu.roll(odd, half, 1)
            )
        return carry

    lax.fori_loop(0, rows // block_q, q_step, 0)
    wide = lax.broadcasted_iota(jnp.int32, (length, LANES), 1)
    for h in range(0, heads, 2):
        cols = slice(h // 2 * LANES, (h // 2 + 1) * LANES)
        for grad, scr in ((dk_ref, dk_scr), (dv_ref, dv_scr)):
            grad[0, :, cols] = jnp.where(
                wide < half, scr[h], pltpu.roll(scr[h + 1], half, 1)
            ).astype(BF)


def attend_back_call(q, d_out, delta, kv, first, low, start, block_q, block_k):
    seqs, rows, q_width = q.shape
    length = kv.shape[1]
    kv_width = kv.shape[2] // 2
    kv_heads = q_width // LANES
    heads = largest_block(kv_heads, 4)
    steps = kv_heads // heads
    half = LANES // 2
    spec_q = pl.BlockSpec((1, rows, heads * LANES), lambda s, p, *_: (s, 0, p))
    spec_kv = pl.BlockSpec((1, length, heads * half), lambda s, p, *_: (s, 0, p))
    return pl.pallas_call(
        functools.partial(attend_back_kernel, block_q, block_k, heads),
        grid_spec=pltpu.PrefetchScalarGridSpec(
            num_scalar_prefetch=2,
            grid=(seqs, steps),
            in_specs=[
                spec_q, spec_q, spec_q, spec_kv,
                pl.BlockSpec((1, length, heads * half), lambda s, p, *_: (s, 0, p + steps)),
                pl.BlockSpec((1, 1, rows), lambda s, p, *_: (s, 0, 0)),
            ],
            out_specs=[spec_q, spec_kv, spec_kv],
            scratch_shapes=[
                pltpu.VMEM((heads, length, LANES), BF),
                pltpu.VMEM((heads, length, LANES), BF),
                pltpu.VMEM((heads, length, LANES), F32),
                pltpu.VMEM((heads, length, LANES), F32),
            ],
        ),
        out_shape=[
            jax.ShapeDtypeStruct(q.shape, F32),
            jax.ShapeDtypeStruct((seqs, length, kv_width), BF),
            jax.ShapeDtypeStruct((seqs, length, kv_width), BF),
        ],
        compiler_params=params(),
        name="attend_back",
    )(low, start, q, d_out, delta, kv, kv, first)


def hidden_kernel(a_ref, w_ref, x_ref, g_ref, att_ref, hidden_ref, normed_ref):
    attended = a_ref[...].astype(BF)
    att_ref[...] = attended
    hidden = x_ref[...].astype(F32) + mm(attended, w_ref[...])
    hidden_ref[...] = hidden
    inverse = lax.rsqrt(jnp.mean(hidden * hidden, axis=-1, keepdims=True) + epsilon)
    normed_ref[...] = (hidden * inverse * g_ref[...]).astype(BF)


def hidden_call(mixed, w_o, x, g):
    total, width = x.shape
    q_width = mixed.shape[1]
    block = largest_block(total, 256)

    def rows(n):
        return pl.BlockSpec((block, n), lambda i: (i, 0))

    return pl.pallas_call(
        hidden_kernel,
        grid=(total // block,),
        in_specs=[rows(q_width), resident(w_o.shape), rows(width), resident(g.shape)],
        out_specs=[rows(q_width), rows(width), rows(width)],
        out_shape=[
            jax.ShapeDtypeStruct((total, q_width), BF),
            jax.ShapeDtypeStruct((total, width), F32),
            jax.ShapeDtypeStruct((total, width), BF),
        ],
        compiler_params=params(),
        name="hidden",
    )(mixed, w_o, x, g)


def ffn_kernel(
    block_t,
    n_ref, c_ref, wg_ref, wu_ref, wd_ref,
    out_ref, dn_ref, gg_ref, gu_ref, gd_ref,
    n_scr, c_scr, act_scr, dg_scr, du_scr,
):
    total, width = n_ref.shape
    chunk = wg_ref.shape[1]

    @pl.when(pl.program_id(0) == 0)
    def _():
        c_scr[...] = c_ref[...].astype(BF)
        n_scr[...] = n_ref[...].T
        out_ref[...] = jnp.zeros_like(out_ref)
        dn_ref[...] = jnp.zeros_like(dn_ref)

    def t_step(i, carry):
        at = pl.ds(pl.multiple_of(i * block_t, block_t), block_t)
        normed = n_ref[at, :]
        gate = mm(normed, wg_ref[...])
        up = mm(normed, wu_ref[...])
        d_act = mm(c_scr[at, :], wd_ref[...], NT)
        sig = 1.0 / (1.0 + jnp.exp(-gate))
        silu = gate * sig
        act = (silu * up).astype(BF)
        d_gate = (d_act * up * (sig * (1.0 + gate - silu))).astype(BF)
        d_up = (d_act * silu).astype(BF)
        act_scr[at, :] = act
        dg_scr[at, :] = d_gate
        du_scr[at, :] = d_up
        out_ref[at, :] += mm(act, wd_ref[...])
        dn_ref[at, :] += mm(d_gate, wg_ref[...], NT) + mm(d_up, wu_ref[...], NT)
        return carry

    lax.fori_loop(0, total // block_t, t_step, 0)

    def d_step(i, carry):
        at = pl.ds(pl.multiple_of(i * 256, 256), 256)
        normed = n_scr[at, :]
        gg_ref[at, :] = mm(normed, dg_scr[...]).astype(BF)
        gu_ref[at, :] = mm(normed, du_scr[...]).astype(BF)
        return carry

    lax.fori_loop(0, width // 256, d_step, 0)
    for c in range(0, chunk, 256):
        gd_ref[c : c + 256, :] = mm(act_scr[:, c : c + 256], c_scr[...], TN).astype(BF)


def ffn_call(normed, cotangent, w_gate, w_up, w_down):
    total, width = normed.shape
    hidden = w_gate.shape[1]
    chunk = largest_block(hidden, 512)
    block_t = largest_block(total, 256)
    cols = pl.BlockSpec((width, chunk), lambda i: (0, i))
    rows = pl.BlockSpec((chunk, width), lambda i: (i, 0))
    return pl.pallas_call(
        functools.partial(ffn_kernel, block_t),
        grid=(hidden // chunk,),
        in_specs=[resident(normed.shape), resident(normed.shape), cols, cols, rows],
        out_specs=[resident(normed.shape), resident(normed.shape), cols, cols, rows],
        out_shape=[
            jax.ShapeDtypeStruct((total, width), F32),
            jax.ShapeDtypeStruct((total, width), F32),
            jax.ShapeDtypeStruct(w_gate.shape, BF),
            jax.ShapeDtypeStruct(w_gate.shape, BF),
            jax.ShapeDtypeStruct(w_down.shape, BF),
        ],
        scratch_shapes=[
            pltpu.VMEM((width, total), BF),
            pltpu.VMEM((total, width), BF),
            pltpu.VMEM((total, chunk), BF),
            pltpu.VMEM((total, chunk), BF),
            pltpu.VMEM((total, chunk), BF),
        ],
        compiler_params=params(),
        cost_estimate=pl.CostEstimate(
            flops=18 * total * width * hidden, bytes_accessed=12 * width * hidden, transcendentals=0
        ),
        name="ffn",
    )(normed, cotangent, w_gate, w_up, w_down)


def middle_kernel(
    head,
    f_ref, dn_ref, h_ref, c_ref, g_ref, w_ref, o_ref, l_ref, ones_ref,
    out_ref, dh_ref, low_ref, do_ref, de_ref, gain_ref,
):
    @pl.when(pl.program_id(0) == 0)
    def _():
        gain_ref[...] = jnp.zeros_like(gain_ref)

    hidden = h_ref[...]
    out_ref[...] = (hidden + f_ref[...]).astype(BF)
    inverse = lax.rsqrt(jnp.mean(hidden * hidden, axis=-1, keepdims=True) + epsilon)
    incoming = dn_ref[...]
    unit = hidden * inverse
    gain_ref[...] += jnp.sum(unit * incoming, axis=0, keepdims=True)
    scaled = incoming * g_ref[...]
    shared = jnp.mean(unit * scaled, axis=-1, keepdims=True)
    d_hidden = c_ref[...] + inverse * (scaled - unit * shared)
    dh_ref[...] = d_hidden
    low = d_hidden.astype(BF)
    low_ref[...] = low
    ones = ones_ref[...]
    wide = ones.shape[0]
    for c in range(0, o_ref.shape[1], wide):
        cols = slice(c, c + wide)
        d_att = mm(low, w_ref[cols, :], NT)
        ratio = 1.0 / l_ref[:, cols]
        do_ref[:, cols] = (d_att * ratio).astype(BF)
        de_ref[:, cols] = head_sum(d_att * o_ref[:, cols], ones) * ratio


def middle_call(ffn, d_normed, hidden, cotangent, g, w_o, mixed, totals, ones, head):
    total, width = hidden.shape
    q_width = mixed.shape[1]
    block = largest_block(total, 256)

    def rows(n):
        return pl.BlockSpec((block, n), lambda i: (i, 0))

    return pl.pallas_call(
        functools.partial(middle_kernel, head),
        grid=(total // block,),
        in_specs=[
            rows(width), rows(width), rows(width), rows(width), resident(g.shape),
            resident(w_o.shape), rows(q_width), rows(q_width), resident(ones.shape),
        ],
        out_specs=[
            rows(width), rows(width), rows(width), rows(q_width), rows(q_width), resident((1, width)),
        ],
        out_shape=[
            jax.ShapeDtypeStruct((total, width), BF),
            jax.ShapeDtypeStruct((total, width), F32),
            jax.ShapeDtypeStruct((total, width), BF),
            jax.ShapeDtypeStruct((total, q_width), BF),
            jax.ShapeDtypeStruct((total, q_width), F32),
            jax.ShapeDtypeStruct((1, width), F32),
        ],
        compiler_params=params(),
        name="middle",
    )(ffn, d_normed, hidden, cotangent, g, w_o, mixed, totals, ones)


def last_kernel(
    q_width, kv_width, head, scale,
    dq_ref, dk_ref, dv_ref, raw_ref, gqk_ref, cos_ref, sin_ref, ones_ref, w_ref, x_ref, g_ref, dh_ref,
    d_ref, in_ref, gain_ref, gq_ref, gk_ref,
):
    @pl.when(pl.program_id(0) == 0)
    def _():
        gain_ref[...] = jnp.zeros_like(gain_ref)
        gq_ref[...] = jnp.zeros_like(gq_ref)
        gk_ref[...] = jnp.zeros_like(gk_ref)

    ones = ones_ref[...]
    wide = ones.shape[0]
    cos = spread(cos_ref[...], wide)
    sin = spread(sin_ref[...], wide)
    qk = q_width + kv_width
    for c in range(0, qk, wide):
        cols = slice(c, c + wide)
        if c < q_width:
            grad, total = dq_ref[:, cols] * scale, gq_ref
        else:
            grad, total = dk_ref[:, c - q_width : c - q_width + wide].astype(F32), gk_ref
        grad = grad * cos + swap_halves(grad * sin, head)
        raw = raw_ref[:, cols]
        inv = lax.rsqrt(head_sum(raw * raw, ones) * (1.0 / head) + epsilon)
        unit = raw * inv
        gained = jnp.sum(unit * grad, axis=0, keepdims=True)
        total[...] += sum(gained[:, i : i + LANES] for i in range(0, wide, LANES))
        scaled = grad * gqk_ref[:, cols]
        shared = head_sum(unit * scaled, ones) * (1.0 / head)
        d_ref[:, cols] = (inv * (scaled - unit * shared)).astype(BF)
    d_ref[:, qk:] = dv_ref[...].astype(BF)
    d_normed = mm(d_ref[...], w_ref[...], NT)
    x = x_ref[...].astype(F32)
    inverse = lax.rsqrt(jnp.mean(x * x, axis=-1, keepdims=True) + epsilon)
    unit = x * inverse
    gain_ref[...] += jnp.sum(unit * d_normed, axis=0, keepdims=True)
    scaled = d_normed * g_ref[...]
    shared = jnp.mean(unit * scaled, axis=-1, keepdims=True)
    in_ref[...] = dh_ref[...] + inverse * (scaled - unit * shared)


def last_call(dq, dk, dv, raw, gqk, cos, sin, ones, w, x, g, d_hidden, head):
    total, width = x.shape
    q_width, kv_width = dq.shape[1], dk.shape[1]
    block = largest_block(total, 256)

    def rows(n):
        return pl.BlockSpec((block, n), lambda i: (i, 0))

    return pl.pallas_call(
        functools.partial(last_kernel, q_width, kv_width, head, head ** (-0.5)),
        grid=(total // block,),
        in_specs=[
            rows(q_width), rows(kv_width), rows(kv_width), rows(q_width + kv_width),
            resident(gqk.shape), rows(LANES), rows(LANES), resident(ones.shape),
            resident(w.shape), rows(width), resident(g.shape), rows(width),
        ],
        out_specs=[
            rows(w.shape[1]), rows(width),
            resident((1, width)), resident((1, LANES)), resident((1, LANES)),
        ],
        out_shape=[
            jax.ShapeDtypeStruct((total, w.shape[1]), BF),
            jax.ShapeDtypeStruct((total, width), F32),
            jax.ShapeDtypeStruct((1, width), F32),
            jax.ShapeDtypeStruct((1, LANES), F32),
            jax.ShapeDtypeStruct((1, LANES), F32),
        ],
        compiler_params=params(),
        name="last",
    )(dq, dk, dv, raw, gqk, cos, sin, ones, w, x, g, d_hidden)


def per_device(
    tokens, segments, cotangent, w_q, w_k, w_v, w_o, w_gate, w_up, w_down, g_attn, g_q, g_k, g_ffn
):
    seqs, rows, width = tokens.shape
    length = segments.shape[1]
    head = g_q.shape[0]
    q_width, kv_width = w_q.shape[1], w_k.shape[1]
    kv_heads = kv_width // head
    q_heads = q_width // head
    total = seqs * rows
    row_start = lax.axis_index("ctx") * rows

    def fetch(weight):
        return lax.all_gather(weight, AXES, axis=0, tiled=True)

    w_qkv = fetch(jnp.concatenate([w_q, w_k, w_v], axis=1))
    w_o = fetch(w_o)
    w_gate = fetch(w_gate)
    w_up = fetch(w_up)
    w_down = fetch(w_down)

    seg_rows = lax.dynamic_slice_in_dim(segments, row_start, rows, 1)
    first = jnp.sum((segments[:, None, :] < seg_rows[:, :, None]).astype(jnp.int32), axis=-1)
    query_pos = row_start + jnp.arange(rows, dtype=jnp.int32)
    positions = (query_pos[None, :] - first).reshape(total)
    frequency = rope_base ** (-jnp.arange(0, head, 2, dtype=F32) / head)
    angles = positions.astype(F32)[:, None] * frequency[None, :]
    cos, sin = jnp.cos(angles), jnp.sin(angles)
    cos = jnp.concatenate([cos] * (2 * LANES // head), axis=1)
    sin = jnp.concatenate([-sin, sin] * (LANES // head), axis=1)
    wide = 2 * LANES
    member = jnp.arange(wide) // head
    ones = (member[:, None] == member[None, :]).astype(BF)
    gqk = jnp.concatenate([g_q] * q_heads + [g_k] * kv_heads)[None, :]
    block_q, block_k = min(128, rows), 128
    low = first[:, ::block_q] // block_k
    start = jnp.full((1,), row_start, jnp.int32)

    x = tokens.reshape(total, width)
    normed, q, kv, raw = qkv_call(
        x, w_qkv, g_attn[None, :], gqk, cos, sin, ones, q_width, kv_width, head
    )
    kv = lax.all_gather(kv.reshape(seqs, rows, 2 * kv_width), "ctx", axis=1, tiled=True)
    q = q.reshape(seqs, rows, q_width)
    mixed, totals = attend_call(q, kv, first[:, :, None], low, start, block_q, block_k)
    mixed, totals = mixed.reshape(total, q_width), totals.reshape(total, q_width)
    attended, hidden, normed_two = hidden_call(mixed, w_o, x, g_ffn[None, :])

    def send(grad):
        return lax.psum_scatter(
            grad.astype(BF), AXES, scatter_dimension=0, tiled=True
        ).astype(F32)

    cotangent = cotangent.reshape(total, width)
    ffn, d_normed_two, grad_gate, grad_up, grad_down = ffn_call(
        normed_two, cotangent, w_gate, w_up, w_down
    )
    out_gate, out_up, out_down = send(grad_gate), send(grad_up), send(grad_down)
    outputs, d_hidden, d_low, d_out, delta, grad_gffn = middle_call(
        ffn, d_normed_two, hidden, cotangent, g_ffn[None, :], w_o, mixed, totals, ones, head
    )
    out_o = send(mm(attended, d_low, TN))
    dq, dk, dv = attend_back_call(
        q, d_out.reshape(q.shape), delta.reshape(q.shape), kv, first[:, None, :], low, start,
        block_q, block_k,
    )
    dkv = lax.psum_scatter(
        jnp.concatenate([dk, dv], axis=2), "ctx", scatter_dimension=1, tiled=True
    ).reshape(total, 2 * kv_width)
    d_qkv, input_grad, grad_gattn, grad_gq, grad_gk = last_call(
        dq.reshape(total, q_width), dkv[:, :kv_width], dkv[:, kv_width:], raw, gqk, cos, sin, ones,
        w_qkv, x, g_attn[None, :], d_hidden, head,
    )
    out_qkv = send(mm(normed, d_qkv, TN))

    def fold(grad):
        return jnp.sum(grad.reshape(LANES // head, head), axis=0)

    gains = lax.psum(
        (grad_gattn[0], fold(grad_gq), fold(grad_gk), grad_gffn[0]), AXES
    )
    return (
        outputs.reshape(tokens.shape),
        input_grad.reshape(tokens.shape),
        out_qkv[:, :q_width],
        out_qkv[:, q_width : q_width + kv_width],
        out_qkv[:, q_width + kv_width :],
        out_o,
        out_gate,
        out_up,
        out_down,
        *gains,
    )


def solution(mesh):
    split = P("dp", "ctx", None)
    shard = P(("dp", "ctx"), None)
    in_specs = (split, P("dp", None), split) + (shard,) * 7 + (P(),) * 4
    out_specs = (split, split) + (shard,) * 7 + (P(),) * 4
    return jax.shard_map(
        per_device, mesh=mesh, in_specs=in_specs, out_specs=out_specs, check_vma=False
    )
```

```python
import functools

import jax
import jax.numpy as jnp
from jax import lax
from jax.experimental import pallas as pl
from jax.experimental.pallas import tpu as pltpu
from jax.sharding import PartitionSpec as P

epsilon = 1e-05
rope_base = 1000000.0
AXES = ("dp", "ctx")
BF = jnp.bfloat16
F32 = jnp.float32
LANES = 128
VMEM_LIMIT = 56 * 2**20
AHEAD = 4
OWN = 6
NN = (((1,), (0,)), ((), ()))
NT = (((1,), (1,)), ((), ()))
TN = (((0,), (0,)), ((), ()))


def mm(a, b, dims=NN):
    return lax.dot_general(a, b, dims, preferred_element_type=F32)


def params(semantics=None):
    return pltpu.CompilerParams(
        vmem_limit_bytes=VMEM_LIMIT,
        dimension_semantics=semantics,
    )


def resident(shape):
    zeros = (0,) * len(shape)
    return pl.BlockSpec(shape, lambda *_: zeros, pipeline_mode=pl.Buffered(1))


def largest_block(size, most):
    return max(b for b in range(1, min(size, most) + 1) if size % b == 0)


def head_sum(field, ones):
    wide = ones.shape[0]
    high = field.astype(BF)
    low = (field - high.astype(F32)).astype(BF)
    parts = [
        mm(high[:, c : c + wide], ones) + mm(low[:, c : c + wide], ones)
        for c in range(0, field.shape[1], wide)
    ]
    return jnp.concatenate(parts, axis=1)


def swap_halves(field, head):
    half = head // 2
    width = field.shape[1]
    lane = lax.broadcasted_iota(jnp.int32, field.shape, 1)
    return jnp.where(
        lane % head < half,
        pltpu.roll(field, width - half, 1),
        pltpu.roll(field, half, 1),
    )


def spread(table, width):
    return jnp.concatenate([table] * (width // table.shape[1]), axis=1)


def qkv_kernel(
    q_width, kv_width, head, scale,
    x_ref, w_ref, g_ref, gqk_ref, cos_ref, sin_ref, ones_ref,
    normed_ref, q_ref, kv_ref, raw_ref,
):
    x = x_ref[...].astype(F32)
    inverse = lax.rsqrt(jnp.mean(x * x, axis=-1, keepdims=True) + epsilon)
    normed = (x * inverse * g_ref[...]).astype(BF)
    normed_ref[...] = normed
    qk = q_width + kv_width
    ones = ones_ref[...]
    wide = ones.shape[0]
    cos = spread(cos_ref[...], wide)
    sin = spread(sin_ref[...], wide)
    for c in range(0, qk, wide):
        raw = mm(normed, w_ref[:, c : c + wide])
        raw_ref[:, c : c + wide] = raw
        inv = lax.rsqrt(head_sum(raw * raw, ones) * (1.0 / head) + epsilon)
        field = raw * inv * gqk_ref[:, c : c + wide]
        turned = (field * cos + swap_halves(field, head) * sin).astype(BF)
        if c < q_width:
            q_ref[:, c : c + wide] = turned * jnp.asarray(scale, BF)
        else:
            kv_ref[:, c - q_width : c - q_width + wide] = turned
    kv_ref[:, kv_width:] = mm(normed, w_ref[:, qk:]).astype(BF)


def qkv_call(x, w, g, gqk, cos, sin, ones, q_width, kv_width, head):
    total, width = x.shape
    block = largest_block(total, 256)
    qk = q_width + kv_width

    def rows(n):
        return pl.BlockSpec((block, n), lambda i: (i, 0))

    return pl.pallas_call(
        functools.partial(qkv_kernel, q_width, kv_width, head, head ** (-0.5)),
        grid=(total // block,),
        in_specs=[
            rows(width), resident(w.shape), resident(g.shape), resident(gqk.shape),
            rows(LANES), rows(LANES), resident(ones.shape),
        ],
        out_specs=[rows(width), rows(q_width), rows(2 * kv_width), rows(qk)],
        out_shape=[
            jax.ShapeDtypeStruct((total, width), BF),
            jax.ShapeDtypeStruct((total, q_width), BF),
            jax.ShapeDtypeStruct((total, 2 * kv_width), BF),
            jax.ShapeDtypeStruct((total, qk), F32),
        ],
        compiler_params=params(),
        name="qkv_rope",
    )(x, w, g, gqk, cos, sin, ones)


def pad_head(pair, odd, fill):
    lane = lax.broadcasted_iota(jnp.int32, pair.shape, 1)
    if odd:
        pair = pltpu.roll(pair, LANES // 2, 1)
    return jnp.where(lane < LANES // 2, pair, jnp.asarray(fill, pair.dtype))


def attend_kernel(
    block_q, block_k, heads,
    low_ref, start_ref, q_ref, k_ref, v_ref, first_ref,
    out_ref, total_ref, k_scr, v_scr,
):
    s = pl.program_id(0)
    rows = q_ref.shape[1]
    length = k_ref.shape[1]
    start = start_ref[0]
    half = LANES // 2
    for h in range(heads):
        c = h // 2 * LANES
        k_scr[h] = pad_head(k_ref[0, :, c : c + LANES].astype(F32), h % 2, 0).astype(BF)
        v_scr[h] = pad_head(v_ref[0, :, c : c + LANES].astype(F32), h % 2, 1).astype(BF)
    lane = lax.broadcasted_iota(jnp.int32, (block_q, LANES), 1)
    key_lane = lax.broadcasted_iota(jnp.int32, (2 * block_q, block_k), 1)
    row = lax.broadcasted_iota(jnp.int32, (2 * block_q, 1), 0) % block_q

    def q_step(i, carry):
        at = pl.multiple_of(i * block_q, block_q)
        first = first_ref[0, pl.ds(at, block_q), :]
        first = jnp.concatenate([first, first], axis=0)
        last = row + (start + at)
        queries = []
        for h in range(heads):
            pair = q_ref[0, pl.ds(at, block_q), h * LANES : (h + 1) * LANES].astype(F32)
            queries.append(
                jnp.concatenate([pad_head(pair, 0, 0), pad_head(pair, 1, 0)], axis=0).astype(BF)
            )

        def k_step(j, sums):
            key_at = pl.multiple_of(j * block_k, block_k)
            key = key_lane + key_at
            live = (key >= first) & (key <= last)
            new = []
            for h in range(heads):
                scores = mm(queries[h], k_scr[h, pl.ds(key_at, block_k), :], NT)
                expo = jnp.where(live, jnp.exp(scores), 0.0).astype(BF)
                new.append(sums[h] + mm(expo, v_scr[h, pl.ds(key_at, block_k), :]))
            return tuple(new)

        end = (start + at + block_q - 1) // block_k + 1
        sums = lax.fori_loop(
            low_ref[s, i], end, k_step,
            tuple(jnp.zeros((2 * block_q, LANES), F32) for _ in range(heads)),
        )
        for h in range(heads):
            even, odd = sums[h][:block_q], sums[h][block_q:]
            both = jnp.where(lane < half, even, pltpu.roll(odd, half, 1))
            tot = jnp.where(lane < half, pltpu.roll(even, half, 1), odd)
            cols = slice(h * LANES, (h + 1) * LANES)
            out_ref[0, pl.ds(at, block_q), cols] = both / tot
            total_ref[0, pl.ds(at, block_q), cols] = tot
        return carry

    lax.fori_loop(0, rows // block_q, q_step, 0)


def attend_call(q, kv, first, low, start, block_q, block_k):
    seqs, rows, q_width = q.shape
    length = kv.shape[1]
    kv_width = kv.shape[2] // 2
    kv_heads = q_width // LANES
    heads = largest_block(kv_heads, 4)
    steps = kv_heads // heads
    half = LANES // 2
    spec_q = pl.BlockSpec((1, rows, heads * LANES), lambda s, p, *_: (s, 0, p))
    return pl.pallas_call(
        functools.partial(attend_kernel, block_q, block_k, heads),
        grid_spec=pltpu.PrefetchScalarGridSpec(
            num_scalar_prefetch=2,
            grid=(seqs, steps),
            in_specs=[
                spec_q,
                pl.BlockSpec((1, length, heads * half), lambda s, p, *_: (s, 0, p)),
                pl.BlockSpec((1, length, heads * half), lambda s, p, *_: (s, 0, p + steps)),
                pl.BlockSpec((1, rows, 1), lambda s, p, *_: (s, 0, 0)),
            ],
            out_specs=[spec_q, spec_q],
            scratch_shapes=[
                pltpu.VMEM((heads, length, LANES), BF),
                pltpu.VMEM((heads, length, LANES), BF),
            ],
        ),
        out_shape=[jax.ShapeDtypeStruct(q.shape, F32)] * 2,
        compiler_params=params(),
        name="attend",
    )(low, start, q, kv, kv, first)


def attend_back_kernel(
    block_q, block_k, heads,
    low_ref, start_ref, q_ref, do_ref, de_ref, k_ref, v_ref, first_ref,
    dq_ref, dk_ref, dv_ref, k_scr, v_scr, dk_scr, dv_scr,
):
    s = pl.program_id(0)
    rows = q_ref.shape[1]
    length = k_ref.shape[1]
    start = start_ref[0]
    half = LANES // 2
    for h in range(heads):
        c = h // 2 * LANES
        k_scr[h] = pad_head(k_ref[0, :, c : c + LANES].astype(F32), h % 2, 0).astype(BF)
        v_scr[h] = pad_head(v_ref[0, :, c : c + LANES].astype(F32), h % 2, 1).astype(BF)
    dk_scr[...] = jnp.zeros_like(dk_scr)
    dv_scr[...] = jnp.zeros_like(dv_scr)
    lane = lax.broadcasted_iota(jnp.int32, (block_q, LANES), 1)
    key_row = lax.broadcasted_iota(jnp.int32, (block_k, 2 * block_q), 0)
    column = lax.broadcasted_iota(jnp.int32, (1, 2 * block_q), 1) % block_q

    def tail(pair, odd, delta):
        if odd:
            pair = pltpu.roll(pair, half, 1)
        else:
            delta = pltpu.roll(delta, half, 1)
        part0 = delta.astype(BF).astype(F32)
        part1 = (delta - part0).astype(BF).astype(F32)
        part2 = delta - part0 - part1
        rest = jnp.where(
            lane == half, part0, jnp.where(lane == half + 1, part1, jnp.where(lane == half + 2, part2, 0.0))
        )
        return jnp.where(lane < half, pair, -rest)

    def q_step(i, carry):
        at = pl.multiple_of(i * block_q, block_q)
        first = first_ref[0, :, pl.ds(at, block_q)]
        first = jnp.concatenate([first, first], axis=1)
        last = column + (start + at)
        queries, grads = [], []
        for h in range(heads):
            cols = slice(h * LANES, (h + 1) * LANES)
            pair = q_ref[0, pl.ds(at, block_q), cols].astype(F32)
            queries.append(
                jnp.concatenate([pad_head(pair, 0, 0), pad_head(pair, 1, 0)], axis=0).astype(BF)
            )
            pair = do_ref[0, pl.ds(at, block_q), cols].astype(F32)
            delta = de_ref[0, pl.ds(at, block_q), cols]
            grads.append(
                jnp.concatenate([tail(pair, 0, delta), tail(pair, 1, delta)], axis=0).astype(BF)
            )

        def k_step(j, sums):
            key_at = pl.multiple_of(j * block_k, block_k)
            key = key_row + key_at
            live = (key >= first) & (key <= last)
            new = []
            for h in range(heads):
                k = k_scr[h, pl.ds(key_at, block_k), :]
                v = v_scr[h, pl.ds(key_at, block_k), :]
                scores = mm(k, queries[h], NT)
                expo = jnp.where(live, jnp.exp(scores), 0.0)
                change = mm(v, grads[h], NT)
                d_scores = (expo * change).astype(BF)
                dv_scr[h, pl.ds(key_at, block_k), :] += mm(expo.astype(BF), grads[h])
                dk_scr[h, pl.ds(key_at, block_k), :] += mm(d_scores, queries[h])
                new.append(sums[h] + mm(d_scores, k, TN))
            return tuple(new)

        end = (start + at + block_q - 1) // block_k + 1
        sums = lax.fori_loop(
            low_ref[s, i], end, k_step,
            tuple(jnp.zeros((2 * block_q, LANES), F32) for _ in range(heads)),
        )
        for h in range(heads):
            even, odd = sums[h][:block_q], sums[h][block_q:]
            cols = slice(h * LANES, (h + 1) * LANES)
            dq_ref[0, pl.ds(at, block_q), cols] = jnp.where(
                lane < half, even, pltpu.roll(odd, half, 1)
            )
        return carry

    lax.fori_loop(0, rows // block_q, q_step, 0)
    wide = lax.broadcasted_iota(jnp.int32, (length, LANES), 1)
    for h in range(0, heads, 2):
        cols = slice(h // 2 * LANES, (h // 2 + 1) * LANES)
        for grad, scr in ((dk_ref, dk_scr), (dv_ref, dv_scr)):
            grad[0, :, cols] = jnp.where(
                wide < half, scr[h], pltpu.roll(scr[h + 1], half, 1)
            ).astype(BF)


def attend_back_call(q, d_out, delta, kv, first, low, start, block_q, block_k):
    seqs, rows, q_width = q.shape
    length = kv.shape[1]
    kv_width = kv.shape[2] // 2
    kv_heads = q_width // LANES
    heads = largest_block(kv_heads, 4)
    steps = kv_heads // heads
    half = LANES // 2
    spec_q = pl.BlockSpec((1, rows, heads * LANES), lambda s, p, *_: (s, 0, p))
    spec_kv = pl.BlockSpec((1, length, heads * half), lambda s, p, *_: (s, 0, p))
    return pl.pallas_call(
        functools.partial(attend_back_kernel, block_q, block_k, heads),
        grid_spec=pltpu.PrefetchScalarGridSpec(
            num_scalar_prefetch=2,
            grid=(seqs, steps),
            in_specs=[
                spec_q, spec_q, spec_q, spec_kv,
                pl.BlockSpec((1, length, heads * half), lambda s, p, *_: (s, 0, p + steps)),
                pl.BlockSpec((1, 1, rows), lambda s, p, *_: (s, 0, 0)),
            ],
            out_specs=[spec_q, spec_kv, spec_kv],
            scratch_shapes=[
                pltpu.VMEM((heads, length, LANES), BF),
                pltpu.VMEM((heads, length, LANES), BF),
                pltpu.VMEM((heads, length, LANES), F32),
                pltpu.VMEM((heads, length, LANES), F32),
            ],
        ),
        out_shape=[
            jax.ShapeDtypeStruct(q.shape, F32),
            jax.ShapeDtypeStruct((seqs, length, kv_width), BF),
            jax.ShapeDtypeStruct((seqs, length, kv_width), BF),
        ],
        compiler_params=params(),
        name="attend_back",
    )(low, start, q, d_out, delta, kv, kv, first)


def hidden_kernel(a_ref, w_ref, x_ref, g_ref, att_ref, hidden_ref, normed_ref):
    attended = a_ref[...].astype(BF)
    att_ref[...] = attended
    hidden = x_ref[...].astype(F32) + mm(attended, w_ref[...])
    hidden_ref[...] = hidden
    inverse = lax.rsqrt(jnp.mean(hidden * hidden, axis=-1, keepdims=True) + epsilon)
    normed_ref[...] = (hidden * inverse * g_ref[...]).astype(BF)


def hidden_call(mixed, w_o, x, g):
    total, width = x.shape
    q_width = mixed.shape[1]
    block = largest_block(total, 256)

    def rows(n):
        return pl.BlockSpec((block, n), lambda i: (i, 0))

    return pl.pallas_call(
        hidden_kernel,
        grid=(total // block,),
        in_specs=[rows(q_width), resident(w_o.shape), rows(width), resident(g.shape)],
        out_specs=[rows(q_width), rows(width), rows(width)],
        out_shape=[
            jax.ShapeDtypeStruct((total, q_width), BF),
            jax.ShapeDtypeStruct((total, width), F32),
            jax.ShapeDtypeStruct((total, width), BF),
        ],
        compiler_params=params(),
        name="hidden",
    )(mixed, w_o, x, g)


def ffn_kernel(
    block_t,
    n_ref, c_ref, wg_ref, wu_ref, wd_ref,
    out_ref, dn_ref, gg_ref, gu_ref, gd_ref,
    n_scr, c_scr, act_scr, dg_scr, du_scr,
):
    total, width = n_ref.shape
    chunk = wg_ref.shape[1]

    @pl.when(pl.program_id(0) == 0)
    def _():
        c_scr[...] = c_ref[...].astype(BF)
        n_scr[...] = n_ref[...].T
        out_ref[...] = jnp.zeros_like(out_ref)
        dn_ref[...] = jnp.zeros_like(dn_ref)

    def t_step(i, carry):
        at = pl.ds(pl.multiple_of(i * block_t, block_t), block_t)
        normed = n_ref[at, :]
        gate = mm(normed, wg_ref[...])
        up = mm(normed, wu_ref[...])
        d_act = mm(c_scr[at, :], wd_ref[...], NT)
        sig = 1.0 / (1.0 + jnp.exp(-gate))
        silu = gate * sig
        act = (silu * up).astype(BF)
        d_gate = (d_act * up * (sig * (1.0 + gate - silu))).astype(BF)
        d_up = (d_act * silu).astype(BF)
        act_scr[at, :] = act
        dg_scr[at, :] = d_gate
        du_scr[at, :] = d_up
        out_ref[at, :] += mm(act, wd_ref[...])
        dn_ref[at, :] += mm(d_gate, wg_ref[...], NT) + mm(d_up, wu_ref[...], NT)
        return carry

    lax.fori_loop(0, total // block_t, t_step, 0)

    def d_step(i, carry):
        at = pl.ds(pl.multiple_of(i * 256, 256), 256)
        normed = n_scr[at, :]
        gg_ref[at, :] = mm(normed, dg_scr[...]).astype(BF)
        gu_ref[at, :] = mm(normed, du_scr[...]).astype(BF)
        return carry

    lax.fori_loop(0, width // 256, d_step, 0)
    for c in range(0, chunk, 256):
        gd_ref[c : c + 256, :] = mm(act_scr[:, c : c + 256], c_scr[...], TN).astype(BF)


def ffn_call(normed, cotangent, w_gate, w_up, w_down):
    total, width = normed.shape
    hidden = w_gate.shape[1]
    chunk = largest_block(hidden, 512)
    block_t = largest_block(total, 256)
    cols = pl.BlockSpec((width, chunk), lambda i: (0, i))
    rows = pl.BlockSpec((chunk, width), lambda i: (i, 0))
    return pl.pallas_call(
        functools.partial(ffn_kernel, block_t),
        grid=(hidden // chunk,),
        in_specs=[resident(normed.shape), resident(normed.shape), cols, cols, rows],
        out_specs=[resident(normed.shape), resident(normed.shape), cols, cols, rows],
        out_shape=[
            jax.ShapeDtypeStruct((total, width), F32),
            jax.ShapeDtypeStruct((total, width), F32),
            jax.ShapeDtypeStruct(w_gate.shape, BF),
            jax.ShapeDtypeStruct(w_gate.shape, BF),
            jax.ShapeDtypeStruct(w_down.shape, BF),
        ],
        scratch_shapes=[
            pltpu.VMEM((width, total), BF),
            pltpu.VMEM((total, width), BF),
            pltpu.VMEM((total, chunk), BF),
            pltpu.VMEM((total, chunk), BF),
            pltpu.VMEM((total, chunk), BF),
        ],
        compiler_params=params(),
        cost_estimate=pl.CostEstimate(
            flops=18 * total * width * hidden, bytes_accessed=12 * width * hidden, transcendentals=0
        ),
        name="ffn",
    )(normed, cotangent, w_gate, w_up, w_down)


def middle_kernel(
    head,
    f_ref, dn_ref, h_ref, c_ref, g_ref, w_ref, o_ref, l_ref, ones_ref,
    out_ref, dh_ref, low_ref, do_ref, de_ref, gain_ref,
):
    @pl.when(pl.program_id(0) == 0)
    def _():
        gain_ref[...] = jnp.zeros_like(gain_ref)

    hidden = h_ref[...]
    out_ref[...] = (hidden + f_ref[...]).astype(BF)
    inverse = lax.rsqrt(jnp.mean(hidden * hidden, axis=-1, keepdims=True) + epsilon)
    incoming = dn_ref[...]
    unit = hidden * inverse
    gain_ref[...] += jnp.sum(unit * incoming, axis=0, keepdims=True)
    scaled = incoming * g_ref[...]
    shared = jnp.mean(unit * scaled, axis=-1, keepdims=True)
    d_hidden = c_ref[...] + inverse * (scaled - unit * shared)
    dh_ref[...] = d_hidden
    low = d_hidden.astype(BF)
    low_ref[...] = low
    ones = ones_ref[...]
    wide = ones.shape[0]
    for c in range(0, o_ref.shape[1], wide):
        cols = slice(c, c + wide)
        d_att = mm(low, w_ref[cols, :], NT)
        ratio = 1.0 / l_ref[:, cols]
        do_ref[:, cols] = (d_att * ratio).astype(BF)
        de_ref[:, cols] = head_sum(d_att * o_ref[:, cols], ones) * ratio


def middle_call(ffn, d_normed, hidden, cotangent, g, w_o, mixed, totals, ones, head):
    total, width = hidden.shape
    q_width = mixed.shape[1]
    block = largest_block(total, 256)

    def rows(n):
        return pl.BlockSpec((block, n), lambda i: (i, 0))

    return pl.pallas_call(
        functools.partial(middle_kernel, head),
        grid=(total // block,),
        in_specs=[
            rows(width), rows(width), rows(width), rows(width), resident(g.shape),
            resident(w_o.shape), rows(q_width), rows(q_width), resident(ones.shape),
        ],
        out_specs=[
            rows(width), rows(width), rows(width), rows(q_width), rows(q_width), resident((1, width)),
        ],
        out_shape=[
            jax.ShapeDtypeStruct((total, width), BF),
            jax.ShapeDtypeStruct((total, width), F32),
            jax.ShapeDtypeStruct((total, width), BF),
            jax.ShapeDtypeStruct((total, q_width), BF),
            jax.ShapeDtypeStruct((total, q_width), F32),
            jax.ShapeDtypeStruct((1, width), F32),
        ],
        compiler_params=params(),
        name="middle",
    )(ffn, d_normed, hidden, cotangent, g, w_o, mixed, totals, ones)


def last_kernel(
    q_width, kv_width, head, scale,
    dq_ref, dk_ref, dv_ref, raw_ref, gqk_ref, cos_ref, sin_ref, ones_ref, w_ref, x_ref, g_ref, dh_ref,
    d_ref, in_ref, gain_ref, gq_ref, gk_ref,
):
    @pl.when(pl.program_id(0) == 0)
    def _():
        gain_ref[...] = jnp.zeros_like(gain_ref)
        gq_ref[...] = jnp.zeros_like(gq_ref)
        gk_ref[...] = jnp.zeros_like(gk_ref)

    ones = ones_ref[...]
    wide = ones.shape[0]
    cos = spread(cos_ref[...], wide)
    sin = spread(sin_ref[...], wide)
    qk = q_width + kv_width
    for c in range(0, qk, wide):
        cols = slice(c, c + wide)
        if c < q_width:
            grad, total = dq_ref[:, cols] * scale, gq_ref
        else:
            grad, total = dk_ref[:, c - q_width : c - q_width + wide].astype(F32), gk_ref
        grad = grad * cos + swap_halves(grad * sin, head)
        raw = raw_ref[:, cols]
        inv = lax.rsqrt(head_sum(raw * raw, ones) * (1.0 / head) + epsilon)
        unit = raw * inv
        gained = jnp.sum(unit * grad, axis=0, keepdims=True)
        total[...] += sum(gained[:, i : i + LANES] for i in range(0, wide, LANES))
        scaled = grad * gqk_ref[:, cols]
        shared = head_sum(unit * scaled, ones) * (1.0 / head)
        d_ref[:, cols] = (inv * (scaled - unit * shared)).astype(BF)
    d_ref[:, qk:] = dv_ref[...].astype(BF)
    d_normed = mm(d_ref[...], w_ref[...], NT)
    x = x_ref[...].astype(F32)
    inverse = lax.rsqrt(jnp.mean(x * x, axis=-1, keepdims=True) + epsilon)
    unit = x * inverse
    gain_ref[...] += jnp.sum(unit * d_normed, axis=0, keepdims=True)
    scaled = d_normed * g_ref[...]
    shared = jnp.mean(unit * scaled, axis=-1, keepdims=True)
    in_ref[...] = dh_ref[...] + inverse * (scaled - unit * shared)


def last_call(dq, dk, dv, raw, gqk, cos, sin, ones, w, x, g, d_hidden, head):
    total, width = x.shape
    q_width, kv_width = dq.shape[1], dk.shape[1]
    block = largest_block(total, 256)

    def rows(n):
        return pl.BlockSpec((block, n), lambda i: (i, 0))

    return pl.pallas_call(
        functools.partial(last_kernel, q_width, kv_width, head, head ** (-0.5)),
        grid=(total // block,),
        in_specs=[
            rows(q_width), rows(kv_width), rows(kv_width), rows(q_width + kv_width),
            resident(gqk.shape), rows(LANES), rows(LANES), resident(ones.shape),
            resident(w.shape), rows(width), resident(g.shape), rows(width),
        ],
        out_specs=[
            rows(w.shape[1]), rows(width),
            resident((1, width)), resident((1, LANES)), resident((1, LANES)),
        ],
        out_shape=[
            jax.ShapeDtypeStruct((total, w.shape[1]), BF),
            jax.ShapeDtypeStruct((total, width), F32),
            jax.ShapeDtypeStruct((1, width), F32),
            jax.ShapeDtypeStruct((1, LANES), F32),
            jax.ShapeDtypeStruct((1, LANES), F32),
        ],
        compiler_params=params(),
        name="last",
    )(dq, dk, dv, raw, gqk, cos, sin, ones, w, x, g, d_hidden)


class Place:
    def __init__(self):
        dp = lax.axis_index("dp")
        self.x = lax.axis_index("ctx")
        self.c = lax.rem(dp, 2)
        self.y = lax.rem(dp // 2, 2)
        self.z = dp // 4

    def peer(self, z=None, y=None, c=None, x=None):
        z = self.z if z is None else z
        y = self.y if y is None else y
        c = self.c if c is None else c
        x = self.x if x is None else x
        return {"dp": (z * 2 + y) * 2 + c, "ctx": x}

    def up(self, d):
        return lax.rem(self.z + d, 4)

    def peers(self):
        return [self.peer(z=self.up(d)) for d in (1, 2, 3)] + [
            self.peer(x=1 - self.x), self.peer(y=1 - self.y), self.peer(c=1 - self.c)
        ]


def greet(place):
    barrier = pltpu.get_barrier_semaphore()
    peers = place.peers()
    for peer in peers:
        pl.semaphore_signal(barrier, inc=1, device_id=peer, device_id_type=pl.DeviceIdType.MESH)
    pl.semaphore_wait(barrier, len(peers))


def remote(src, dst, sems, at, peer):
    send, recv = sems
    return pltpu.make_async_remote_copy(
        src_ref=src, dst_ref=dst, send_sem=send.at[at], recv_sem=recv.at[at],
        device_id=peer, device_id_type=pl.DeviceIdType.MESH,
    )


def gather_kernel(pieces, count, *refs):
    ins, outs = refs[:count], refs[count : 2 * count]
    sems, local = refs[2 * count : 2 * count + 2], refs[2 * count + 2]
    me = Place()
    greet(me)

    def block(p, z, y, c, x):
        array, rows, cols, _ = pieces[p]
        return outs[array].at[z, y, c, x, rows, cols]

    def own(p):
        array, rows, cols, _ = pieces[p]
        return ins[array].at[rows, cols]

    every = slice(None)

    def to_z(p):
        return [
            remote(own(p), block(p, me.z, me.y, me.c, me.x), sems, (p, d - 1), me.peer(z=me.up(d)))
            for d in (1, 2, 3)
        ]

    def keep(p):
        return pltpu.make_async_copy(own(p), block(p, me.z, me.y, me.c, me.x), local.at[p])

    def first(p):
        mine = block(p, every, me.y, me.c, me.x)
        peer = me.peer(x=1 - me.x) if pieces[p][3] else me.peer(y=1 - me.y)
        return [remote(mine, mine, sems, (p, 3), peer)]

    def second(p):
        if pieces[p][3]:
            mine, peer = block(p, every, me.y, me.c, every), me.peer(y=1 - me.y)
        else:
            mine, peer = block(p, every, every, me.c, me.x), me.peer(x=1 - me.x)
        return [remote(mine, mine, sems, (p, 4), peer)]

    def third(p):
        mine = block(p, every, every, me.c, every)
        return [remote(mine, mine, sems, (p, 5), me.peer(c=1 - me.c))]

    n = len(pieces)
    stages = [to_z, first, second, third]
    pair = 2

    def begin(p):
        keep(p).start()
        for copy in to_z(p):
            copy.start()

    for p in range(min(n, AHEAD)):
        begin(p)
    for t in range(0, n + 3 * pair, pair):
        for p in range(t + AHEAD, min(n, t + AHEAD + pair)):
            begin(p)
        for s in (1, 2, 3):
            for p in range(t - (s - 1) * pair, t - (s - 1) * pair + pair):
                if 0 <= p < n:
                    if s == 1:
                        keep(p).wait()
                    for copy in stages[s - 1](p):
                        copy.wait_recv()
                    for copy in stages[s](p):
                        copy.start()
    for p in range(n):
        third(p)[0].wait_recv()
    for p in range(n):
        for stage in stages:
            for copy in stage(p):
                copy.wait_send()


def gather_call(shards, pieces, collective):
    count = len(shards)
    outs = pl.pallas_call(
        functools.partial(gather_kernel, pieces, count),
        in_specs=[pl.BlockSpec(memory_space=pl.ANY)] * count,
        out_specs=[pl.BlockSpec(memory_space=pl.ANY)] * count,
        out_shape=[jax.ShapeDtypeStruct((4, 2, 2, 2) + s.shape, s.dtype) for s in shards],
        scratch_shapes=[
            pltpu.SemaphoreType.DMA((len(pieces), 6)),
            pltpu.SemaphoreType.DMA((len(pieces), 6)),
            pltpu.SemaphoreType.DMA((len(pieces),)),
        ],
        compiler_params=pltpu.CompilerParams(
            collective_id=collective, has_side_effects=True, vmem_limit_bytes=VMEM_LIMIT
        ),
        name="gather",
    )(*shards)
    return [o.reshape(32 * s.shape[0], s.shape[1]) for o, s in zip(outs, shards)]


def add_into(total, more):
    def step(i, carry):
        total[i] = (total[i].astype(F32) + more[i].astype(F32)).astype(total.dtype)
        return carry

    lax.fori_loop(0, total.shape[0], step, 0)


def scatter_kernel(pieces, count, *refs):
    ins, outs = refs[:count], refs[count : 2 * count]
    n = len(pieces)
    shapes, homes = piece_homes(pieces)
    scratch = refs[2 * count : 2 * count + 5 * len(shapes)]
    homes = [
        (scratch[5 * k : 5 * k + 4], i, scratch[5 * k + 4].at[i % OWN], (k, i % OWN)) for k, i in homes
    ]
    sems, local = refs[-3:-1], refs[-1]
    me = Place()
    greet(me)
    every = slice(None)

    def at(p, s):
        return homes[p][0][s].at[homes[p][1]]

    def part(p, c):
        array, rows, cols, _ = pieces[p]
        return ins[array].at[every, every, c, every, rows, cols]

    def load(p):
        return pltpu.make_async_copy(part(p, me.c), homes[p][2], local.at[homes[p][3]])

    def pairs(p):
        return [remote(part(p, 1 - me.c), at(p, 0), sems, (p, 0), me.peer(c=1 - me.c))]

    def first(p):
        if pieces[p][3]:
            give, peer = at(p, 0).at[every, every, 1 - me.x], me.peer(x=1 - me.x)
        else:
            give, peer = at(p, 0).at[every, 1 - me.y], me.peer(y=1 - me.y)
        return [remote(give, at(p, 1), sems, (p, 1), peer)]

    def second(p):
        if pieces[p][3]:
            peer, other = me.peer(y=1 - me.y), 1 - me.y
        else:
            peer, other = me.peer(x=1 - me.x), 1 - me.x
        return [remote(at(p, 1).at[every, other], at(p, 2), sems, (p, 2), peer)]

    def third(p):
        return [
            remote(at(p, 2).at[me.up(d)], at(p, 3).at[d - 1], sems, (p, 2 + d), me.peer(z=me.up(d)))
            for d in (1, 2, 3)
        ]

    stages = [pairs, first, second, third]

    def settle(p, s):
        if s == 0:
            load(p).wait()
            add_into(at(p, 0), homes[p][2])
        elif s == 1:
            kept = at(p, 0).at[every, every, me.x] if pieces[p][3] else at(p, 0).at[every, me.y]
            add_into(at(p, 1), kept)
        elif s == 2:
            add_into(at(p, 2), at(p, 1).at[every, me.y if pieces[p][3] else me.x])
        else:
            array, rows, cols, _ = pieces[p]
            more = at(p, 3)
            outs[array][rows, cols] = (
                at(p, 2)[me.z].astype(F32) + more[0].astype(F32) + more[1].astype(F32) + more[2].astype(F32)
            )

    pair = 2

    def begin(p):
        load(p).start()
        for copy in pairs(p):
            copy.start()

    for p in range(min(n, AHEAD)):
        begin(p)
    for t in range(0, n + 3 * pair, pair):
        for s in range(4):
            for p in range(t - s * pair, t - s * pair + pair):
                if 0 <= p < n:
                    for copy in stages[s](p):
                        copy.wait_recv()
                    settle(p, s)
                    if s < 3:
                        for copy in stages[s + 1](p):
                            copy.start()
            if s == 0:
                for p in range(t + AHEAD, min(n, t + AHEAD + pair)):
                    begin(p)
    for p in range(n):
        for stage in stages:
            for copy in stage(p):
                copy.wait_send()


def piece_homes(pieces):
    shapes, homes = [], []
    for _, rows, cols, _ in pieces:
        shape = (rows.stop - rows.start, cols.stop - cols.start)
        if shape not in shapes:
            shapes.append(shape)
        kind = shapes.index(shape)
        homes.append((kind, sum(k == kind for k, _ in homes)))
    return shapes, homes


def scatter_call(grads, pieces, collective):
    count = len(grads)
    shards = [(g.shape[0] // 32, g.shape[1]) for g in grads]
    grads = [g.reshape((4, 2, 2, 2) + s) for g, s in zip(grads, shards)]
    shapes, homes = piece_homes(pieces)
    scratch = []
    for kind, shape in enumerate(shapes):
        n = sum(k == kind for k, _ in homes)
        scratch += [
            pltpu.VMEM((n, 4, 2, 2) + shape, BF),
            pltpu.VMEM((n, 4, 2) + shape, BF),
            pltpu.VMEM((n, 4) + shape, BF),
            pltpu.VMEM((n, 3) + shape, BF),
            pltpu.VMEM((OWN, 4, 2, 2) + shape, BF),
        ]
    return pl.pallas_call(
        functools.partial(scatter_kernel, pieces, count),
        in_specs=[pl.BlockSpec(memory_space=pl.ANY)] * count,
        out_specs=[pl.BlockSpec(memory_space=pltpu.VMEM)] * count,
        out_shape=[jax.ShapeDtypeStruct(s, F32) for s in shards],
        scratch_shapes=scratch + [
            pltpu.SemaphoreType.DMA((len(pieces), 6)),
            pltpu.SemaphoreType.DMA((len(pieces), 6)),
            pltpu.SemaphoreType.DMA((len(shapes), OWN)),
        ],
        compiler_params=pltpu.CompilerParams(
            collective_id=collective, has_side_effects=True, vmem_limit_bytes=VMEM_LIMIT
        ),
        name="scatter",
    )(*grads)


def col_pieces(array, rows, cols, width=512, high=None):
    high = high or rows
    return [
        (array, slice(r, r + high), slice(c, c + width), (c // width) % 2 == 0)
        for r in range(0, rows, high)
        for c in range(0, cols, width)
    ]


def interleave(one, two):
    return [p for pair in zip(one, two) for p in pair]


def per_device(
    tokens, segments, cotangent, w_q, w_k, w_v, w_o, w_gate, w_up, w_down, g_attn, g_q, g_k, g_ffn
):
    seqs, rows, width = tokens.shape
    length = segments.shape[1]
    head = g_q.shape[0]
    q_width, kv_width = w_q.shape[1], w_k.shape[1]
    kv_heads = kv_width // head
    q_heads = q_width // head
    total = seqs * rows
    row_start = lax.axis_index("ctx") * rows

    def fetch(weight):
        return lax.all_gather(weight, AXES, axis=0, tiled=True)

    w_qkv = jnp.concatenate([w_q, w_k, w_v], axis=1)
    own_kernels = (lax.axis_size("dp"), lax.axis_size("ctx")) == (16, 2)
    share = w_q.shape[0]
    gate_pieces = interleave(
        [(0,) + p[1:3] + (True,) for p in col_pieces(0, share, w_gate.shape[1])],
        [(1,) + p[1:3] + (False,) for p in col_pieces(1, share, w_up.shape[1])],
    )
    qkv_pieces = col_pieces(0, share, w_qkv.shape[1])
    o_pieces = col_pieces(1, share, w_o.shape[1])
    w_down = fetch(w_down)
    if own_kernels:
        w_qkv, w_o = gather_call([w_qkv, w_o], qkv_pieces + o_pieces, 0)
    else:
        w_qkv, w_o, w_gate, w_up = fetch(w_qkv), fetch(w_o), fetch(w_gate), fetch(w_up)

    seg_rows = lax.dynamic_slice_in_dim(segments, row_start, rows, 1)
    first = jnp.sum((segments[:, None, :] < seg_rows[:, :, None]).astype(jnp.int32), axis=-1)
    query_pos = row_start + jnp.arange(rows, dtype=jnp.int32)
    positions = (query_pos[None, :] - first).reshape(total)
    frequency = rope_base ** (-jnp.arange(0, head, 2, dtype=F32) / head)
    angles = positions.astype(F32)[:, None] * frequency[None, :]
    cos, sin = jnp.cos(angles), jnp.sin(angles)
    cos = jnp.concatenate([cos] * (2 * LANES // head), axis=1)
    sin = jnp.concatenate([-sin, sin] * (LANES // head), axis=1)
    wide = 2 * LANES
    member = jnp.arange(wide) // head
    ones = (member[:, None] == member[None, :]).astype(BF)
    gqk = jnp.concatenate([g_q] * q_heads + [g_k] * kv_heads)[None, :]
    block_q, block_k = min(128, rows), 128
    low = first[:, ::block_q] // block_k
    start = jnp.full((1,), row_start, jnp.int32)

    x = tokens.reshape(total, width)
    normed, q, kv, raw = qkv_call(
        x, w_qkv, g_attn[None, :], gqk, cos, sin, ones, q_width, kv_width, head
    )
    kv = lax.all_gather(kv.reshape(seqs, rows, 2 * kv_width), "ctx", axis=1, tiled=True)
    q = q.reshape(seqs, rows, q_width)
    mixed, totals = attend_call(q, kv, first[:, :, None], low, start, block_q, block_k)
    mixed, totals = mixed.reshape(total, q_width), totals.reshape(total, q_width)
    attended, hidden, normed_two = hidden_call(mixed, w_o, x, g_ffn[None, :])

    def send(grad):
        return lax.psum_scatter(
            grad.astype(BF), AXES, scatter_dimension=0, tiled=True
        ).astype(F32)

    cotangent = cotangent.reshape(total, width)
    if own_kernels:
        normed_two, w_gate, w_up = lax.optimization_barrier((normed_two, w_gate, w_up))
        w_gate, w_up = gather_call([w_gate, w_up], gate_pieces, 1)
    ffn, d_normed_two, grad_gate, grad_up, grad_down = ffn_call(
        normed_two, cotangent, w_gate, w_up, w_down
    )
    if own_kernels:
        out_gate, out_up = scatter_call([grad_gate, grad_up], gate_pieces, 2)
    else:
        out_gate, out_up, out_down = send(grad_gate), send(grad_up), send(grad_down)
    outputs, d_hidden, d_low, d_out, delta, grad_gffn = middle_call(
        ffn, d_normed_two, hidden, cotangent, g_ffn[None, :], w_o, mixed, totals, ones, head
    )
    grad_o = mm(attended, d_low, TN).astype(BF)
    dq, dk, dv = attend_back_call(
        q, d_out.reshape(q.shape), delta.reshape(q.shape), kv, first[:, None, :], low, start,
        block_q, block_k,
    )
    dkv = lax.psum_scatter(
        jnp.concatenate([dk, dv], axis=2), "ctx", scatter_dimension=1, tiled=True
    ).reshape(total, 2 * kv_width)
    d_qkv, input_grad, grad_gattn, grad_gq, grad_gk = last_call(
        dq.reshape(total, q_width), dkv[:, :kv_width], dkv[:, kv_width:], raw, gqk, cos, sin, ones,
        w_qkv, x, g_attn[None, :], d_hidden, head,
    )
    grad_qkv = mm(normed, d_qkv, TN).astype(BF)
    if own_kernels:
        down_pieces = [(2,) + p[1:] for p in col_pieces(2, w_down.shape[0] // 32, width, 256, 48)]
        out_qkv, out_o, out_down = scatter_call(
            [grad_qkv, grad_o, grad_down], down_pieces + o_pieces + qkv_pieces, 3
        )
    else:
        out_qkv, out_o = send(grad_qkv), send(grad_o)

    def fold(grad):
        return jnp.sum(grad.reshape(LANES // head, head), axis=0)

    gains = lax.psum(
        (grad_gattn[0], fold(grad_gq), fold(grad_gk), grad_gffn[0]), AXES
    )
    return (
        outputs.reshape(tokens.shape),
        input_grad.reshape(tokens.shape),
        out_qkv[:, :q_width],
        out_qkv[:, q_width : q_width + kv_width],
        out_qkv[:, q_width + kv_width :],
        out_o,
        out_gate,
        out_up,
        out_down,
        *gains,
    )


def solution(mesh):
    split = P("dp", "ctx", None)
    shard = P(("dp", "ctx"), None)
    in_specs = (split, P("dp", None), split) + (shard,) * 7 + (P(),) * 4
    out_specs = (split, split) + (shard,) * 7 + (P(),) * 4
    return jax.shard_map(
        per_device, mesh=mesh, in_specs=in_specs, out_specs=out_specs, check_vma=False
    )
```

```python
import functools

import jax
import jax.numpy as jnp
from jax import lax
from jax.experimental import pallas as pl
from jax.experimental.pallas import tpu as pltpu
from jax.sharding import PartitionSpec as P

epsilon = 1e-05
rope_base = 1000000.0
AXES = ("dp", "ctx")
BF = jnp.bfloat16
F32 = jnp.float32
LANES = 128
VMEM_LIMIT = 56 * 2**20
AHEAD = 4
OWN = 6
NN = (((1,), (0,)), ((), ()))
NT = (((1,), (1,)), ((), ()))
TN = (((0,), (0,)), ((), ()))


def mm(a, b, dims=NN):
    return lax.dot_general(a, b, dims, preferred_element_type=F32)


def params(semantics=None):
    return pltpu.CompilerParams(
        vmem_limit_bytes=VMEM_LIMIT,
        dimension_semantics=semantics,
    )


def resident(shape):
    zeros = (0,) * len(shape)
    return pl.BlockSpec(shape, lambda *_: zeros, pipeline_mode=pl.Buffered(1))


def largest_block(size, most):
    return max(b for b in range(1, min(size, most) + 1) if size % b == 0)


def head_sum(field, ones):
    wide = ones.shape[0]
    high = field.astype(BF)
    low = (field - high.astype(F32)).astype(BF)
    parts = [
        mm(high[:, c : c + wide], ones) + mm(low[:, c : c + wide], ones)
        for c in range(0, field.shape[1], wide)
    ]
    return jnp.concatenate(parts, axis=1)


def swap_halves(field, head):
    half = head // 2
    width = field.shape[1]
    lane = lax.broadcasted_iota(jnp.int32, field.shape, 1)
    return jnp.where(
        lane % head < half,
        pltpu.roll(field, width - half, 1),
        pltpu.roll(field, half, 1),
    )


def spread(table, width):
    return jnp.concatenate([table] * (width // table.shape[1]), axis=1)


def project_kernel(
    rope_width, head, scale,
    x_ref, w_ref, g_ref, gain_ref, cos_ref, sin_ref, ones_ref,
    normed_ref, out_ref, raw_ref,
):
    x = x_ref[...].astype(F32)
    inverse = lax.rsqrt(jnp.mean(x * x, axis=-1, keepdims=True) + epsilon)
    normed = (x * inverse * g_ref[...]).astype(BF)
    normed_ref[...] = normed
    ones = ones_ref[...]
    wide = ones.shape[0]
    cos = spread(cos_ref[...], wide)
    sin = spread(sin_ref[...], wide)
    for c in range(0, rope_width, wide):
        raw = mm(normed, w_ref[:, c : c + wide])
        raw_ref[:, c : c + wide] = raw
        inv = lax.rsqrt(head_sum(raw * raw, ones) * (1.0 / head) + epsilon)
        field = raw * inv * gain_ref[:, c : c + wide]
        turned = (field * cos + swap_halves(field, head) * sin).astype(BF)
        out_ref[:, c : c + wide] = turned if scale is None else turned * jnp.asarray(scale, BF)
    if rope_width < w_ref.shape[1]:
        out_ref[:, rope_width:] = mm(normed, w_ref[:, rope_width:]).astype(BF)


def project_call(x, w, cols, rope_width, g, gains, cos, sin, ones, head, scale, name):
    total, width = x.shape
    block = largest_block(total, 256)
    at, count = cols[0] // cols[1], cols[1]

    def rows(n):
        return pl.BlockSpec((block, n), lambda i: (i, 0))

    return pl.pallas_call(
        functools.partial(project_kernel, rope_width, head, scale),
        grid=(total // block,),
        in_specs=[
            rows(width),
            pl.BlockSpec((width, count), lambda i: (0, at), pipeline_mode=pl.Buffered(1)),
            resident(g.shape), resident(gains.shape),
            rows(LANES), rows(LANES), resident(ones.shape),
        ],
        out_specs=[rows(width), rows(count), rows(rope_width)],
        out_shape=[
            jax.ShapeDtypeStruct((total, width), BF),
            jax.ShapeDtypeStruct((total, count), BF),
            jax.ShapeDtypeStruct((total, rope_width), F32),
        ],
        compiler_params=params(),
        cost_estimate=pl.CostEstimate(
            flops=2 * total * width * count, bytes_accessed=2 * width * count + 10 * total * count,
            transcendentals=0,
        ),
        name=name,
    )(x, w, g, gains, cos, sin, ones)


def pad_head(pair, odd, fill):
    lane = lax.broadcasted_iota(jnp.int32, pair.shape, 1)
    if odd:
        pair = pltpu.roll(pair, LANES // 2, 1)
    return jnp.where(lane < LANES // 2, pair, jnp.asarray(fill, pair.dtype))


def attend_kernel(
    block_q, block_k, heads, more, last_part,
    low_ref, high_ref, start_ref, q_ref, k_ref, v_ref, first_ref, *refs,
):
    prior = refs[:2] if more else ()
    out_ref, total_ref, k_scr, v_scr = refs[len(prior) :]
    s = pl.program_id(0)
    rows = q_ref.shape[1]
    start = start_ref[0]
    half = LANES // 2
    for h in range(heads):
        c = h // 2 * LANES
        k_scr[h] = pad_head(k_ref[0, :, c : c + LANES].astype(F32), h % 2, 0).astype(BF)
        v_scr[h] = pad_head(v_ref[0, :, c : c + LANES].astype(F32), h % 2, 1).astype(BF)
    lane = lax.broadcasted_iota(jnp.int32, (block_q, LANES), 1)
    key_lane = lax.broadcasted_iota(jnp.int32, (2 * block_q, block_k), 1)
    row = lax.broadcasted_iota(jnp.int32, (2 * block_q, 1), 0) % block_q

    def q_step(i, carry):
        at = pl.multiple_of(i * block_q, block_q)
        first = first_ref[0, pl.ds(at, block_q), :]
        first = jnp.concatenate([first, first], axis=0)
        last = row + (start + at)
        queries = []
        for h in range(heads):
            pair = q_ref[0, pl.ds(at, block_q), h * LANES : (h + 1) * LANES].astype(F32)
            queries.append(
                jnp.concatenate([pad_head(pair, 0, 0), pad_head(pair, 1, 0)], axis=0).astype(BF)
            )

        def k_step(j, sums):
            key_at = pl.multiple_of(j * block_k, block_k)
            key = key_lane + key_at
            live = (key >= first) & (key <= last)
            new = []
            for h in range(heads):
                scores = mm(queries[h], k_scr[h, pl.ds(key_at, block_k), :], NT)
                expo = jnp.where(live, jnp.exp(scores), 0.0).astype(BF)
                new.append(sums[h] + mm(expo, v_scr[h, pl.ds(key_at, block_k), :]))
            return tuple(new)

        sums = lax.fori_loop(
            low_ref[s, i], high_ref[s, i], k_step,
            tuple(jnp.zeros((2 * block_q, LANES), F32) for _ in range(heads)),
        )
        for h in range(heads):
            even, odd = sums[h][:block_q], sums[h][block_q:]
            both = jnp.where(lane < half, even, pltpu.roll(odd, half, 1))
            tot = jnp.where(lane < half, pltpu.roll(even, half, 1), odd)
            cols = slice(h * LANES, (h + 1) * LANES)
            if more:
                both += prior[0][0, pl.ds(at, block_q), cols]
                tot += prior[1][0, pl.ds(at, block_q), cols]
            out_ref[0, pl.ds(at, block_q), cols] = both / tot if last_part else both
            total_ref[0, pl.ds(at, block_q), cols] = tot
        return carry

    lax.fori_loop(0, rows // block_q, q_step, 0)


def attend_call(q, kv, first, keys, block_q, block_k, prior=(), last_part=True):
    seqs, rows, q_width = q.shape
    length = kv.shape[1]
    kv_heads = q_width // LANES
    heads = largest_block(kv_heads, 4)
    steps = kv_heads // heads
    half = LANES // 2
    spec_q = pl.BlockSpec((1, rows, heads * LANES), lambda s, p, *_: (s, 0, p))
    return pl.pallas_call(
        functools.partial(attend_kernel, block_q, block_k, heads, bool(prior), last_part),
        grid_spec=pltpu.PrefetchScalarGridSpec(
            num_scalar_prefetch=3,
            grid=(seqs, steps),
            in_specs=[
                spec_q,
                pl.BlockSpec((1, length, heads * half), lambda s, p, *_: (s, 0, p)),
                pl.BlockSpec((1, length, heads * half), lambda s, p, *_: (s, 0, p + steps)),
                pl.BlockSpec((1, rows, 1), lambda s, p, *_: (s, 0, 0)),
            ] + [spec_q] * len(prior),
            out_specs=[spec_q, spec_q],
            scratch_shapes=[
                pltpu.VMEM((heads, length, LANES), BF),
                pltpu.VMEM((heads, length, LANES), BF),
            ],
        ),
        out_shape=[jax.ShapeDtypeStruct(q.shape, F32)] * 2,
        compiler_params=params(),
        cost_estimate=pl.CostEstimate(
            flops=4 * seqs * rows * length * q_width, bytes_accessed=16 * seqs * rows * q_width,
            transcendentals=0,
        ),
        name="attend",
    )(*keys, q, kv, kv, first[:, :, None], *prior)


def attend_back_kernel(
    block_q, block_k, heads, more,
    low_ref, high_ref, start_ref, q_ref, do_ref, de_ref, k_ref, v_ref, first_ref, *refs,
):
    prior_ref = refs[0] if more else None
    dq_ref, dk_ref, dv_ref, k_scr, v_scr, dk_scr, dv_scr = refs[int(more) :]
    s = pl.program_id(0)
    rows = q_ref.shape[1]
    length = k_ref.shape[1]
    start = start_ref[0]
    half = LANES // 2
    for h in range(heads):
        c = h // 2 * LANES
        k_scr[h] = pad_head(k_ref[0, :, c : c + LANES].astype(F32), h % 2, 0).astype(BF)
        v_scr[h] = pad_head(v_ref[0, :, c : c + LANES].astype(F32), h % 2, 1).astype(BF)
    dk_scr[...] = jnp.zeros_like(dk_scr)
    dv_scr[...] = jnp.zeros_like(dv_scr)
    lane = lax.broadcasted_iota(jnp.int32, (block_q, LANES), 1)
    key_row = lax.broadcasted_iota(jnp.int32, (block_k, 2 * block_q), 0)
    column = lax.broadcasted_iota(jnp.int32, (1, 2 * block_q), 1) % block_q

    def tail(pair, odd, delta):
        if odd:
            pair = pltpu.roll(pair, half, 1)
        else:
            delta = pltpu.roll(delta, half, 1)
        part0 = delta.astype(BF).astype(F32)
        part1 = (delta - part0).astype(BF).astype(F32)
        part2 = delta - part0 - part1
        rest = jnp.where(
            lane == half, part0, jnp.where(lane == half + 1, part1, jnp.where(lane == half + 2, part2, 0.0))
        )
        return jnp.where(lane < half, pair, -rest)

    def q_step(i, carry):
        at = pl.multiple_of(i * block_q, block_q)
        first = first_ref[0, :, pl.ds(at, block_q)]
        first = jnp.concatenate([first, first], axis=1)
        last = column + (start + at)
        queries, grads = [], []
        for h in range(heads):
            cols = slice(h * LANES, (h + 1) * LANES)
            pair = q_ref[0, pl.ds(at, block_q), cols].astype(F32)
            queries.append(
                jnp.concatenate([pad_head(pair, 0, 0), pad_head(pair, 1, 0)], axis=0).astype(BF)
            )
            pair = do_ref[0, pl.ds(at, block_q), cols].astype(F32)
            delta = de_ref[0, pl.ds(at, block_q), cols]
            grads.append(
                jnp.concatenate([tail(pair, 0, delta), tail(pair, 1, delta)], axis=0).astype(BF)
            )

        def k_step(j, sums):
            key_at = pl.multiple_of(j * block_k, block_k)
            key = key_row + key_at
            live = (key >= first) & (key <= last)
            new = []
            for h in range(heads):
                k = k_scr[h, pl.ds(key_at, block_k), :]
                v = v_scr[h, pl.ds(key_at, block_k), :]
                scores = mm(k, queries[h], NT)
                expo = jnp.where(live, jnp.exp(scores), 0.0)
                change = mm(v, grads[h], NT)
                d_scores = (expo * change).astype(BF)
                dv_scr[h, pl.ds(key_at, block_k), :] += mm(expo.astype(BF), grads[h])
                dk_scr[h, pl.ds(key_at, block_k), :] += mm(d_scores, queries[h])
                new.append(sums[h] + mm(d_scores, k, TN))
            return tuple(new)

        sums = lax.fori_loop(
            low_ref[s, i], high_ref[s, i], k_step,
            tuple(jnp.zeros((2 * block_q, LANES), F32) for _ in range(heads)),
        )
        for h in range(heads):
            even, odd = sums[h][:block_q], sums[h][block_q:]
            cols = slice(h * LANES, (h + 1) * LANES)
            grad = jnp.where(lane < half, even, pltpu.roll(odd, half, 1))
            if more:
                grad += prior_ref[0, pl.ds(at, block_q), cols]
            dq_ref[0, pl.ds(at, block_q), cols] = grad
        return carry

    lax.fori_loop(0, rows // block_q, q_step, 0)
    wide = lax.broadcasted_iota(jnp.int32, (length, LANES), 1)
    for h in range(0, heads, 2):
        cols = slice(h // 2 * LANES, (h // 2 + 1) * LANES)
        for grad, scr in ((dk_ref, dk_scr), (dv_ref, dv_scr)):
            grad[0, :, cols] = jnp.where(
                wide < half, scr[h], pltpu.roll(scr[h + 1], half, 1)
            ).astype(BF)


def attend_back_call(q, d_out, delta, kv, first, keys, block_q, block_k, prior=()):
    seqs, rows, q_width = q.shape
    length = kv.shape[1]
    kv_width = kv.shape[2] // 2
    kv_heads = q_width // LANES
    heads = largest_block(kv_heads, 4)
    steps = kv_heads // heads
    half = LANES // 2
    spec_q = pl.BlockSpec((1, rows, heads * LANES), lambda s, p, *_: (s, 0, p))
    spec_kv = pl.BlockSpec((1, length, heads * half), lambda s, p, *_: (s, 0, p))
    return pl.pallas_call(
        functools.partial(attend_back_kernel, block_q, block_k, heads, bool(prior)),
        grid_spec=pltpu.PrefetchScalarGridSpec(
            num_scalar_prefetch=3,
            grid=(seqs, steps),
            in_specs=[
                spec_q, spec_q, spec_q, spec_kv,
                pl.BlockSpec((1, length, heads * half), lambda s, p, *_: (s, 0, p + steps)),
                pl.BlockSpec((1, 1, rows), lambda s, p, *_: (s, 0, 0)),
            ] + [spec_q] * len(prior),
            out_specs=[spec_q, spec_kv, spec_kv],
            scratch_shapes=[
                pltpu.VMEM((heads, length, LANES), BF),
                pltpu.VMEM((heads, length, LANES), BF),
                pltpu.VMEM((heads, length, LANES), F32),
                pltpu.VMEM((heads, length, LANES), F32),
            ],
        ),
        out_shape=[
            jax.ShapeDtypeStruct(q.shape, F32),
            jax.ShapeDtypeStruct((seqs, length, kv_width), BF),
            jax.ShapeDtypeStruct((seqs, length, kv_width), BF),
        ],
        compiler_params=params(),
        cost_estimate=pl.CostEstimate(
            flops=10 * seqs * rows * length * q_width, bytes_accessed=16 * seqs * rows * q_width,
            transcendentals=0,
        ),
        name="attend_back",
    )(*keys, q, d_out, delta, kv, kv, first[:, None, :], *prior)


def hidden_kernel(a_ref, w_ref, x_ref, g_ref, att_ref, hidden_ref, normed_ref):
    attended = a_ref[...].astype(BF)
    att_ref[...] = attended
    hidden = x_ref[...].astype(F32) + mm(attended, w_ref[...])
    hidden_ref[...] = hidden
    inverse = lax.rsqrt(jnp.mean(hidden * hidden, axis=-1, keepdims=True) + epsilon)
    normed_ref[...] = (hidden * inverse * g_ref[...]).astype(BF)


def hidden_call(mixed, w_o, x, g):
    total, width = x.shape
    q_width = mixed.shape[1]
    block = largest_block(total, 256)

    def rows(n):
        return pl.BlockSpec((block, n), lambda i: (i, 0))

    return pl.pallas_call(
        hidden_kernel,
        grid=(total // block,),
        in_specs=[rows(q_width), resident(w_o.shape), rows(width), resident(g.shape)],
        out_specs=[rows(q_width), rows(width), rows(width)],
        out_shape=[
            jax.ShapeDtypeStruct((total, q_width), BF),
            jax.ShapeDtypeStruct((total, width), F32),
            jax.ShapeDtypeStruct((total, width), BF),
        ],
        compiler_params=params(),
        name="hidden",
    )(mixed, w_o, x, g)


def ffn_kernel(
    block_t, steps,
    n_ref, c_ref, wg_ref, wu_ref, wd_ref,
    out_ref, dn_ref, gd_ref, gg_ref, gu_ref,
    n_scr, act_scr, dg_scr, du_scr, *refs,
):
    total, width = n_ref.shape
    chunk = wg_ref.shape[1]
    step = pl.program_id(0)
    sums = GradSums(gg_ref, gu_ref, refs) if refs else None

    @pl.when(step == 0)
    def _():
        if sums:
            sums.hello()
        n_scr[...] = n_ref[...].T
        out_ref[...] = jnp.zeros_like(out_ref)
        dn_ref[...] = jnp.zeros_like(dn_ref)

    def t_step(i, carry):
        at = pl.ds(pl.multiple_of(i * block_t, block_t), block_t)
        normed = n_ref[at, :]
        gate = mm(normed, wg_ref[...])
        up = mm(normed, wu_ref[...])
        d_act = mm(c_ref[at, :], wd_ref[...], NT)
        sig = 1.0 / (1.0 + jnp.exp(-gate))
        silu = gate * sig
        act = (silu * up).astype(BF)
        d_gate = (d_act * up * (sig * (1.0 + gate - silu))).astype(BF)
        d_up = (d_act * silu).astype(BF)
        act_scr[at, :] = act
        dg_scr[at, :] = d_gate
        du_scr[at, :] = d_up
        out_ref[at, :] += mm(act, wd_ref[...])
        dn_ref[at, :] += mm(d_gate, wg_ref[...], NT) + mm(d_up, wu_ref[...], NT)
        return carry

    def d_step(i, carry):
        at = pl.ds(pl.multiple_of(i * 256, 256), 256)
        normed = n_scr[at, :]
        gate = mm(normed, dg_scr[...]).astype(BF)
        up = mm(normed, du_scr[...]).astype(BF)
        if sums:
            sums.keep(step, i, gate, up)
        else:
            gg_ref[at, :] = gate
            gu_ref[at, :] = up
        return carry

    @pl.when(step < steps)
    def _():
        lax.fori_loop(0, total // block_t, t_step, 0)
        lax.fori_loop(0, width // 256, d_step, 0)
        for c in range(0, chunk, 256):
            gd_ref[c : c + 256, :] = mm(act_scr[:, c : c + 256], c_ref[...], TN).astype(BF)

    if sums:
        sums.advance(step, steps)


class GradSums:
    def __init__(self, gg_ref, gu_ref, refs):
        self.outs = (gg_ref, gu_ref)
        self.made, self.r0, self.r1, self.r2, self.r3, self.send, self.recv = refs
        self.me = Place()

    def hello(self):
        barrier = pltpu.get_barrier_semaphore()
        for peer in self.me.peers():
            pl.semaphore_signal(
                barrier, inc=1, device_id=peer, device_id_type=pl.DeviceIdType.MESH
            )

    def keep(self, step, i, gate, up):
        shape = self.made.shape[3:]
        self.made[lax.rem(step, 2), 0, i] = gate.reshape(shape)
        self.made[lax.rem(step, 2), 1, i] = up.reshape(shape)

    def hop(self, k, j, s):
        me, every = self.me, slice(None)
        sems = (self.send, self.recv)
        r0, r1, r2, r3 = (r.at[k, j] for r in (self.r0, self.r1, self.r2, self.r3))
        to_x, to_y = me.peer(x=1 - me.x), me.peer(y=1 - me.y)
        if s == 0:
            give = self.made.at[lax.rem(k, 2), j, every, every, 1 - me.c]
            return [remote(give, r0, sems, (k, j, 0), me.peer(c=1 - me.c))]
        if s == 1:
            if j == 0:
                return [remote(r0.at[every, every, 1 - me.x], r1, sems, (k, j, 1), to_x)]
            return [remote(r0.at[every, 1 - me.y], r1, sems, (k, j, 1), to_y)]
        if s == 2:
            other, peer = (1 - me.y, to_y) if j == 0 else (1 - me.x, to_x)
            return [remote(r1.at[every, other], r2, sems, (k, j, 2), peer)]
        return [
            remote(r2.at[me.up(d)], r3.at[d - 1], sems, (k, j, 2 + d), me.peer(z=me.up(d)))
            for d in (1, 2, 3)
        ]

    def settle(self, k, j, s):
        me, every = self.me, slice(None)
        r0, r1, r2, r3 = (r.at[k, j] for r in (self.r0, self.r1, self.r2, self.r3))
        for copy in self.hop(k, j, s):
            copy.wait()
        if s == 0:
            add_into(r0, self.made.at[lax.rem(k, 2), j, every, every, me.c])
        elif s == 1:
            add_into(r1, r0.at[every, every, me.x] if j == 0 else r0.at[every, me.y])
        elif s == 2:
            add_into(r2, r1.at[every, me.y if j == 0 else me.x])
        else:
            width = r2.shape[-1]
            cols = pl.ds(pl.multiple_of(k * width, width), width)
            self.outs[j][:, cols] = (
                r2[me.z].astype(F32) + r3[0].astype(F32) + r3[1].astype(F32) + r3[2].astype(F32)
            )

    def advance(self, step, steps):
        @pl.when(step == 0)
        def _():
            pl.semaphore_wait(pltpu.get_barrier_semaphore(), len(self.me.peers()))

        for s in (3, 2, 1, 0):
            k = step - 1 - s

            @pl.when((k >= 0) & (k < steps))
            def _(s=s, k=k):
                for j in (0, 1):
                    self.settle(k, j, s)
                    if s < 3:
                        for copy in self.hop(k, j, s + 1):
                            copy.start()

        @pl.when(step < steps)
        def _():
            for j in (0, 1):
                for copy in self.hop(step, j, 0):
                    copy.start()


def ffn_call(normed, grad_low, w_gate, w_up, w_down, collective=None):
    total, width = normed.shape
    hidden = w_gate.shape[1]
    chunk = largest_block(hidden, 512)
    steps = hidden // chunk
    block_t = largest_block(total, 256)
    fused = collective is not None
    last = steps - 1
    cols = pl.BlockSpec((width, chunk), lambda i: (0, jnp.minimum(i, last)))
    rows = pl.BlockSpec((chunk, width), lambda i: (jnp.minimum(i, last), 0))
    grads = [jax.ShapeDtypeStruct(w_gate.shape, BF)] * 2
    scratch = []
    if fused:
        share = width // 32
        grads = [jax.ShapeDtypeStruct((share, hidden), F32)] * 2
        piece = (share, chunk)
        scratch = [
            pltpu.VMEM((2, 2, 4, 2, 2, 2) + piece, BF),
            pltpu.VMEM((steps, 2, 4, 2, 2) + piece, BF),
            pltpu.VMEM((steps, 2, 4, 2) + piece, BF),
            pltpu.VMEM((steps, 2, 4) + piece, BF),
            pltpu.VMEM((steps, 2, 3) + piece, BF),
            pltpu.SemaphoreType.DMA((steps, 2, 6)),
            pltpu.SemaphoreType.DMA((steps, 2, 6)),
        ]
    grad_spec = resident(grads[0].shape) if fused else cols
    return pl.pallas_call(
        functools.partial(ffn_kernel, block_t, steps),
        grid=(steps + 4 * fused,),
        in_specs=[resident(normed.shape), resident(normed.shape), cols, cols, rows],
        out_specs=[resident(normed.shape), resident(normed.shape), rows, grad_spec, grad_spec],
        out_shape=[
            jax.ShapeDtypeStruct((total, width), F32),
            jax.ShapeDtypeStruct((total, width), F32),
            jax.ShapeDtypeStruct(w_down.shape, BF),
        ] + grads,
        scratch_shapes=[
            pltpu.VMEM((width, total), BF),
            pltpu.VMEM((total, chunk), BF),
            pltpu.VMEM((total, chunk), BF),
            pltpu.VMEM((total, chunk), BF),
        ] + scratch,
        compiler_params=pltpu.CompilerParams(
            vmem_limit_bytes=60 * 2**20, collective_id=collective, has_side_effects=fused
        ),
        cost_estimate=pl.CostEstimate(
            flops=18 * total * width * hidden, bytes_accessed=12 * width * hidden, transcendentals=0
        ),
        name="ffn",
    )(normed, grad_low, w_gate, w_up, w_down)


def middle_kernel(
    head,
    f_ref, dn_ref, h_ref, c_ref, g_ref, w_ref, o_ref, l_ref, ones_ref,
    out_ref, dh_ref, low_ref, do_ref, de_ref, gain_ref,
):
    @pl.when(pl.program_id(0) == 0)
    def _():
        gain_ref[...] = jnp.zeros_like(gain_ref)

    hidden = h_ref[...]
    out_ref[...] = (hidden + f_ref[...]).astype(BF)
    inverse = lax.rsqrt(jnp.mean(hidden * hidden, axis=-1, keepdims=True) + epsilon)
    incoming = dn_ref[...]
    unit = hidden * inverse
    gain_ref[...] += jnp.sum(unit * incoming, axis=0, keepdims=True)
    scaled = incoming * g_ref[...]
    shared = jnp.mean(unit * scaled, axis=-1, keepdims=True)
    d_hidden = c_ref[...] + inverse * (scaled - unit * shared)
    dh_ref[...] = d_hidden
    low = d_hidden.astype(BF)
    low_ref[...] = low
    ones = ones_ref[...]
    wide = ones.shape[0]
    for c in range(0, o_ref.shape[1], wide):
        cols = slice(c, c + wide)
        d_att = mm(low, w_ref[cols, :], NT)
        ratio = 1.0 / l_ref[:, cols]
        do_ref[:, cols] = (d_att * ratio).astype(BF)
        de_ref[:, cols] = head_sum(d_att * o_ref[:, cols], ones) * ratio


def middle_call(ffn, d_normed, hidden, cotangent, g, w_o, mixed, totals, ones, head):
    total, width = hidden.shape
    q_width = mixed.shape[1]
    block = largest_block(total, 256)

    def rows(n):
        return pl.BlockSpec((block, n), lambda i: (i, 0))

    return pl.pallas_call(
        functools.partial(middle_kernel, head),
        grid=(total // block,),
        in_specs=[
            rows(width), rows(width), rows(width), rows(width), resident(g.shape),
            resident(w_o.shape), rows(q_width), rows(q_width), resident(ones.shape),
        ],
        out_specs=[
            rows(width), rows(width), rows(width), rows(q_width), rows(q_width), resident((1, width)),
        ],
        out_shape=[
            jax.ShapeDtypeStruct((total, width), BF),
            jax.ShapeDtypeStruct((total, width), F32),
            jax.ShapeDtypeStruct((total, width), BF),
            jax.ShapeDtypeStruct((total, q_width), BF),
            jax.ShapeDtypeStruct((total, q_width), F32),
            jax.ShapeDtypeStruct((1, width), F32),
        ],
        compiler_params=params(),
        name="middle",
    )(ffn, d_normed, hidden, cotangent, g, w_o, mixed, totals, ones)


def last_kernel(
    q_width, kv_width, head, scale,
    dq_ref, dk_ref, dv_ref, rawq_ref, rawk_ref, gqk_ref, cos_ref, sin_ref, ones_ref, w_ref, x_ref, g_ref,
    dh_ref, *refs,
):
    got_ref = refs[0] if len(refs) == 6 else None
    d_ref, in_ref, gain_ref, gq_ref, gk_ref = refs[-5:]

    @pl.when(pl.program_id(0) == 0)
    def _():
        gain_ref[...] = jnp.zeros_like(gain_ref)
        gq_ref[...] = jnp.zeros_like(gq_ref)
        gk_ref[...] = jnp.zeros_like(gk_ref)

    ones = ones_ref[...]
    wide = ones.shape[0]
    cos = spread(cos_ref[...], wide)
    sin = spread(sin_ref[...], wide)
    qk = q_width + kv_width
    for c in range(0, qk, wide):
        cols = slice(c, c + wide)
        if c < q_width:
            grad, total, raw = dq_ref[:, cols] * scale, gq_ref, rawq_ref[:, cols]
        else:
            at = slice(c - q_width, c - q_width + wide)
            grad, total, raw = dk_ref[:, at].astype(F32), gk_ref, rawk_ref[:, at]
            if got_ref is not None:
                grad += got_ref[:, at].astype(F32)
        grad = grad * cos + swap_halves(grad * sin, head)
        inv = lax.rsqrt(head_sum(raw * raw, ones) * (1.0 / head) + epsilon)
        unit = raw * inv
        gained = jnp.sum(unit * grad, axis=0, keepdims=True)
        total[...] += sum(gained[:, i : i + LANES] for i in range(0, wide, LANES))
        scaled = grad * gqk_ref[:, cols]
        shared = head_sum(unit * scaled, ones) * (1.0 / head)
        d_ref[:, cols] = (inv * (scaled - unit * shared)).astype(BF)
    d_values = dv_ref[...].astype(F32)
    if got_ref is not None:
        d_values += got_ref[:, kv_width:].astype(F32)
    d_ref[:, qk:] = d_values.astype(BF)
    d_normed = mm(d_ref[...], w_ref[...], NT)
    x = x_ref[...].astype(F32)
    inverse = lax.rsqrt(jnp.mean(x * x, axis=-1, keepdims=True) + epsilon)
    unit = x * inverse
    gain_ref[...] += jnp.sum(unit * d_normed, axis=0, keepdims=True)
    scaled = d_normed * g_ref[...]
    shared = jnp.mean(unit * scaled, axis=-1, keepdims=True)
    in_ref[...] = dh_ref[...] + inverse * (scaled - unit * shared)


def last_call(dq, dk, dv, raw_q, raw_k, gqk, cos, sin, ones, w, x, g, d_hidden, head, got=()):
    total, width = x.shape
    q_width, kv_width = dq.shape[1], dk.shape[1]
    block = largest_block(total, 256)

    def rows(n):
        return pl.BlockSpec((block, n), lambda i: (i, 0))

    return pl.pallas_call(
        functools.partial(last_kernel, q_width, kv_width, head, head ** (-0.5)),
        grid=(total // block,),
        in_specs=[
            rows(q_width), rows(kv_width), rows(kv_width), rows(q_width), rows(kv_width),
            resident(gqk.shape), rows(LANES), rows(LANES), resident(ones.shape),
            resident(w.shape), rows(width), resident(g.shape), rows(width),
        ] + [rows(2 * kv_width)] * len(got),
        out_specs=[
            rows(w.shape[1]), rows(width),
            resident((1, width)), resident((1, LANES)), resident((1, LANES)),
        ],
        out_shape=[
            jax.ShapeDtypeStruct((total, w.shape[1]), BF),
            jax.ShapeDtypeStruct((total, width), F32),
            jax.ShapeDtypeStruct((1, width), F32),
            jax.ShapeDtypeStruct((1, LANES), F32),
            jax.ShapeDtypeStruct((1, LANES), F32),
        ],
        compiler_params=params(),
        name="last",
    )(dq, dk, dv, raw_q, raw_k, gqk, cos, sin, ones, w, x, g, d_hidden, *got)


class Place:
    def __init__(self):
        dp = lax.axis_index("dp")
        self.x = lax.axis_index("ctx")
        self.c = lax.rem(dp, 2)
        self.y = lax.rem(dp // 2, 2)
        self.z = dp // 4

    def peer(self, z=None, y=None, c=None, x=None):
        z = self.z if z is None else z
        y = self.y if y is None else y
        c = self.c if c is None else c
        x = self.x if x is None else x
        return {"dp": (z * 2 + y) * 2 + c, "ctx": x}

    def up(self, d):
        return lax.rem(self.z + d, 4)

    def peers(self):
        return [self.peer(z=self.up(d)) for d in (1, 2, 3)] + [
            self.peer(x=1 - self.x), self.peer(y=1 - self.y), self.peer(c=1 - self.c)
        ]


def greet(place):
    barrier = pltpu.get_barrier_semaphore()
    peers = place.peers()
    for peer in peers:
        pl.semaphore_signal(barrier, inc=1, device_id=peer, device_id_type=pl.DeviceIdType.MESH)
    pl.semaphore_wait(barrier, len(peers))


def remote(src, dst, sems, at, peer):
    send, recv = sems
    return pltpu.make_async_remote_copy(
        src_ref=src, dst_ref=dst, send_sem=send.at[at], recv_sem=recv.at[at],
        device_id=peer, device_id_type=pl.DeviceIdType.MESH,
    )


def gather_kernel(pieces, count, *refs):
    ins, outs = refs[:count], refs[count : 2 * count]
    sems, local = refs[2 * count : 2 * count + 2], refs[2 * count + 2]
    me = Place()
    greet(me)

    def block(p, z, y, c, x):
        array, rows, cols, _ = pieces[p]
        return outs[array].at[z, y, c, x, rows, cols]

    def own(p):
        array, rows, cols, _ = pieces[p]
        return ins[array].at[rows, cols]

    every = slice(None)

    def to_z(p):
        return [
            remote(own(p), block(p, me.z, me.y, me.c, me.x), sems, (p, d - 1), me.peer(z=me.up(d)))
            for d in (1, 2, 3)
        ]

    def keep(p):
        return pltpu.make_async_copy(own(p), block(p, me.z, me.y, me.c, me.x), local.at[p])

    def first(p):
        mine = block(p, every, me.y, me.c, me.x)
        peer = me.peer(x=1 - me.x) if pieces[p][3] else me.peer(y=1 - me.y)
        return [remote(mine, mine, sems, (p, 3), peer)]

    def second(p):
        if pieces[p][3]:
            mine, peer = block(p, every, me.y, me.c, every), me.peer(y=1 - me.y)
        else:
            mine, peer = block(p, every, every, me.c, me.x), me.peer(x=1 - me.x)
        return [remote(mine, mine, sems, (p, 4), peer)]

    def third(p):
        mine = block(p, every, every, me.c, every)
        return [remote(mine, mine, sems, (p, 5), me.peer(c=1 - me.c))]

    n = len(pieces)
    stages = [to_z, first, second, third]
    pair = 2

    def begin(p):
        keep(p).start()
        for copy in to_z(p):
            copy.start()

    for p in range(min(n, AHEAD)):
        begin(p)
    for t in range(0, n + 3 * pair, pair):
        for p in range(t + AHEAD, min(n, t + AHEAD + pair)):
            begin(p)
        for s in (1, 2, 3):
            for p in range(t - (s - 1) * pair, t - (s - 1) * pair + pair):
                if 0 <= p < n:
                    if s == 1:
                        keep(p).wait()
                    for copy in stages[s - 1](p):
                        copy.wait_recv()
                    for copy in stages[s](p):
                        copy.start()
    for p in range(n):
        third(p)[0].wait_recv()
    for p in range(n):
        for stage in stages:
            for copy in stage(p):
                copy.wait_send()


def gather_call(shards, pieces, collective):
    count = len(shards)
    outs = pl.pallas_call(
        functools.partial(gather_kernel, pieces, count),
        in_specs=[pl.BlockSpec(memory_space=pl.ANY)] * count,
        out_specs=[pl.BlockSpec(memory_space=pl.ANY)] * count,
        out_shape=[jax.ShapeDtypeStruct((4, 2, 2, 2) + s.shape, s.dtype) for s in shards],
        scratch_shapes=[
            pltpu.SemaphoreType.DMA((len(pieces), 6)),
            pltpu.SemaphoreType.DMA((len(pieces), 6)),
            pltpu.SemaphoreType.DMA((len(pieces),)),
        ],
        compiler_params=pltpu.CompilerParams(
            collective_id=collective, has_side_effects=True, vmem_limit_bytes=VMEM_LIMIT
        ),
        name="gather",
    )(*shards)
    return [o.reshape(32 * s.shape[0], s.shape[1]) for o, s in zip(outs, shards)]


def add_into(total, more):
    def step(i, carry):
        total[i] = (total[i].astype(F32) + more[i].astype(F32)).astype(total.dtype)
        return carry

    lax.fori_loop(0, total.shape[0], step, 0)


def scatter_kernel(pieces, count, gains, *refs):
    if gains:
        gain_ref, gain_out = refs[count], refs[2 * count + 1]
        sum_scr, got_scr, z_scr, gain_send, gain_recv = refs[-5:]
        refs = refs[:count] + refs[count + 1 : 2 * count + 1] + refs[2 * count + 2 : -5]
    ins, outs = refs[:count], refs[count : 2 * count]
    n = len(pieces)
    shapes, homes = piece_homes(pieces)
    scratch = refs[2 * count : 2 * count + 5 * len(shapes)]
    homes = [
        (scratch[5 * k : 5 * k + 4], i, scratch[5 * k + 4].at[i % OWN], (k, i % OWN)) for k, i in homes
    ]
    sems, local = refs[-3:-1], refs[-1]
    me = Place()
    greet(me)
    every = slice(None)

    def at(p, s):
        return homes[p][0][s].at[homes[p][1]]

    def part(p, c):
        array, rows, cols, _ = pieces[p]
        return ins[array].at[every, every, c, every, rows, cols]

    def load(p):
        return pltpu.make_async_copy(part(p, me.c), homes[p][2], local.at[homes[p][3]])

    def pairs(p):
        return [remote(part(p, 1 - me.c), at(p, 0), sems, (p, 0), me.peer(c=1 - me.c))]

    def first(p):
        if pieces[p][3]:
            give, peer = at(p, 0).at[every, every, 1 - me.x], me.peer(x=1 - me.x)
        else:
            give, peer = at(p, 0).at[every, 1 - me.y], me.peer(y=1 - me.y)
        return [remote(give, at(p, 1), sems, (p, 1), peer)]

    def second(p):
        if pieces[p][3]:
            peer, other = me.peer(y=1 - me.y), 1 - me.y
        else:
            peer, other = me.peer(x=1 - me.x), 1 - me.x
        return [remote(at(p, 1).at[every, other], at(p, 2), sems, (p, 2), peer)]

    def third(p):
        return [
            remote(at(p, 2).at[me.up(d)], at(p, 3).at[d - 1], sems, (p, 2 + d), me.peer(z=me.up(d)))
            for d in (1, 2, 3)
        ]

    stages = [pairs, first, second, third]

    def settle(p, s):
        if s == 0:
            load(p).wait()
            add_into(at(p, 0), homes[p][2])
        elif s == 1:
            kept = at(p, 0).at[every, every, me.x] if pieces[p][3] else at(p, 0).at[every, me.y]
            add_into(at(p, 1), kept)
        elif s == 2:
            add_into(at(p, 2), at(p, 1).at[every, me.y if pieces[p][3] else me.x])
        else:
            array, rows, cols, _ = pieces[p]
            more = at(p, 3)
            outs[array][rows, cols] = (
                at(p, 2)[me.z].astype(F32) + more[0].astype(F32) + more[1].astype(F32) + more[2].astype(F32)
            )

    pair = 2

    def begin(p):
        load(p).start()
        for copy in pairs(p):
            copy.start()

    hops = []
    if gains:
        near = [me.peer(c=1 - me.c), me.peer(x=1 - me.x), me.peer(y=1 - me.y)]
        hops = [
            [remote(sum_scr.at[i], got_scr.at[i], (gain_send, gain_recv), i, peer)]
            for i, peer in enumerate(near)
        ] + [[
            remote(sum_scr.at[3], z_scr.at[me.z], (gain_send, gain_recv), 2 + d, me.peer(z=me.up(d)))
            for d in (1, 2, 3)
        ]]

    def gain_step(i):
        if i == 0:
            sum_scr[0] = gain_ref[...]
        else:
            for copy in hops[i - 1]:
                copy.wait_recv()
            if i < 4:
                sum_scr[i] = sum_scr[i - 1] + got_scr[i - 1]
        if i == 3:
            z_scr[me.z] = sum_scr[3]
        if i < 4:
            for copy in hops[i]:
                copy.start()
        else:
            gain_out[...] = (z_scr[0] + z_scr[1]) + (z_scr[2] + z_scr[3])
            for hop in hops:
                for copy in hop:
                    copy.wait_send()

    for p in range(min(n, AHEAD)):
        begin(p)
    rounds = range(0, n + 3 * pair, pair)
    for t in rounds:
        if gains:
            for i in range(5):
                if i * (len(rounds) - 1) // 4 == t // pair:
                    gain_step(i)
        for s in range(4):
            for p in range(t - s * pair, t - s * pair + pair):
                if 0 <= p < n:
                    for copy in stages[s](p):
                        copy.wait_recv()
                    settle(p, s)
                    if s < 3:
                        for copy in stages[s + 1](p):
                            copy.start()
            if s == 0:
                for p in range(t + AHEAD, min(n, t + AHEAD + pair)):
                    begin(p)
    for p in range(n):
        for stage in stages:
            for copy in stage(p):
                copy.wait_send()


def piece_homes(pieces):
    shapes, homes = [], []
    for _, rows, cols, _ in pieces:
        shape = (rows.stop - rows.start, cols.stop - cols.start)
        if shape not in shapes:
            shapes.append(shape)
        kind = shapes.index(shape)
        homes.append((kind, sum(k == kind for k, _ in homes)))
    return shapes, homes


def scatter_call(grads, pieces, collective, gains=()):
    count = len(grads)
    shards = [(g.shape[0] // 32, g.shape[1]) for g in grads]
    grads = [g.reshape((4, 2, 2, 2) + s) for g, s in zip(grads, shards)]
    shapes, homes = piece_homes(pieces)
    scratch = []
    for kind, shape in enumerate(shapes):
        n = sum(k == kind for k, _ in homes)
        scratch += [
            pltpu.VMEM((n, 4, 2, 2) + shape, BF),
            pltpu.VMEM((n, 4, 2) + shape, BF),
            pltpu.VMEM((n, 4) + shape, BF),
            pltpu.VMEM((n, 3) + shape, BF),
            pltpu.VMEM((OWN, 4, 2, 2) + shape, BF),
        ]
    return pl.pallas_call(
        functools.partial(scatter_kernel, pieces, count, len(gains)),
        in_specs=[pl.BlockSpec(memory_space=pl.ANY)] * count
        + [pl.BlockSpec(memory_space=pltpu.VMEM)] * len(gains),
        out_specs=[pl.BlockSpec(memory_space=pltpu.VMEM)] * (count + len(gains)),
        out_shape=[jax.ShapeDtypeStruct(s, F32) for s in shards]
        + [jax.ShapeDtypeStruct(g.shape, F32) for g in gains],
        scratch_shapes=scratch + [
            pltpu.SemaphoreType.DMA((len(pieces), 6)),
            pltpu.SemaphoreType.DMA((len(pieces), 6)),
            pltpu.SemaphoreType.DMA((len(shapes), OWN)),
        ] + [
            scratch
            for g in gains
            for scratch in (
                pltpu.VMEM((4,) + g.shape, F32),
                pltpu.VMEM((3,) + g.shape, F32),
                pltpu.VMEM((4,) + g.shape, F32),
                pltpu.SemaphoreType.DMA((6,)),
                pltpu.SemaphoreType.DMA((6,)),
            )
        ],
        compiler_params=pltpu.CompilerParams(
            collective_id=collective, has_side_effects=True, vmem_limit_bytes=VMEM_LIMIT
        ),
        name="scatter",
    )(*grads, *gains)


def col_pieces(array, rows, cols, width=512, high=None):
    high = high or rows
    return [
        (array, slice(r, r + high), slice(c, c + width), (c // width) % 2 == 0)
        for r in range(0, rows, high)
        for c in range(0, cols, width)
    ]


def interleave(one, two):
    return [p for pair in zip(one, two) for p in pair]


def per_device(
    tokens, segments, cotangent, w_q, w_k, w_v, w_o, w_gate, w_up, w_down, g_attn, g_q, g_k, g_ffn
):
    seqs, rows, width = tokens.shape
    length = segments.shape[1]
    head = g_q.shape[0]
    q_width, kv_width = w_q.shape[1], w_k.shape[1]
    kv_heads = kv_width // head
    q_heads = q_width // head
    total = seqs * rows
    row_start = lax.axis_index("ctx") * rows
    own_kernels = (lax.axis_size("dp"), lax.axis_size("ctx")) == (16, 2)
    share = w_q.shape[0]

    def fetch(weight):
        return lax.all_gather(weight, AXES, axis=0, tiled=True)

    def send(grad):
        return lax.psum_scatter(grad, AXES, scatter_dimension=0, tiled=True).astype(F32)

    seg_rows = lax.dynamic_slice_in_dim(segments, row_start, rows, 1)
    first = jnp.sum((segments[:, None, :] < seg_rows[:, :, None]).astype(jnp.int32), axis=-1)
    query_pos = row_start + jnp.arange(rows, dtype=jnp.int32)
    positions = (query_pos[None, :] - first).reshape(total)
    frequency = rope_base ** (-jnp.arange(0, head, 2, dtype=F32) / head)
    angles = positions.astype(F32)[:, None] * frequency[None, :]
    cos, sin = jnp.cos(angles), jnp.sin(angles)
    cos = jnp.concatenate([cos] * (2 * LANES // head), axis=1)
    sin = jnp.concatenate([-sin, sin] * (LANES // head), axis=1)
    wide = 2 * LANES
    member = jnp.arange(wide) // head
    ones = (member[:, None] == member[None, :]).astype(BF)
    gains_q = jnp.concatenate([g_q] * q_heads)[None, :]
    gains_k = jnp.concatenate([g_k] * kv_heads)[None, :]
    x = tokens.reshape(total, width)
    cotangent = cotangent.reshape(total, width)

    w_qkv = jnp.concatenate([w_q, w_k, w_v], axis=1)
    w_gate, w_down = fetch(w_gate), fetch(w_down)
    grad_low = cotangent.astype(BF)
    if own_kernels:
        up_pieces = col_pieces(0, share, w_up.shape[1], 256)
        qkv_pieces = col_pieces(0, share, w_qkv.shape[1])
        o_pieces = col_pieces(0, share, w_o.shape[1])
        [w_qkv] = gather_call([w_qkv], qkv_pieces, 0)
    else:
        w_qkv, w_o, w_up = fetch(w_qkv), fetch(w_o), fetch(w_up)

    tables = (cos, sin, ones, head)
    normed, kv, raw_k = project_call(
        x, w_qkv, (q_width, 2 * kv_width), kv_width, g_attn[None, :], gains_k, *tables, None, "project_kv"
    )
    kv = kv.reshape(seqs, rows, 2 * kv_width)
    if own_kernels:
        before = lax.ppermute(kv, "ctx", [(0, 1)])
    _, q, raw_q = project_call(
        x, w_qkv, (0, q_width), q_width, g_attn[None, :], gains_q, *tables, head ** (-0.5), "project_q"
    )
    q = q.reshape(seqs, rows, q_width)
    block_q, block_k = min(128, rows), 128
    at = jnp.arange(0, rows, block_q, dtype=jnp.int32)[None, :]
    lowest = first[:, ::block_q]
    zero = jnp.zeros((1,), jnp.int32)
    if own_kernels:
        own_first = first - row_start
        own_keys = (
            jnp.maximum(lowest - row_start, 0) // block_k,
            jnp.broadcast_to((at + block_q - 1) // block_k + 1, lowest.shape),
            zero,
        )
        far_first = own_first + rows
        far_keys = (
            jnp.clip(lowest - row_start + rows, 0, rows) // block_k,
            jnp.full(lowest.shape, rows // block_k, jnp.int32),
            zero + rows,
        )
        near = attend_call(q, kv, own_first, own_keys, block_q, block_k, last_part=False)
        w_o, _ = lax.optimization_barrier((w_o, near))
        [w_o] = gather_call([w_o], o_pieces, 4)
        mixed, totals = attend_call(q, before, far_first, far_keys, block_q, block_k, near)
    else:
        kv = lax.all_gather(kv, "ctx", axis=1, tiled=True)
        all_keys = (
            lowest // block_k,
            jnp.broadcast_to((row_start + at + block_q - 1) // block_k + 1, lowest.shape),
            zero + row_start,
        )
        mixed, totals = attend_call(q, kv, first, all_keys, block_q, block_k)
    mixed, totals = mixed.reshape(total, q_width), totals.reshape(total, q_width)
    attended, hidden, normed_two = hidden_call(mixed, w_o, x, g_ffn[None, :])

    if own_kernels:
        normed_two, w_up = lax.optimization_barrier((normed_two, w_up))
        [w_up] = gather_call([w_up], up_pieces, 1)
        ffn, d_normed_two, grad_down, out_gate, out_up = ffn_call(
            normed_two, grad_low, w_gate, w_up, w_down, 2
        )
    else:
        ffn, d_normed_two, grad_down, out_gate, out_up = ffn_call(
            normed_two, grad_low, w_gate, w_up, w_down
        )
        out_gate, out_up = send(out_gate), send(out_up)
    out_down = send(grad_down)
    outputs, d_hidden, d_low, d_out, delta, grad_gffn = middle_call(
        ffn, d_normed_two, hidden, cotangent, g_ffn[None, :], w_o, mixed, totals, ones, head
    )
    d_out, delta = d_out.reshape(q.shape), delta.reshape(q.shape)
    if own_kernels:
        far_dq, dk, dv = attend_back_call(
            q, d_out, delta, before, far_first, far_keys, block_q, block_k
        )
        got = lax.ppermute(jnp.concatenate([dk, dv], axis=2), "ctx", [(1, 0)])
        dq, dk, dv = attend_back_call(
            q, d_out, delta, kv, own_first, own_keys, block_q, block_k, (far_dq,)
        )
        dk, dv, got = dk.reshape(total, kv_width), dv.reshape(total, kv_width), (got.reshape(total, -1),)
    else:
        dq, dk, dv = attend_back_call(q, d_out, delta, kv, first, all_keys, block_q, block_k)
        dkv = lax.psum_scatter(
            jnp.concatenate([dk, dv], axis=2), "ctx", scatter_dimension=1, tiled=True
        ).reshape(total, 2 * kv_width)
        dk, dv, got = dkv[:, :kv_width], dkv[:, kv_width:], ()
    grad_o = mm(attended, d_low, TN).astype(BF)
    d_qkv, input_grad, grad_gattn, grad_gq, grad_gk = last_call(
        dq.reshape(total, q_width), dk, dv, raw_q, raw_k,
        jnp.concatenate([gains_q, gains_k], axis=1), cos, sin, ones,
        w_qkv, x, g_attn[None, :], d_hidden, head, got,
    )
    grad_qkv = mm(normed, d_qkv, TN).astype(BF)
    if own_kernels:
        flat = jnp.concatenate([grad_gattn, grad_gffn, grad_gq, grad_gk], axis=1).reshape(-1, LANES)
        flat = jnp.pad(flat, ((0, -flat.shape[0] % 8), (0, 0)))
        o_pieces = [(1,) + p[1:] for p in o_pieces]
        out_qkv, out_o, flat = scatter_call([grad_qkv, grad_o], o_pieces + qkv_pieces, 3, (flat,))
        flat = flat.reshape(1, -1)
        grad_gattn, grad_gffn = flat[:, :width], flat[:, width : 2 * width]
        grad_gq = flat[:, 2 * width : 2 * width + LANES]
        grad_gk = flat[:, 2 * width + LANES : 2 * width + 2 * LANES]
    else:
        out_qkv, out_o = send(grad_qkv), send(grad_o)
        grad_gattn, grad_gffn, grad_gq, grad_gk = lax.psum(
            (grad_gattn, grad_gffn, grad_gq, grad_gk), AXES
        )

    def fold(grad):
        return jnp.sum(grad.reshape(LANES // head, head), axis=0)

    return (
        outputs.reshape(tokens.shape),
        input_grad.reshape(tokens.shape),
        out_qkv[:, :q_width],
        out_qkv[:, q_width : q_width + kv_width],
        out_qkv[:, q_width + kv_width :],
        out_o,
        out_gate,
        out_up,
        out_down,
        grad_gattn[0],
        fold(grad_gq),
        fold(grad_gk),
        grad_gffn[0],
    )


def solution(mesh):
    split = P("dp", "ctx", None)
    shard = P(("dp", "ctx"), None)
    in_specs = (split, P("dp", None), split) + (shard,) * 7 + (P(),) * 4
    out_specs = (split, split) + (shard,) * 7 + (P(),) * 4
    return jax.shard_map(
        per_device, mesh=mesh, in_specs=in_specs, out_specs=out_specs, check_vma=False
    )
```

```python
import functools

import jax
import jax.numpy as jnp
from jax import lax
from jax.experimental import pallas as pl
from jax.experimental.pallas import tpu as pltpu
from jax.sharding import PartitionSpec as P

epsilon = 1e-05
rope_base = 1000000.0
AXES = ("dp", "ctx")
BF = jnp.bfloat16
F32 = jnp.float32
LANES = 128
VMEM_LIMIT = 56 * 2**20
AHEAD = 4
OWN = 6
NN = (((1,), (0,)), ((), ()))
NT = (((1,), (1,)), ((), ()))
TN = (((0,), (0,)), ((), ()))


def mm(a, b, dims=NN):
    return lax.dot_general(a, b, dims, preferred_element_type=F32)


def params(semantics=None):
    return pltpu.CompilerParams(
        vmem_limit_bytes=VMEM_LIMIT,
        dimension_semantics=semantics,
    )


def resident(shape):
    zeros = (0,) * len(shape)
    return pl.BlockSpec(shape, lambda *_: zeros, pipeline_mode=pl.Buffered(1))


def largest_block(size, most):
    return max(b for b in range(1, min(size, most) + 1) if size % b == 0)


def head_sum(field, ones):
    wide = ones.shape[0]
    high = field.astype(BF)
    low = (field - high.astype(F32)).astype(BF)
    parts = [
        mm(high[:, c : c + wide], ones) + mm(low[:, c : c + wide], ones)
        for c in range(0, field.shape[1], wide)
    ]
    return jnp.concatenate(parts, axis=1)


def swap_halves(field, head):
    half = head // 2
    width = field.shape[1]
    lane = lax.broadcasted_iota(jnp.int32, field.shape, 1)
    return jnp.where(
        lane % head < half,
        pltpu.roll(field, width - half, 1),
        pltpu.roll(field, half, 1),
    )


def spread(table, width):
    return jnp.concatenate([table] * (width // table.shape[1]), axis=1)


def project_kernel(
    rope_width, head, scale,
    x_ref, w_ref, g_ref, gain_ref, cos_ref, sin_ref, ones_ref,
    normed_ref, out_ref, raw_ref,
):
    x = x_ref[...].astype(F32)
    inverse = lax.rsqrt(jnp.mean(x * x, axis=-1, keepdims=True) + epsilon)
    normed = (x * inverse * g_ref[...]).astype(BF)
    normed_ref[...] = normed
    ones = ones_ref[...]
    wide = ones.shape[0]
    cos = spread(cos_ref[...], wide)
    sin = spread(sin_ref[...], wide)
    for c in range(0, rope_width, wide):
        raw = mm(normed, w_ref[:, c : c + wide])
        raw_ref[:, c : c + wide] = raw
        inv = lax.rsqrt(head_sum(raw * raw, ones) * (1.0 / head) + epsilon)
        field = raw * inv * gain_ref[:, c : c + wide]
        turned = (field * cos + swap_halves(field, head) * sin).astype(BF)
        out_ref[:, c : c + wide] = turned if scale is None else turned * jnp.asarray(scale, BF)
    if rope_width < w_ref.shape[1]:
        out_ref[:, rope_width:] = mm(normed, w_ref[:, rope_width:]).astype(BF)


def project_call(x, w, cols, rope_width, g, gains, cos, sin, ones, head, scale, name):
    total, width = x.shape
    block = largest_block(total, 256)
    at, count = cols[0] // cols[1], cols[1]

    def rows(n):
        return pl.BlockSpec((block, n), lambda i: (i, 0))

    return pl.pallas_call(
        functools.partial(project_kernel, rope_width, head, scale),
        grid=(total // block,),
        in_specs=[
            rows(width),
            pl.BlockSpec((width, count), lambda i: (0, at), pipeline_mode=pl.Buffered(1)),
            resident(g.shape), resident(gains.shape),
            rows(LANES), rows(LANES), resident(ones.shape),
        ],
        out_specs=[rows(width), rows(count), rows(rope_width)],
        out_shape=[
            jax.ShapeDtypeStruct((total, width), BF),
            jax.ShapeDtypeStruct((total, count), BF),
            jax.ShapeDtypeStruct((total, rope_width), F32),
        ],
        compiler_params=params(),
        cost_estimate=pl.CostEstimate(
            flops=2 * total * width * count, bytes_accessed=2 * width * count + 10 * total * count,
            transcendentals=0,
        ),
        name=name,
    )(x, w, g, gains, cos, sin, ones)


def pad_head(pair, odd, fill):
    lane = lax.broadcasted_iota(jnp.int32, pair.shape, 1)
    if odd:
        pair = pltpu.roll(pair, LANES // 2, 1)
    return jnp.where(lane < LANES // 2, pair, jnp.asarray(fill, pair.dtype))


def attend_kernel(
    block_q, block_k, heads, more, last_part,
    low_ref, high_ref, start_ref, q_ref, k_ref, v_ref, first_ref, *refs,
):
    prior = refs[:2] if more else ()
    out_ref, total_ref, k_scr, v_scr = refs[len(prior) :]
    s = pl.program_id(0)
    rows = q_ref.shape[1]
    start = start_ref[0]
    half = LANES // 2
    for h in range(heads):
        c = h // 2 * LANES
        k_scr[h] = pad_head(k_ref[0, :, c : c + LANES].astype(F32), h % 2, 0).astype(BF)
        v_scr[h] = pad_head(v_ref[0, :, c : c + LANES].astype(F32), h % 2, 1).astype(BF)
    lane = lax.broadcasted_iota(jnp.int32, (block_q, LANES), 1)
    key_lane = lax.broadcasted_iota(jnp.int32, (2 * block_q, block_k), 1)
    row = lax.broadcasted_iota(jnp.int32, (2 * block_q, 1), 0) % block_q

    def q_step(i, carry):
        at = pl.multiple_of(i * block_q, block_q)
        first = first_ref[0, pl.ds(at, block_q), :]
        first = jnp.concatenate([first, first], axis=0)
        last = row + (start + at)
        queries = []
        for h in range(heads):
            pair = q_ref[0, pl.ds(at, block_q), h * LANES : (h + 1) * LANES].astype(F32)
            queries.append(
                jnp.concatenate([pad_head(pair, 0, 0), pad_head(pair, 1, 0)], axis=0).astype(BF)
            )

        def k_step(j, sums):
            key_at = pl.multiple_of(j * block_k, block_k)
            key = key_lane + key_at
            live = (key >= first) & (key <= last)
            new = []
            for h in range(heads):
                scores = mm(queries[h], k_scr[h, pl.ds(key_at, block_k), :], NT)
                expo = jnp.where(live, jnp.exp(scores), 0.0).astype(BF)
                new.append(sums[h] + mm(expo, v_scr[h, pl.ds(key_at, block_k), :]))
            return tuple(new)

        sums = lax.fori_loop(
            low_ref[s, i], high_ref[s, i], k_step,
            tuple(jnp.zeros((2 * block_q, LANES), F32) for _ in range(heads)),
        )
        for h in range(heads):
            even, odd = sums[h][:block_q], sums[h][block_q:]
            both = jnp.where(lane < half, even, pltpu.roll(odd, half, 1))
            tot = jnp.where(lane < half, pltpu.roll(even, half, 1), odd)
            cols = slice(h * LANES, (h + 1) * LANES)
            if more:
                both += prior[0][0, pl.ds(at, block_q), cols]
                tot += prior[1][0, pl.ds(at, block_q), cols]
            out_ref[0, pl.ds(at, block_q), cols] = both / tot if last_part else both
            total_ref[0, pl.ds(at, block_q), cols] = tot
        return carry

    lax.fori_loop(0, rows // block_q, q_step, 0)


def attend_call(q, kv, first, keys, block_q, block_k, prior=(), last_part=True):
    seqs, rows, q_width = q.shape
    length = kv.shape[1]
    kv_heads = q_width // LANES
    heads = largest_block(kv_heads, 8)
    steps = kv_heads // heads
    half = LANES // 2
    spec_q = pl.BlockSpec((1, rows, heads * LANES), lambda s, p, *_: (s, 0, p))
    return pl.pallas_call(
        functools.partial(attend_kernel, block_q, block_k, heads, bool(prior), last_part),
        grid_spec=pltpu.PrefetchScalarGridSpec(
            num_scalar_prefetch=3,
            grid=(seqs, steps),
            in_specs=[
                spec_q,
                pl.BlockSpec((1, length, heads * half), lambda s, p, *_: (s, 0, p)),
                pl.BlockSpec((1, length, heads * half), lambda s, p, *_: (s, 0, p + steps)),
                pl.BlockSpec((1, rows, 1), lambda s, p, *_: (s, 0, 0)),
            ] + [spec_q] * len(prior),
            out_specs=[spec_q, spec_q],
            scratch_shapes=[
                pltpu.VMEM((heads, length, LANES), BF),
                pltpu.VMEM((heads, length, LANES), BF),
            ],
        ),
        out_shape=[jax.ShapeDtypeStruct(q.shape, F32)] * 2,
        compiler_params=params(),
        cost_estimate=pl.CostEstimate(
            flops=4 * seqs * rows * length * q_width, bytes_accessed=16 * seqs * rows * q_width,
            transcendentals=0,
        ),
        name="attend",
    )(*keys, q, kv, kv, first[:, :, None], *prior)


def attend_back_kernel(
    block_q, block_k, heads, more,
    low_ref, high_ref, start_ref, q_ref, do_ref, de_ref, k_ref, v_ref, first_ref, *refs,
):
    prior_ref = refs[0] if more else None
    dq_ref, dk_ref, dv_ref, k_scr, v_scr, dk_scr, dv_scr = refs[int(more) :]
    s = pl.program_id(0)
    rows = q_ref.shape[1]
    length = k_ref.shape[1]
    start = start_ref[0]
    half = LANES // 2
    for h in range(heads):
        c = h // 2 * LANES
        k_scr[h] = pad_head(k_ref[0, :, c : c + LANES].astype(F32), h % 2, 0).astype(BF)
        v_scr[h] = pad_head(v_ref[0, :, c : c + LANES].astype(F32), h % 2, 1).astype(BF)
    dk_scr[...] = jnp.zeros_like(dk_scr)
    dv_scr[...] = jnp.zeros_like(dv_scr)
    lane = lax.broadcasted_iota(jnp.int32, (block_q, LANES), 1)
    key_row = lax.broadcasted_iota(jnp.int32, (block_k, 2 * block_q), 0)
    column = lax.broadcasted_iota(jnp.int32, (1, 2 * block_q), 1) % block_q

    def tail(pair, odd, delta):
        if odd:
            pair = pltpu.roll(pair, half, 1)
        else:
            delta = pltpu.roll(delta, half, 1)
        part0 = delta.astype(BF).astype(F32)
        part1 = (delta - part0).astype(BF).astype(F32)
        part2 = delta - part0 - part1
        rest = jnp.where(
            lane == half, part0, jnp.where(lane == half + 1, part1, jnp.where(lane == half + 2, part2, 0.0))
        )
        return jnp.where(lane < half, pair, -rest)

    def q_step(i, carry):
        at = pl.multiple_of(i * block_q, block_q)
        first = first_ref[0, :, pl.ds(at, block_q)]
        first = jnp.concatenate([first, first], axis=1)
        last = column + (start + at)
        queries, grads = [], []
        for h in range(heads):
            cols = slice(h * LANES, (h + 1) * LANES)
            pair = q_ref[0, pl.ds(at, block_q), cols].astype(F32)
            queries.append(
                jnp.concatenate([pad_head(pair, 0, 0), pad_head(pair, 1, 0)], axis=0).astype(BF)
            )
            pair = do_ref[0, pl.ds(at, block_q), cols].astype(F32)
            delta = de_ref[0, pl.ds(at, block_q), cols]
            grads.append(
                jnp.concatenate([tail(pair, 0, delta), tail(pair, 1, delta)], axis=0).astype(BF)
            )

        def k_step(j, sums):
            key_at = pl.multiple_of(j * block_k, block_k)
            key = key_row + key_at
            live = (key >= first) & (key <= last)
            new = []
            for h in range(heads):
                k = k_scr[h, pl.ds(key_at, block_k), :]
                v = v_scr[h, pl.ds(key_at, block_k), :]
                scores = mm(k, queries[h], NT)
                expo = jnp.where(live, jnp.exp(scores), 0.0)
                change = mm(v, grads[h], NT)
                d_scores = (expo * change).astype(BF)
                dv_scr[h, pl.ds(key_at, block_k), :] += mm(expo.astype(BF), grads[h])
                dk_scr[h, pl.ds(key_at, block_k), :] += mm(d_scores, queries[h])
                new.append(sums[h] + mm(d_scores, k, TN))
            return tuple(new)

        sums = lax.fori_loop(
            low_ref[s, i], high_ref[s, i], k_step,
            tuple(jnp.zeros((2 * block_q, LANES), F32) for _ in range(heads)),
        )
        for h in range(heads):
            even, odd = sums[h][:block_q], sums[h][block_q:]
            cols = slice(h * LANES, (h + 1) * LANES)
            grad = jnp.where(lane < half, even, pltpu.roll(odd, half, 1))
            if more:
                grad += prior_ref[0, pl.ds(at, block_q), cols]
            dq_ref[0, pl.ds(at, block_q), cols] = grad
        return carry

    lax.fori_loop(0, rows // block_q, q_step, 0)
    wide = lax.broadcasted_iota(jnp.int32, (length, LANES), 1)
    for h in range(0, heads, 2):
        cols = slice(h // 2 * LANES, (h // 2 + 1) * LANES)
        for grad, scr in ((dk_ref, dk_scr), (dv_ref, dv_scr)):
            grad[0, :, cols] = jnp.where(
                wide < half, scr[h], pltpu.roll(scr[h + 1], half, 1)
            ).astype(BF)


def attend_back_call(q, d_out, delta, kv, first, keys, block_q, block_k, prior=()):
    seqs, rows, q_width = q.shape
    length = kv.shape[1]
    kv_width = kv.shape[2] // 2
    kv_heads = q_width // LANES
    heads = largest_block(kv_heads, 8)
    steps = kv_heads // heads
    half = LANES // 2
    spec_q = pl.BlockSpec((1, rows, heads * LANES), lambda s, p, *_: (s, 0, p))
    spec_kv = pl.BlockSpec((1, length, heads * half), lambda s, p, *_: (s, 0, p))
    return pl.pallas_call(
        functools.partial(attend_back_kernel, block_q, block_k, heads, bool(prior)),
        grid_spec=pltpu.PrefetchScalarGridSpec(
            num_scalar_prefetch=3,
            grid=(seqs, steps),
            in_specs=[
                spec_q, spec_q, spec_q, spec_kv,
                pl.BlockSpec((1, length, heads * half), lambda s, p, *_: (s, 0, p + steps)),
                pl.BlockSpec((1, 1, rows), lambda s, p, *_: (s, 0, 0)),
            ] + [spec_q] * len(prior),
            out_specs=[spec_q, spec_kv, spec_kv],
            scratch_shapes=[
                pltpu.VMEM((heads, length, LANES), BF),
                pltpu.VMEM((heads, length, LANES), BF),
                pltpu.VMEM((heads, length, LANES), F32),
                pltpu.VMEM((heads, length, LANES), F32),
            ],
        ),
        out_shape=[
            jax.ShapeDtypeStruct(q.shape, F32),
            jax.ShapeDtypeStruct((seqs, length, kv_width), BF),
            jax.ShapeDtypeStruct((seqs, length, kv_width), BF),
        ],
        compiler_params=params(),
        cost_estimate=pl.CostEstimate(
            flops=10 * seqs * rows * length * q_width, bytes_accessed=16 * seqs * rows * q_width,
            transcendentals=0,
        ),
        name="attend_back",
    )(*keys, q, d_out, delta, kv, kv, first[:, None, :], *prior)


def hidden_kernel(a_ref, w_ref, x_ref, g_ref, att_ref, hidden_ref, normed_ref):
    attended = a_ref[...].astype(BF)
    att_ref[...] = attended
    hidden = x_ref[...].astype(F32) + mm(attended, w_ref[...])
    hidden_ref[...] = hidden
    inverse = lax.rsqrt(jnp.mean(hidden * hidden, axis=-1, keepdims=True) + epsilon)
    normed_ref[...] = (hidden * inverse * g_ref[...]).astype(BF)


def hidden_call(mixed, w_o, x, g):
    total, width = x.shape
    q_width = mixed.shape[1]
    block = largest_block(total, 256)

    def rows(n):
        return pl.BlockSpec((block, n), lambda i: (i, 0))

    return pl.pallas_call(
        hidden_kernel,
        grid=(total // block,),
        in_specs=[rows(q_width), resident(w_o.shape), rows(width), resident(g.shape)],
        out_specs=[rows(q_width), rows(width), rows(width)],
        out_shape=[
            jax.ShapeDtypeStruct((total, q_width), BF),
            jax.ShapeDtypeStruct((total, width), F32),
            jax.ShapeDtypeStruct((total, width), BF),
        ],
        compiler_params=params(),
        name="hidden",
    )(mixed, w_o, x, g)


def ffn_block(block_t, n_ref, c_ref, wg, wu, wd, out_ref, dn_ref, act_scr, dg_scr, du_scr):
    total = n_ref.shape[0]

    def t_step(i, carry):
        at = pl.ds(pl.multiple_of(i * block_t, block_t), block_t)
        normed = n_ref[at, :]
        gate = mm(normed, wg())
        up = mm(normed, wu())
        d_act = mm(c_ref[at, :], wd(), NT)
        sig = 1.0 / (1.0 + jnp.exp(-gate))
        silu = gate * sig
        act = (silu * up).astype(BF)
        d_gate = (d_act * up * (sig * (1.0 + gate - silu))).astype(BF)
        d_up = (d_act * silu).astype(BF)
        act_scr[at, :] = act
        dg_scr[at, :] = d_gate
        du_scr[at, :] = d_up
        out_ref[at, :] += mm(act, wd())
        dn_ref[at, :] += mm(d_gate, wg(), NT) + mm(d_up, wu(), NT)
        return carry

    lax.fori_loop(0, total // block_t, t_step, 0, unroll=total // block_t)


def down_grad(gd_ref, act_scr, c_ref):
    for c in range(0, act_scr.shape[1], 256):
        gd_ref[c : c + 256, :] = mm(act_scr[:, c : c + 256], c_ref[...], TN).astype(BF)


def ffn_kernel(
    block_t,
    n_ref, c_ref, wg_ref, wu_ref, wd_ref,
    out_ref, dn_ref, gd_ref, gg_ref, gu_ref,
    n_scr, act_scr, dg_scr, du_scr,
):
    @pl.when(pl.program_id(0) == 0)
    def _():
        n_scr[...] = n_ref[...].T
        out_ref[...] = jnp.zeros_like(out_ref)
        dn_ref[...] = jnp.zeros_like(dn_ref)

    ffn_block(
        block_t, n_ref, c_ref, lambda: wg_ref[...], lambda: wu_ref[...], lambda: wd_ref[...],
        out_ref, dn_ref, act_scr, dg_scr, du_scr,
    )

    def d_step(i, carry):
        at = pl.ds(pl.multiple_of(i * 256, 256), 256)
        normed = n_scr[at, :]
        gg_ref[at, :] = mm(normed, dg_scr[...]).astype(BF)
        gu_ref[at, :] = mm(normed, du_scr[...]).astype(BF)
        return carry

    width = n_ref.shape[1]
    lax.fori_loop(0, width // 256, d_step, 0, unroll=width // 256)
    down_grad(gd_ref, act_scr, c_ref)


def ffn_call(normed, grad_low, w_gate, w_up, w_down):
    total, width = normed.shape
    hidden = w_gate.shape[1]
    chunk = largest_block(hidden, 512)
    block_t = largest_block(total, 256)
    cols = pl.BlockSpec((width, chunk), lambda i: (0, i))
    rows = pl.BlockSpec((chunk, width), lambda i: (i, 0))
    return pl.pallas_call(
        functools.partial(ffn_kernel, block_t),
        grid=(hidden // chunk,),
        in_specs=[resident(normed.shape), resident(normed.shape), cols, cols, rows],
        out_specs=[resident(normed.shape), resident(normed.shape), rows, cols, cols],
        out_shape=[
            jax.ShapeDtypeStruct((total, width), F32),
            jax.ShapeDtypeStruct((total, width), F32),
            jax.ShapeDtypeStruct(w_down.shape, BF),
            jax.ShapeDtypeStruct(w_gate.shape, BF),
            jax.ShapeDtypeStruct(w_gate.shape, BF),
        ],
        scratch_shapes=[
            pltpu.VMEM((width, total), BF),
            pltpu.VMEM((total, chunk), BF),
            pltpu.VMEM((total, chunk), BF),
            pltpu.VMEM((total, chunk), BF),
        ],
        compiler_params=params(),
        name="ffn",
    )(normed, grad_low, w_gate, w_up, w_down)


class ColumnGather:
    def __init__(self, me, own, whole, slots, send, recv, keep_sems, load_sems):
        self.me, self.own, self.whole, self.slots = me, own, whole, slots
        self.sems, self.keep_sems, self.load_sems = (send, recv), keep_sems, load_sems

    def cols(self, k):
        width = self.slots.shape[-1]
        start = k * width
        return pl.ds(start if isinstance(k, int) else pl.multiple_of(start, width), width)

    def keep(self, j):
        me = self.me
        return pltpu.make_async_copy(
            self.own[j], self.whole[j].at[me.z, me.y, me.c, me.x], self.keep_sems.at[j]
        )

    def hop(self, k, j, s):
        me, every = self.me, slice(None)
        whole = self.whole[j]

        def mine(z, y, c, x):
            return whole.at[z, y, c, x, every, self.cols(k)]

        if s == 0:
            give = self.own[j].at[:, self.cols(k)]
            return [
                remote(give, mine(me.z, me.y, me.c, me.x), self.sems, (k, j, d - 1), me.peer(z=me.up(d)))
                for d in (1, 2, 3)
            ]
        to_x, to_y = me.peer(x=1 - me.x), me.peer(y=1 - me.y)
        if s == 1:
            give, peer = mine(every, me.y, me.c, me.x), (to_x if j == 0 else to_y)
        elif s == 2 and j == 0:
            give, peer = mine(every, me.y, me.c, every), to_y
        elif s == 2:
            give, peer = mine(every, every, me.c, me.x), to_x
        else:
            give, peer = mine(every, every, me.c, every), me.peer(c=1 - me.c)
        return [remote(give, give, self.sems, (k, j, 2 + s), peer)]

    def load(self, k, j):
        every = slice(None)
        slot = k % 2 if isinstance(k, int) else lax.rem(k, 2)
        return pltpu.make_async_copy(
            self.whole[j].at[every, every, every, every, every, self.cols(k)],
            self.slots.at[slot, j], self.load_sems.at[slot, j],
        )

    def start(self, k, s):
        for j in (0, 1):
            for copy in self.hop(k, j, s):
                copy.start()

    def wait(self, k, s):
        for j in (0, 1):
            for copy in self.hop(k, j, s):
                copy.wait()

    def open(self):
        for j in (0, 1):
            self.keep(j).start()
        for k in range(3):
            self.start(k, 0)
        for j in (0, 1):
            self.keep(j).wait()
        for k, s in ((0, 1), (1, 1), (0, 2), (2, 1), (1, 2), (0, 3), (3, 1), (2, 2), (1, 3), (4, 1), (3, 2), (5, 1)):
            self.wait(k, s - 1)
            self.start(k, s)
            if s == 1:
                self.start(k + 3, 0)
        self.fetch(0)

    def fetch(self, k):
        self.wait(k, 3)
        for j in (0, 1):
            self.load(k, j).start()

    def ready(self, k):
        for j in (0, 1):
            self.load(k, j).wait()

    def advance(self, step, steps):
        for s, early in ((1, 6), (2, 4), (3, 2)):
            k = step + early

            @pl.when(k < steps)
            def _(k=k, s=s):
                self.wait(k, s - 1)
                self.start(k, s)

        @pl.when(step + 9 < steps)
        def _():
            self.start(step + 9, 0)

        @pl.when(step + 1 < steps)
        def _():
            self.fetch(step + 1)


class GradSums:
    def __init__(self, me, outs, made, r0, r1, r2, r3, send, recv):
        self.me, self.outs, self.made = me, outs, made
        self.r0, self.r1, self.r2, self.r3, self.send, self.recv = r0, r1, r2, r3, send, recv

    def keep(self, step, i, j, grad):
        self.made[lax.rem(step, 2), j, i] = grad.astype(BF).reshape(self.made.shape[3:])

    def hop(self, k, j, s):
        me, every = self.me, slice(None)
        sems = (self.send, self.recv)
        r0, r1, r2, r3 = (r.at[k, j] for r in (self.r0, self.r1, self.r2, self.r3))
        to_x, to_y = me.peer(x=1 - me.x), me.peer(y=1 - me.y)
        if s == 0:
            give = self.made.at[lax.rem(k, 2), j, every, every, 1 - me.c]
            return [remote(give, r0, sems, (k, j, 0), me.peer(c=1 - me.c))]
        if s == 1:
            if j == 0:
                return [remote(r0.at[every, every, 1 - me.x], r1, sems, (k, j, 1), to_x)]
            return [remote(r0.at[every, 1 - me.y], r1, sems, (k, j, 1), to_y)]
        if s == 2:
            other, peer = (1 - me.y, to_y) if j == 0 else (1 - me.x, to_x)
            return [remote(r1.at[every, other], r2, sems, (k, j, 2), peer)]
        return [
            remote(r2.at[me.up(d)], r3.at[d - 1], sems, (k, j, 2 + d), me.peer(z=me.up(d)))
            for d in (1, 2, 3)
        ]

    def settle(self, k, j, s):
        me, every = self.me, slice(None)
        r0, r1, r2, r3 = (r.at[k, j] for r in (self.r0, self.r1, self.r2, self.r3))
        for copy in self.hop(k, j, s):
            copy.wait()
        if s == 0:
            add_into(r0, self.made.at[lax.rem(k, 2), j, every, every, me.c])
        elif s == 1:
            add_into(r1, r0.at[every, every, me.x] if j == 0 else r0.at[every, me.y])
        elif s == 2:
            add_into(r2, r1.at[every, me.y if j == 0 else me.x])
        else:
            width = r2.shape[-1]
            cols = pl.ds(pl.multiple_of(k * width, width), width)
            self.outs[j][:, cols] = (
                r2[me.z].astype(F32) + r3[0].astype(F32) + r3[1].astype(F32) + r3[2].astype(F32)
            )

    def advance(self, step, steps):
        for s, late in ((3, 6), (2, 5), (1, 3), (0, 1)):
            k = step - late

            @pl.when((k >= 0) & (k < steps))
            def _(s=s, k=k):
                for j in (0, 1):
                    self.settle(k, j, s)
                    if s < 3:
                        for copy in self.hop(k, j, s + 1):
                            copy.start()


def feed_kernel(
    block_t, steps, block_m, head,
    n_ref, c_ref, wd_ref, own_gate, own_up, h_ref, cot_ref, g_ref, w_ref, o_ref, l_ref, ones_ref,
    gd_ref, gg_ref, gu_ref, all_gate, all_up, out_ref, dh_ref, low_ref, do_ref, de_ref, gain_ref,
    n_scr, act_scr, dg_scr, du_scr, f_scr, dn_scr, slots, made, r0, r1, r2, r3,
    g_send, g_recv, s_send, s_recv, keep_sems, load_sems,
):
    step = pl.program_id(0)
    me = Place()
    gather = ColumnGather(
        me, (own_gate, own_up), (all_gate, all_up), slots, g_send, g_recv, keep_sems, load_sems
    )
    sums = GradSums(me, (gg_ref, gu_ref), made, r0, r1, r2, r3, s_send, s_recv)

    @pl.when(step == 0)
    def _():
        greet(me)
        n_scr[...] = n_ref[...].T
        f_scr[...] = jnp.zeros_like(f_scr)
        dn_scr[...] = jnp.zeros_like(dn_scr)
        gather.open()

    @pl.when(step < steps)
    def _():
        gather.ready(step)
        slot = lax.rem(step, 2)
        width, chunk = n_ref.shape[1], wd_ref.shape[0]
        ffn_block(
            block_t, n_ref, c_ref,
            lambda: slots[slot, 0].reshape(width, chunk),
            lambda: slots[slot, 1].reshape(width, chunk),
            lambda: wd_ref[...],
            f_scr, dn_scr, act_scr, dg_scr, du_scr,
        )
        for i in range(width // 256):
            normed = n_scr[256 * i : 256 * i + 256, :]
            sums.keep(step, i, 0, mm(normed, dg_scr[...]))
            sums.keep(step, i, 1, mm(normed, du_scr[...]))
        down_grad(gd_ref, act_scr, c_ref)

    gather.advance(step, steps)
    sums.advance(step, steps)

    @pl.when(step < steps)
    def _():
        for j in (0, 1):
            for copy in sums.hop(step, j, 0):
                copy.start()

    @pl.when(step == steps)
    def _():
        gain_ref[...] = jnp.zeros_like(gain_ref)

    @pl.when(step >= steps)
    def _():
        at = pl.ds(pl.multiple_of((step - steps) * block_m, block_m), block_m)
        middle_block(
            head, f_scr[at, :], dn_scr[at, :], h_ref, cot_ref, g_ref, w_ref, o_ref, l_ref, ones_ref,
            out_ref, dh_ref, low_ref, do_ref, de_ref, gain_ref,
        )


def feed_call(
    normed, grad_low, w_down, own_gate, own_up, hidden, cotangent, g, w_o, mixed, totals, ones, head,
    collective,
):
    total, width = normed.shape
    share, units = own_gate.shape
    q_width = mixed.shape[1]
    chunk = largest_block(units, 512)
    steps = units // chunk
    block_t, block_m = largest_block(total, 256), largest_block(total, 128)
    last = steps - 1
    piece = (share, chunk)

    def after(n):
        return pl.BlockSpec((block_m, n), lambda i: (jnp.maximum(i - steps, 0), 0))

    anywhere = pl.BlockSpec(memory_space=pl.ANY)
    rows = pl.BlockSpec((chunk, width), lambda i: (jnp.minimum(i, last), 0))
    whole = jax.ShapeDtypeStruct((4, 2, 2, 2, share, units), BF)
    outs = pl.pallas_call(
        functools.partial(feed_kernel, block_t, steps, block_m, head),
        grid=(steps + total // block_m,),
        in_specs=[
            resident(normed.shape), resident(normed.shape), rows, anywhere, anywhere,
            after(width), after(width), resident(g.shape), resident(w_o.shape), after(q_width),
            after(q_width), resident(ones.shape),
        ],
        out_specs=[
            rows, resident((share, units)), resident((share, units)), anywhere, anywhere,
            after(width), after(width), after(width), after(q_width), after(q_width),
            resident((1, width)),
        ],
        out_shape=[
            jax.ShapeDtypeStruct(w_down.shape, BF),
            jax.ShapeDtypeStruct((share, units), F32),
            jax.ShapeDtypeStruct((share, units), F32),
            whole, whole,
            jax.ShapeDtypeStruct((total, width), BF),
            jax.ShapeDtypeStruct((total, width), F32),
            jax.ShapeDtypeStruct((total, width), BF),
            jax.ShapeDtypeStruct((total, q_width), BF),
            jax.ShapeDtypeStruct((total, q_width), F32),
            jax.ShapeDtypeStruct((1, width), F32),
        ],
        scratch_shapes=[
            pltpu.VMEM((width, total), BF),
            pltpu.VMEM((total, chunk), BF),
            pltpu.VMEM((total, chunk), BF),
            pltpu.VMEM((total, chunk), BF),
            pltpu.VMEM((total, width), F32),
            pltpu.VMEM((total, width), F32),
            pltpu.VMEM((2, 2, 4, 2, 2, 2) + piece, BF),
            pltpu.VMEM((2, 2, 4, 2, 2, 2) + piece, BF),
            pltpu.VMEM((steps, 2, 4, 2, 2) + piece, BF),
            pltpu.VMEM((steps, 2, 4, 2) + piece, BF),
            pltpu.VMEM((steps, 2, 4) + piece, BF),
            pltpu.VMEM((steps, 2, 3) + piece, BF),
        ]
        + [pltpu.SemaphoreType.DMA((steps, 2, 6))] * 4
        + [pltpu.SemaphoreType.DMA((2,)), pltpu.SemaphoreType.DMA((2, 2))],
        compiler_params=pltpu.CompilerParams(
            vmem_limit_bytes=62 * 2**20, collective_id=collective, has_side_effects=True
        ),
        cost_estimate=pl.CostEstimate(
            flops=18 * total * width * units, bytes_accessed=12 * width * units, transcendentals=0
        ),
        name="feed",
    )(
        normed, grad_low, w_down, own_gate, own_up, hidden, cotangent, g, w_o, mixed, totals, ones
    )
    return outs[:3] + outs[5:]


def middle_block(
    head, ffn, incoming, h_ref, c_ref, g_ref, w_ref, o_ref, l_ref, ones_ref,
    out_ref, dh_ref, low_ref, do_ref, de_ref, gain_ref,
):
    hidden = h_ref[...]
    out_ref[...] = (hidden + ffn).astype(BF)
    inverse = lax.rsqrt(jnp.mean(hidden * hidden, axis=-1, keepdims=True) + epsilon)
    unit = hidden * inverse
    gain_ref[...] += jnp.sum(unit * incoming, axis=0, keepdims=True)
    scaled = incoming * g_ref[...]
    shared = jnp.mean(unit * scaled, axis=-1, keepdims=True)
    d_hidden = c_ref[...] + inverse * (scaled - unit * shared)
    dh_ref[...] = d_hidden
    low = d_hidden.astype(BF)
    low_ref[...] = low
    ones = ones_ref[...]
    wide = ones.shape[0]
    for c in range(0, o_ref.shape[1], wide):
        cols = slice(c, c + wide)
        d_att = mm(low, w_ref[cols, :], NT)
        ratio = 1.0 / l_ref[:, cols]
        do_ref[:, cols] = (d_att * ratio).astype(BF)
        de_ref[:, cols] = head_sum(d_att * o_ref[:, cols], ones) * ratio


def middle_kernel(head, f_ref, dn_ref, *refs):
    gain_ref = refs[-1]

    @pl.when(pl.program_id(0) == 0)
    def _():
        gain_ref[...] = jnp.zeros_like(gain_ref)

    middle_block(head, f_ref[...], dn_ref[...], *refs)


def middle_call(ffn, d_normed, hidden, cotangent, g, w_o, mixed, totals, ones, head):
    total, width = hidden.shape
    q_width = mixed.shape[1]
    block = largest_block(total, 256)

    def rows(n):
        return pl.BlockSpec((block, n), lambda i: (i, 0))

    return pl.pallas_call(
        functools.partial(middle_kernel, head),
        grid=(total // block,),
        in_specs=[
            rows(width), rows(width), rows(width), rows(width), resident(g.shape),
            resident(w_o.shape), rows(q_width), rows(q_width), resident(ones.shape),
        ],
        out_specs=[
            rows(width), rows(width), rows(width), rows(q_width), rows(q_width), resident((1, width)),
        ],
        out_shape=[
            jax.ShapeDtypeStruct((total, width), BF),
            jax.ShapeDtypeStruct((total, width), F32),
            jax.ShapeDtypeStruct((total, width), BF),
            jax.ShapeDtypeStruct((total, q_width), BF),
            jax.ShapeDtypeStruct((total, q_width), F32),
            jax.ShapeDtypeStruct((1, width), F32),
        ],
        compiler_params=params(),
        name="middle",
    )(ffn, d_normed, hidden, cotangent, g, w_o, mixed, totals, ones)


def last_kernel(
    q_width, kv_width, head, scale,
    dq_ref, dk_ref, dv_ref, rawq_ref, rawk_ref, gqk_ref, cos_ref, sin_ref, ones_ref, w_ref, x_ref, g_ref,
    dh_ref, *refs,
):
    got_ref = refs[0] if len(refs) == 6 else None
    d_ref, in_ref, gain_ref, gq_ref, gk_ref = refs[-5:]

    @pl.when(pl.program_id(0) == 0)
    def _():
        gain_ref[...] = jnp.zeros_like(gain_ref)
        gq_ref[...] = jnp.zeros_like(gq_ref)
        gk_ref[...] = jnp.zeros_like(gk_ref)

    ones = ones_ref[...]
    wide = ones.shape[0]
    cos = spread(cos_ref[...], wide)
    sin = spread(sin_ref[...], wide)
    qk = q_width + kv_width
    for c in range(0, qk, wide):
        cols = slice(c, c + wide)
        if c < q_width:
            grad, total, raw = dq_ref[:, cols] * scale, gq_ref, rawq_ref[:, cols]
        else:
            at = slice(c - q_width, c - q_width + wide)
            grad, total, raw = dk_ref[:, at].astype(F32), gk_ref, rawk_ref[:, at]
            if got_ref is not None:
                grad += got_ref[:, at].astype(F32)
        grad = grad * cos + swap_halves(grad * sin, head)
        inv = lax.rsqrt(head_sum(raw * raw, ones) * (1.0 / head) + epsilon)
        unit = raw * inv
        gained = jnp.sum(unit * grad, axis=0, keepdims=True)
        total[...] += sum(gained[:, i : i + LANES] for i in range(0, wide, LANES))
        scaled = grad * gqk_ref[:, cols]
        shared = head_sum(unit * scaled, ones) * (1.0 / head)
        d_ref[:, cols] = (inv * (scaled - unit * shared)).astype(BF)
    d_values = dv_ref[...].astype(F32)
    if got_ref is not None:
        d_values += got_ref[:, kv_width:].astype(F32)
    d_ref[:, qk:] = d_values.astype(BF)
    d_normed = mm(d_ref[...], w_ref[...], NT)
    x = x_ref[...].astype(F32)
    inverse = lax.rsqrt(jnp.mean(x * x, axis=-1, keepdims=True) + epsilon)
    unit = x * inverse
    gain_ref[...] += jnp.sum(unit * d_normed, axis=0, keepdims=True)
    scaled = d_normed * g_ref[...]
    shared = jnp.mean(unit * scaled, axis=-1, keepdims=True)
    in_ref[...] = dh_ref[...] + inverse * (scaled - unit * shared)


def last_call(dq, dk, dv, raw_q, raw_k, gqk, cos, sin, ones, w, x, g, d_hidden, head, got=()):
    total, width = x.shape
    q_width, kv_width = dq.shape[1], dk.shape[1]
    block = largest_block(total, 256)

    def rows(n):
        return pl.BlockSpec((block, n), lambda i: (i, 0))

    return pl.pallas_call(
        functools.partial(last_kernel, q_width, kv_width, head, head ** (-0.5)),
        grid=(total // block,),
        in_specs=[
            rows(q_width), rows(kv_width), rows(kv_width), rows(q_width), rows(kv_width),
            resident(gqk.shape), rows(LANES), rows(LANES), resident(ones.shape),
            resident(w.shape), rows(width), resident(g.shape), rows(width),
        ] + [rows(2 * kv_width)] * len(got),
        out_specs=[
            rows(w.shape[1]), rows(width),
            resident((1, width)), resident((1, LANES)), resident((1, LANES)),
        ],
        out_shape=[
            jax.ShapeDtypeStruct((total, w.shape[1]), BF),
            jax.ShapeDtypeStruct((total, width), F32),
            jax.ShapeDtypeStruct((1, width), F32),
            jax.ShapeDtypeStruct((1, LANES), F32),
            jax.ShapeDtypeStruct((1, LANES), F32),
        ],
        compiler_params=params(),
        name="last",
    )(dq, dk, dv, raw_q, raw_k, gqk, cos, sin, ones, w, x, g, d_hidden, *got)


class Place:
    def __init__(self):
        dp = lax.axis_index("dp")
        self.x = lax.axis_index("ctx")
        self.c = lax.rem(dp, 2)
        self.y = lax.rem(dp // 2, 2)
        self.z = dp // 4

    def peer(self, z=None, y=None, c=None, x=None):
        z = self.z if z is None else z
        y = self.y if y is None else y
        c = self.c if c is None else c
        x = self.x if x is None else x
        return {"dp": (z * 2 + y) * 2 + c, "ctx": x}

    def up(self, d):
        return lax.rem(self.z + d, 4)

    def peers(self):
        return [self.peer(z=self.up(d)) for d in (1, 2, 3)] + [
            self.peer(x=1 - self.x), self.peer(y=1 - self.y), self.peer(c=1 - self.c)
        ]


def greet(place):
    barrier = pltpu.get_barrier_semaphore()
    peers = place.peers()
    for peer in peers:
        pl.semaphore_signal(barrier, inc=1, device_id=peer, device_id_type=pl.DeviceIdType.MESH)
    pl.semaphore_wait(barrier, len(peers))


def remote(src, dst, sems, at, peer):
    send, recv = sems
    return pltpu.make_async_remote_copy(
        src_ref=src, dst_ref=dst, send_sem=send.at[at], recv_sem=recv.at[at],
        device_id=peer, device_id_type=pl.DeviceIdType.MESH,
    )


def gather_kernel(pieces, count, *refs):
    ins, outs = refs[:count], refs[count : 2 * count]
    sems, local = refs[2 * count : 2 * count + 2], refs[2 * count + 2]
    me = Place()
    greet(me)

    def block(p, z, y, c, x):
        array, rows, cols, _ = pieces[p]
        return outs[array].at[z, y, c, x, rows, cols]

    def own(p):
        array, rows, cols, _ = pieces[p]
        return ins[array].at[rows, cols]

    every = slice(None)

    def to_z(p):
        return [
            remote(own(p), block(p, me.z, me.y, me.c, me.x), sems, (p, d - 1), me.peer(z=me.up(d)))
            for d in (1, 2, 3)
        ]

    def keep(p):
        return pltpu.make_async_copy(own(p), block(p, me.z, me.y, me.c, me.x), local.at[p])

    def first(p):
        mine = block(p, every, me.y, me.c, me.x)
        peer = me.peer(x=1 - me.x) if pieces[p][3] else me.peer(y=1 - me.y)
        return [remote(mine, mine, sems, (p, 3), peer)]

    def second(p):
        if pieces[p][3]:
            mine, peer = block(p, every, me.y, me.c, every), me.peer(y=1 - me.y)
        else:
            mine, peer = block(p, every, every, me.c, me.x), me.peer(x=1 - me.x)
        return [remote(mine, mine, sems, (p, 4), peer)]

    def third(p):
        mine = block(p, every, every, me.c, every)
        return [remote(mine, mine, sems, (p, 5), me.peer(c=1 - me.c))]

    n = len(pieces)
    stages = [to_z, first, second, third]
    pair = 2

    def begin(p):
        keep(p).start()
        for copy in to_z(p):
            copy.start()

    for p in range(min(n, AHEAD)):
        begin(p)
    for t in range(0, n + 3 * pair, pair):
        for p in range(t + AHEAD, min(n, t + AHEAD + pair)):
            begin(p)
        for s in (1, 2, 3):
            for p in range(t - (s - 1) * pair, t - (s - 1) * pair + pair):
                if 0 <= p < n:
                    if s == 1:
                        keep(p).wait()
                    for copy in stages[s - 1](p):
                        copy.wait_recv()
                    for copy in stages[s](p):
                        copy.start()
    for p in range(n):
        third(p)[0].wait_recv()
    for p in range(n):
        for stage in stages:
            for copy in stage(p):
                copy.wait_send()


def gather_call(shards, pieces, collective):
    count = len(shards)
    outs = pl.pallas_call(
        functools.partial(gather_kernel, pieces, count),
        in_specs=[pl.BlockSpec(memory_space=pl.ANY)] * count,
        out_specs=[pl.BlockSpec(memory_space=pl.ANY)] * count,
        out_shape=[jax.ShapeDtypeStruct((4, 2, 2, 2) + s.shape, s.dtype) for s in shards],
        scratch_shapes=[
            pltpu.SemaphoreType.DMA((len(pieces), 6)),
            pltpu.SemaphoreType.DMA((len(pieces), 6)),
            pltpu.SemaphoreType.DMA((len(pieces),)),
        ],
        compiler_params=pltpu.CompilerParams(
            collective_id=collective, has_side_effects=True, vmem_limit_bytes=VMEM_LIMIT
        ),
        name="gather",
    )(*shards)
    return [o.reshape(32 * s.shape[0], s.shape[1]) for o, s in zip(outs, shards)]


def add_into(total, more):
    def step(i, carry):
        total[i] = (total[i].astype(F32) + more[i].astype(F32)).astype(total.dtype)
        return carry

    lax.fori_loop(0, total.shape[0], step, 0)


def scatter_kernel(pieces, count, gains, *refs):
    if gains:
        gain_ref, gain_out = refs[count], refs[2 * count + 1]
        sum_scr, got_scr, z_scr, gain_send, gain_recv = refs[-5:]
        refs = refs[:count] + refs[count + 1 : 2 * count + 1] + refs[2 * count + 2 : -5]
    ins, outs = refs[:count], refs[count : 2 * count]
    n = len(pieces)
    shapes, homes = piece_homes(pieces)
    scratch = refs[2 * count : 2 * count + 5 * len(shapes)]
    homes = [
        (scratch[5 * k : 5 * k + 4], i, scratch[5 * k + 4].at[i % OWN], (k, i % OWN)) for k, i in homes
    ]
    sems, local = refs[-3:-1], refs[-1]
    me = Place()
    greet(me)
    every = slice(None)

    def at(p, s):
        return homes[p][0][s].at[homes[p][1]]

    def part(p, c):
        array, rows, cols, _ = pieces[p]
        return ins[array].at[every, every, c, every, rows, cols]

    def load(p):
        return pltpu.make_async_copy(part(p, me.c), homes[p][2], local.at[homes[p][3]])

    def pairs(p):
        return [remote(part(p, 1 - me.c), at(p, 0), sems, (p, 0), me.peer(c=1 - me.c))]

    def first(p):
        if pieces[p][3]:
            give, peer = at(p, 0).at[every, every, 1 - me.x], me.peer(x=1 - me.x)
        else:
            give, peer = at(p, 0).at[every, 1 - me.y], me.peer(y=1 - me.y)
        return [remote(give, at(p, 1), sems, (p, 1), peer)]

    def second(p):
        if pieces[p][3]:
            peer, other = me.peer(y=1 - me.y), 1 - me.y
        else:
            peer, other = me.peer(x=1 - me.x), 1 - me.x
        return [remote(at(p, 1).at[every, other], at(p, 2), sems, (p, 2), peer)]

    def third(p):
        return [
            remote(at(p, 2).at[me.up(d)], at(p, 3).at[d - 1], sems, (p, 2 + d), me.peer(z=me.up(d)))
            for d in (1, 2, 3)
        ]

    stages = [pairs, first, second, third]

    def settle(p, s):
        if s == 0:
            load(p).wait()
            add_into(at(p, 0), homes[p][2])
        elif s == 1:
            kept = at(p, 0).at[every, every, me.x] if pieces[p][3] else at(p, 0).at[every, me.y]
            add_into(at(p, 1), kept)
        elif s == 2:
            add_into(at(p, 2), at(p, 1).at[every, me.y if pieces[p][3] else me.x])
        else:
            array, rows, cols, _ = pieces[p]
            more = at(p, 3)
            outs[array][rows, cols] = (
                at(p, 2)[me.z].astype(F32) + more[0].astype(F32) + more[1].astype(F32) + more[2].astype(F32)
            )

    pair = 2

    def begin(p):
        load(p).start()
        for copy in pairs(p):
            copy.start()

    hops = []
    if gains:
        near = [me.peer(c=1 - me.c), me.peer(x=1 - me.x), me.peer(y=1 - me.y)]
        hops = [
            [remote(sum_scr.at[i], got_scr.at[i], (gain_send, gain_recv), i, peer)]
            for i, peer in enumerate(near)
        ] + [[
            remote(sum_scr.at[3], z_scr.at[me.z], (gain_send, gain_recv), 2 + d, me.peer(z=me.up(d)))
            for d in (1, 2, 3)
        ]]

    def gain_step(i):
        if i == 0:
            sum_scr[0] = gain_ref[...]
        else:
            for copy in hops[i - 1]:
                copy.wait_recv()
            if i < 4:
                sum_scr[i] = sum_scr[i - 1] + got_scr[i - 1]
        if i == 3:
            z_scr[me.z] = sum_scr[3]
        if i < 4:
            for copy in hops[i]:
                copy.start()
        else:
            gain_out[...] = (z_scr[0] + z_scr[1]) + (z_scr[2] + z_scr[3])
            for hop in hops:
                for copy in hop:
                    copy.wait_send()

    for p in range(min(n, AHEAD)):
        begin(p)
    rounds = range(0, n + 3 * pair, pair)
    for t in rounds:
        if gains:
            for i in range(5):
                if i * (len(rounds) - 1) // 4 == t // pair:
                    gain_step(i)
        for s in range(4):
            for p in range(t - s * pair, t - s * pair + pair):
                if 0 <= p < n:
                    for copy in stages[s](p):
                        copy.wait_recv()
                    settle(p, s)
                    if s < 3:
                        for copy in stages[s + 1](p):
                            copy.start()
            if s == 0:
                for p in range(t + AHEAD, min(n, t + AHEAD + pair)):
                    begin(p)
    for p in range(n):
        for stage in stages:
            for copy in stage(p):
                copy.wait_send()


def piece_homes(pieces):
    shapes, homes = [], []
    for _, rows, cols, _ in pieces:
        shape = (rows.stop - rows.start, cols.stop - cols.start)
        if shape not in shapes:
            shapes.append(shape)
        kind = shapes.index(shape)
        homes.append((kind, sum(k == kind for k, _ in homes)))
    return shapes, homes


def scatter_call(grads, pieces, collective, gains=()):
    count = len(grads)
    shards = [(g.shape[0] // 32, g.shape[1]) for g in grads]
    grads = [g.reshape((4, 2, 2, 2) + s) for g, s in zip(grads, shards)]
    shapes, homes = piece_homes(pieces)
    scratch = []
    for kind, shape in enumerate(shapes):
        n = sum(k == kind for k, _ in homes)
        scratch += [
            pltpu.VMEM((n, 4, 2, 2) + shape, BF),
            pltpu.VMEM((n, 4, 2) + shape, BF),
            pltpu.VMEM((n, 4) + shape, BF),
            pltpu.VMEM((n, 3) + shape, BF),
            pltpu.VMEM((OWN, 4, 2, 2) + shape, BF),
        ]
    return pl.pallas_call(
        functools.partial(scatter_kernel, pieces, count, len(gains)),
        in_specs=[pl.BlockSpec(memory_space=pl.ANY)] * count
        + [pl.BlockSpec(memory_space=pltpu.VMEM)] * len(gains),
        out_specs=[pl.BlockSpec(memory_space=pltpu.VMEM)] * (count + len(gains)),
        out_shape=[jax.ShapeDtypeStruct(s, F32) for s in shards]
        + [jax.ShapeDtypeStruct(g.shape, F32) for g in gains],
        scratch_shapes=scratch + [
            pltpu.SemaphoreType.DMA((len(pieces), 6)),
            pltpu.SemaphoreType.DMA((len(pieces), 6)),
            pltpu.SemaphoreType.DMA((len(shapes), OWN)),
        ] + [
            scratch
            for g in gains
            for scratch in (
                pltpu.VMEM((4,) + g.shape, F32),
                pltpu.VMEM((3,) + g.shape, F32),
                pltpu.VMEM((4,) + g.shape, F32),
                pltpu.SemaphoreType.DMA((6,)),
                pltpu.SemaphoreType.DMA((6,)),
            )
        ],
        compiler_params=pltpu.CompilerParams(
            collective_id=collective, has_side_effects=True, vmem_limit_bytes=VMEM_LIMIT
        ),
        name="scatter",
    )(*grads, *gains)


def col_pieces(array, rows, cols, width=512, high=None):
    high = high or rows
    return [
        (array, slice(r, r + high), slice(c, c + width), (c // width) % 2 == 0)
        for r in range(0, rows, high)
        for c in range(0, cols, width)
    ]


def interleave(one, two):
    return [p for pair in zip(one, two) for p in pair]


def per_device(
    tokens, segments, cotangent, w_q, w_k, w_v, w_o, w_gate, w_up, w_down, g_attn, g_q, g_k, g_ffn
):
    seqs, rows, width = tokens.shape
    length = segments.shape[1]
    head = g_q.shape[0]
    q_width, kv_width = w_q.shape[1], w_k.shape[1]
    kv_heads = kv_width // head
    q_heads = q_width // head
    total = seqs * rows
    row_start = lax.axis_index("ctx") * rows
    own_kernels = (lax.axis_size("dp"), lax.axis_size("ctx")) == (16, 2)
    share = w_q.shape[0]

    def fetch(weight):
        return lax.all_gather(weight, AXES, axis=0, tiled=True)

    def send(grad):
        return lax.psum_scatter(grad, AXES, scatter_dimension=0, tiled=True).astype(F32)

    seg_rows = lax.dynamic_slice_in_dim(segments, row_start, rows, 1)
    first = jnp.sum((segments[:, None, :] < seg_rows[:, :, None]).astype(jnp.int32), axis=-1)
    query_pos = row_start + jnp.arange(rows, dtype=jnp.int32)
    positions = (query_pos[None, :] - first).reshape(total)
    frequency = rope_base ** (-jnp.arange(0, head, 2, dtype=F32) / head)
    angles = positions.astype(F32)[:, None] * frequency[None, :]
    cos, sin = jnp.cos(angles), jnp.sin(angles)
    cos = jnp.concatenate([cos] * (2 * LANES // head), axis=1)
    sin = jnp.concatenate([-sin, sin] * (LANES // head), axis=1)
    wide = 2 * LANES
    member = jnp.arange(wide) // head
    ones = (member[:, None] == member[None, :]).astype(BF)
    gains_q = jnp.concatenate([g_q] * q_heads)[None, :]
    gains_k = jnp.concatenate([g_k] * kv_heads)[None, :]
    x = tokens.reshape(total, width)
    cotangent = cotangent.reshape(total, width)

    w_qkv = jnp.concatenate([w_q, w_k, w_v], axis=1)
    w_down = fetch(w_down)
    grad_low = cotangent.astype(BF)
    if own_kernels:
        qkv_pieces = col_pieces(0, share, w_qkv.shape[1])
        o_pieces = col_pieces(0, share, w_o.shape[1])
        [w_qkv] = gather_call([w_qkv], qkv_pieces, 0)
    else:
        w_qkv, w_o = fetch(w_qkv), fetch(w_o)
        w_gate, w_up = fetch(w_gate), fetch(w_up)

    tables = (cos, sin, ones, head)
    normed, kv, raw_k = project_call(
        x, w_qkv, (q_width, 2 * kv_width), kv_width, g_attn[None, :], gains_k, *tables, None, "project_kv"
    )
    kv = kv.reshape(seqs, rows, 2 * kv_width)
    if own_kernels:
        before = lax.ppermute(kv, "ctx", [(0, 1)])
    _, q, raw_q = project_call(
        x, w_qkv, (0, q_width), q_width, g_attn[None, :], gains_q, *tables, head ** (-0.5), "project_q"
    )
    q = q.reshape(seqs, rows, q_width)
    block_q, block_k = min(256, rows), min(256, length)
    at = jnp.arange(0, rows, block_q, dtype=jnp.int32)[None, :]
    lowest = first[:, ::block_q]
    zero = jnp.zeros((1,), jnp.int32)
    if own_kernels:
        own_first = first - row_start
        own_keys = (
            jnp.maximum(lowest - row_start, 0) // block_k,
            jnp.broadcast_to((at + block_q - 1) // block_k + 1, lowest.shape),
            zero,
        )
        far_first = own_first + rows
        far_keys = (
            jnp.clip(lowest - row_start + rows, 0, rows) // block_k,
            jnp.full(lowest.shape, rows // block_k, jnp.int32),
            zero + rows,
        )
        near = attend_call(q, kv, own_first, own_keys, block_q, block_k, last_part=False)
        w_o, _ = lax.optimization_barrier((w_o, near))
        [w_o] = gather_call([w_o], [p[:3] + (True,) for p in o_pieces], 4)
        mixed, totals = attend_call(q, before, far_first, far_keys, block_q, block_k, near)
    else:
        kv = lax.all_gather(kv, "ctx", axis=1, tiled=True)
        all_keys = (
            lowest // block_k,
            jnp.broadcast_to((row_start + at + block_q - 1) // block_k + 1, lowest.shape),
            zero + row_start,
        )
        mixed, totals = attend_call(q, kv, first, all_keys, block_q, block_k)
    mixed, totals = mixed.reshape(total, q_width), totals.reshape(total, q_width)
    attended, hidden, normed_two = hidden_call(mixed, w_o, x, g_ffn[None, :])

    middle_args = (hidden, cotangent, g_ffn[None, :], w_o, mixed, totals, ones, head)
    if own_kernels:
        grad_down, out_gate, out_up, outputs, d_hidden, d_low, d_out, delta, grad_gffn = feed_call(
            normed_two, grad_low, w_down, w_gate, w_up, *middle_args, 2
        )
    else:
        ffn, d_normed_two, grad_down, out_gate, out_up = ffn_call(
            normed_two, grad_low, w_gate, w_up, w_down
        )
        out_gate, out_up = send(out_gate), send(out_up)
        outputs, d_hidden, d_low, d_out, delta, grad_gffn = middle_call(
            ffn, d_normed_two, *middle_args
        )
    out_down = send(grad_down)
    d_out, delta = d_out.reshape(q.shape), delta.reshape(q.shape)
    if own_kernels:
        far_dq, dk, dv = attend_back_call(
            q, d_out, delta, before, far_first, far_keys, block_q, block_k
        )
        got = lax.ppermute(jnp.concatenate([dk, dv], axis=2), "ctx", [(1, 0)])
        dq, dk, dv = attend_back_call(
            q, d_out, delta, kv, own_first, own_keys, block_q, block_k, (far_dq,)
        )
        dk, dv, got = dk.reshape(total, kv_width), dv.reshape(total, kv_width), (got.reshape(total, -1),)
    else:
        dq, dk, dv = attend_back_call(q, d_out, delta, kv, first, all_keys, block_q, block_k)
        dkv = lax.psum_scatter(
            jnp.concatenate([dk, dv], axis=2), "ctx", scatter_dimension=1, tiled=True
        ).reshape(total, 2 * kv_width)
        dk, dv, got = dkv[:, :kv_width], dkv[:, kv_width:], ()
    grad_o = mm(attended, d_low, TN).astype(BF)
    d_qkv, input_grad, grad_gattn, grad_gq, grad_gk = last_call(
        dq.reshape(total, q_width), dk, dv, raw_q, raw_k,
        jnp.concatenate([gains_q, gains_k], axis=1), cos, sin, ones,
        w_qkv, x, g_attn[None, :], d_hidden, head, got,
    )
    grad_qkv = mm(normed, d_qkv, TN).astype(BF)
    if own_kernels:
        flat = jnp.concatenate([grad_gattn, grad_gffn, grad_gq, grad_gk], axis=1).reshape(-1, LANES)
        flat = jnp.pad(flat, ((0, -flat.shape[0] % 8), (0, 0)))
        o_pieces = [(1,) + p[1:] for p in o_pieces]
        out_qkv, out_o, flat = scatter_call([grad_qkv, grad_o], o_pieces + qkv_pieces, 3, (flat,))
        flat = flat.reshape(1, -1)
        grad_gattn, grad_gffn = flat[:, :width], flat[:, width : 2 * width]
        grad_gq = flat[:, 2 * width : 2 * width + LANES]
        grad_gk = flat[:, 2 * width + LANES : 2 * width + 2 * LANES]
    else:
        out_qkv, out_o = send(grad_qkv), send(grad_o)
        grad_gattn, grad_gffn, grad_gq, grad_gk = lax.psum(
            (grad_gattn, grad_gffn, grad_gq, grad_gk), AXES
        )

    def fold(grad):
        return jnp.sum(grad.reshape(LANES // head, head), axis=0)

    return (
        outputs.reshape(tokens.shape),
        input_grad.reshape(tokens.shape),
        out_qkv[:, :q_width],
        out_qkv[:, q_width : q_width + kv_width],
        out_qkv[:, q_width + kv_width :],
        out_o,
        out_gate,
        out_up,
        out_down,
        grad_gattn[0],
        fold(grad_gq),
        fold(grad_gk),
        grad_gffn[0],
    )


def solution(mesh):
    split = P("dp", "ctx", None)
    shard = P(("dp", "ctx"), None)
    in_specs = (split, P("dp", None), split) + (shard,) * 7 + (P(),) * 4
    out_specs = (split, split) + (shard,) * 7 + (P(),) * 4
    return jax.shard_map(
        per_device, mesh=mesh, in_specs=in_specs, out_specs=out_specs, check_vma=False
    )
```

```python
import functools
import itertools

import jax
import jax.numpy as jnp
from jax import lax
from jax.experimental import pallas as pl
from jax.experimental.pallas import tpu as pltpu
from jax.sharding import PartitionSpec as P

epsilon = 1e-05
rope_base = 1000000.0
AXES = ("dp", "ctx")
BF = jnp.bfloat16
F32 = jnp.float32
LANES = 128
VMEM_LIMIT = 56 * 2**20
AHEAD = 4
OWN = 6
NN = (((1,), (0,)), ((), ()))
NT = (((1,), (1,)), ((), ()))
TN = (((0,), (0,)), ((), ()))


def mm(a, b, dims=NN):
    return lax.dot_general(a, b, dims, preferred_element_type=F32)


def params(semantics=None):
    return pltpu.CompilerParams(
        vmem_limit_bytes=VMEM_LIMIT,
        dimension_semantics=semantics,
    )


def resident(shape):
    zeros = (0,) * len(shape)
    return pl.BlockSpec(shape, lambda *_: zeros, pipeline_mode=pl.Buffered(1))


def largest_block(size, most):
    return max(b for b in range(1, min(size, most) + 1) if size % b == 0)


def head_sum(field, ones):
    wide = ones.shape[0]
    high = field.astype(BF)
    low = (field - high.astype(F32)).astype(BF)
    parts = [
        mm(high[:, c : c + wide], ones) + mm(low[:, c : c + wide], ones)
        for c in range(0, field.shape[1], wide)
    ]
    return jnp.concatenate(parts, axis=1)


def swap_halves(field, head):
    half = head // 2
    width = field.shape[1]
    lane = lax.broadcasted_iota(jnp.int32, field.shape, 1)
    return jnp.where(
        lane % head < half,
        pltpu.roll(field, width - half, 1),
        pltpu.roll(field, half, 1),
    )


def spread(table, width):
    return jnp.concatenate([table] * (width // table.shape[1]), axis=1)


def project_kernel(
    rope_width, head, scale,
    x_ref, w_ref, g_ref, gain_ref, cos_ref, sin_ref, ones_ref,
    normed_ref, out_ref, raw_ref,
):
    x = x_ref[...].astype(F32)
    inverse = lax.rsqrt(jnp.mean(x * x, axis=-1, keepdims=True) + epsilon)
    normed = (x * inverse * g_ref[...]).astype(BF)
    normed_ref[...] = normed
    ones = ones_ref[...]
    wide = ones.shape[0]
    cos = spread(cos_ref[...], wide)
    sin = spread(sin_ref[...], wide)
    for c in range(0, rope_width, wide):
        raw = mm(normed, w_ref[:, c : c + wide])
        raw_ref[:, c : c + wide] = raw
        inv = lax.rsqrt(head_sum(raw * raw, ones) * (1.0 / head) + epsilon)
        field = raw * inv * gain_ref[:, c : c + wide]
        turned = (field * cos + swap_halves(field, head) * sin).astype(BF)
        out_ref[:, c : c + wide] = turned if scale is None else turned * jnp.asarray(scale, BF)
    if rope_width < w_ref.shape[1]:
        out_ref[:, rope_width:] = mm(normed, w_ref[:, rope_width:]).astype(BF)


def project_call(x, w, cols, rope_width, g, gains, cos, sin, ones, head, scale, name):
    total, width = x.shape
    block = largest_block(total, 256)
    at, count = cols[0] // cols[1], cols[1]

    def rows(n):
        return pl.BlockSpec((block, n), lambda i: (i, 0))

    return pl.pallas_call(
        functools.partial(project_kernel, rope_width, head, scale),
        grid=(total // block,),
        in_specs=[
            rows(width),
            pl.BlockSpec((width, count), lambda i: (0, at), pipeline_mode=pl.Buffered(1)),
            resident(g.shape), resident(gains.shape),
            rows(LANES), rows(LANES), resident(ones.shape),
        ],
        out_specs=[rows(width), rows(count), rows(rope_width)],
        out_shape=[
            jax.ShapeDtypeStruct((total, width), BF),
            jax.ShapeDtypeStruct((total, count), BF),
            jax.ShapeDtypeStruct((total, rope_width), F32),
        ],
        compiler_params=params(),
        cost_estimate=pl.CostEstimate(
            flops=2 * total * width * count, bytes_accessed=2 * width * count + 10 * total * count,
            transcendentals=0,
        ),
        name=name,
    )(x, w, g, gains, cos, sin, ones)


def pad_head(pair, odd, fill):
    lane = lax.broadcasted_iota(jnp.int32, pair.shape, 1)
    if odd:
        pair = pltpu.roll(pair, LANES // 2, 1)
    return jnp.where(lane < LANES // 2, pair, jnp.asarray(fill, pair.dtype))


def attend_kernel(
    block_q, block_k, heads, more, last_part,
    low_ref, high_ref, start_ref, q_ref, k_ref, v_ref, first_ref, *refs,
):
    prior = refs[:2] if more else ()
    out_ref, total_ref, k_scr, v_scr = refs[len(prior) :]
    s = pl.program_id(0)
    rows = q_ref.shape[1]
    start = start_ref[0]
    half = LANES // 2
    for h in range(heads):
        c = h // 2 * LANES
        k_scr[h] = pad_head(k_ref[0, :, c : c + LANES].astype(F32), h % 2, 0).astype(BF)
        v_scr[h] = pad_head(v_ref[0, :, c : c + LANES].astype(F32), h % 2, 1).astype(BF)
    lane = lax.broadcasted_iota(jnp.int32, (block_q, LANES), 1)
    key_lane = lax.broadcasted_iota(jnp.int32, (2 * block_q, block_k), 1)
    row = lax.broadcasted_iota(jnp.int32, (2 * block_q, 1), 0) % block_q

    def q_step(i, carry):
        at = pl.multiple_of(i * block_q, block_q)
        first = first_ref[0, pl.ds(at, block_q), :]
        first = jnp.concatenate([first, first], axis=0)
        last = row + (start + at)
        queries = []
        for h in range(heads):
            pair = q_ref[0, pl.ds(at, block_q), h * LANES : (h + 1) * LANES].astype(F32)
            queries.append(
                jnp.concatenate([pad_head(pair, 0, 0), pad_head(pair, 1, 0)], axis=0).astype(BF)
            )

        def k_step(j, sums):
            key_at = pl.multiple_of(j * block_k, block_k)
            key = key_lane + key_at
            live = (key >= first) & (key <= last)
            new = []
            for h in range(heads):
                scores = mm(queries[h], k_scr[h, pl.ds(key_at, block_k), :], NT)
                expo = jnp.where(live, jnp.exp(scores), 0.0).astype(BF)
                new.append(sums[h] + mm(expo, v_scr[h, pl.ds(key_at, block_k), :]))
            return tuple(new)

        sums = lax.fori_loop(
            low_ref[s, i], high_ref[s, i], k_step,
            tuple(jnp.zeros((2 * block_q, LANES), F32) for _ in range(heads)),
        )
        for h in range(heads):
            even, odd = sums[h][:block_q], sums[h][block_q:]
            both = jnp.where(lane < half, even, pltpu.roll(odd, half, 1))
            tot = jnp.where(lane < half, pltpu.roll(even, half, 1), odd)
            cols = slice(h * LANES, (h + 1) * LANES)
            if more:
                both += prior[0][0, pl.ds(at, block_q), cols]
                tot += prior[1][0, pl.ds(at, block_q), cols]
            out_ref[0, pl.ds(at, block_q), cols] = both / tot if last_part else both
            total_ref[0, pl.ds(at, block_q), cols] = tot
        return carry

    lax.fori_loop(0, rows // block_q, q_step, 0)


def attend_call(q, kv, first, keys, block_q, block_k, prior=(), last_part=True):
    seqs, rows, q_width = q.shape
    length = kv.shape[1]
    kv_heads = q_width // LANES
    heads = largest_block(kv_heads, 8)
    steps = kv_heads // heads
    half = LANES // 2
    spec_q = pl.BlockSpec((1, rows, heads * LANES), lambda s, p, *_: (s, 0, p))
    return pl.pallas_call(
        functools.partial(attend_kernel, block_q, block_k, heads, bool(prior), last_part),
        grid_spec=pltpu.PrefetchScalarGridSpec(
            num_scalar_prefetch=3,
            grid=(seqs, steps),
            in_specs=[
                spec_q,
                pl.BlockSpec((1, length, heads * half), lambda s, p, *_: (s, 0, p)),
                pl.BlockSpec((1, length, heads * half), lambda s, p, *_: (s, 0, p + steps)),
                pl.BlockSpec((1, rows, 1), lambda s, p, *_: (s, 0, 0)),
            ] + [spec_q] * len(prior),
            out_specs=[spec_q, spec_q],
            scratch_shapes=[
                pltpu.VMEM((heads, length, LANES), BF),
                pltpu.VMEM((heads, length, LANES), BF),
            ],
        ),
        out_shape=[jax.ShapeDtypeStruct(q.shape, F32)] * 2,
        compiler_params=params(),
        cost_estimate=pl.CostEstimate(
            flops=4 * seqs * rows * length * q_width, bytes_accessed=16 * seqs * rows * q_width,
            transcendentals=0,
        ),
        name="attend",
    )(*keys, q, kv, kv, first[:, :, None], *prior)


def attend_back_kernel(
    block_q, block_k, heads, more,
    low_ref, high_ref, start_ref, q_ref, do_ref, de_ref, k_ref, v_ref, first_ref, *refs,
):
    prior_ref = refs[0] if more else None
    dq_ref, dk_ref, dv_ref, k_scr, v_scr, dk_scr, dv_scr = refs[int(more) :]
    s = pl.program_id(0)
    rows = q_ref.shape[1]
    length = k_ref.shape[1]
    start = start_ref[0]
    half = LANES // 2
    for h in range(heads):
        c = h // 2 * LANES
        k_scr[h] = pad_head(k_ref[0, :, c : c + LANES].astype(F32), h % 2, 0).astype(BF)
        v_scr[h] = pad_head(v_ref[0, :, c : c + LANES].astype(F32), h % 2, 1).astype(BF)
    dk_scr[...] = jnp.zeros_like(dk_scr)
    dv_scr[...] = jnp.zeros_like(dv_scr)
    lane = lax.broadcasted_iota(jnp.int32, (block_q, LANES), 1)
    key_row = lax.broadcasted_iota(jnp.int32, (block_k, 2 * block_q), 0)
    column = lax.broadcasted_iota(jnp.int32, (1, 2 * block_q), 1) % block_q

    def tail(pair, odd, delta):
        if odd:
            pair = pltpu.roll(pair, half, 1)
        else:
            delta = pltpu.roll(delta, half, 1)
        part0 = delta.astype(BF).astype(F32)
        part1 = (delta - part0).astype(BF).astype(F32)
        part2 = delta - part0 - part1
        rest = jnp.where(
            lane == half, part0, jnp.where(lane == half + 1, part1, jnp.where(lane == half + 2, part2, 0.0))
        )
        return jnp.where(lane < half, pair, -rest)

    def q_step(i, carry):
        at = pl.multiple_of(i * block_q, block_q)
        first = first_ref[0, :, pl.ds(at, block_q)]
        first = jnp.concatenate([first, first], axis=1)
        last = column + (start + at)
        queries, grads = [], []
        for h in range(heads):
            cols = slice(h * LANES, (h + 1) * LANES)
            pair = q_ref[0, pl.ds(at, block_q), cols].astype(F32)
            queries.append(
                jnp.concatenate([pad_head(pair, 0, 0), pad_head(pair, 1, 0)], axis=0).astype(BF)
            )
            pair = do_ref[0, pl.ds(at, block_q), cols].astype(F32)
            delta = de_ref[0, pl.ds(at, block_q), cols]
            grads.append(
                jnp.concatenate([tail(pair, 0, delta), tail(pair, 1, delta)], axis=0).astype(BF)
            )

        def k_step(j, sums):
            key_at = pl.multiple_of(j * block_k, block_k)
            key = key_row + key_at
            live = (key >= first) & (key <= last)
            new = []
            for h in range(heads):
                k = k_scr[h, pl.ds(key_at, block_k), :]
                v = v_scr[h, pl.ds(key_at, block_k), :]
                scores = mm(k, queries[h], NT)
                expo = jnp.where(live, jnp.exp(scores), 0.0)
                change = mm(v, grads[h], NT)
                d_scores = (expo * change).astype(BF)
                dv_scr[h, pl.ds(key_at, block_k), :] += mm(expo.astype(BF), grads[h])
                dk_scr[h, pl.ds(key_at, block_k), :] += mm(d_scores, queries[h])
                new.append(sums[h] + mm(d_scores, k, TN))
            return tuple(new)

        sums = lax.fori_loop(
            low_ref[s, i], high_ref[s, i], k_step,
            tuple(jnp.zeros((2 * block_q, LANES), F32) for _ in range(heads)),
        )
        for h in range(heads):
            even, odd = sums[h][:block_q], sums[h][block_q:]
            cols = slice(h * LANES, (h + 1) * LANES)
            grad = jnp.where(lane < half, even, pltpu.roll(odd, half, 1))
            if more:
                grad += prior_ref[0, pl.ds(at, block_q), cols]
            dq_ref[0, pl.ds(at, block_q), cols] = grad
        return carry

    lax.fori_loop(0, rows // block_q, q_step, 0)
    wide = lax.broadcasted_iota(jnp.int32, (length, LANES), 1)
    for h in range(0, heads, 2):
        cols = slice(h // 2 * LANES, (h // 2 + 1) * LANES)
        for grad, scr in ((dk_ref, dk_scr), (dv_ref, dv_scr)):
            grad[0, :, cols] = jnp.where(
                wide < half, scr[h], pltpu.roll(scr[h + 1], half, 1)
            ).astype(BF)


def attend_back_call(q, d_out, delta, kv, first, keys, block_q, block_k, prior=()):
    seqs, rows, q_width = q.shape
    length = kv.shape[1]
    kv_width = kv.shape[2] // 2
    kv_heads = q_width // LANES
    heads = largest_block(kv_heads, 8)
    steps = kv_heads // heads
    half = LANES // 2
    spec_q = pl.BlockSpec((1, rows, heads * LANES), lambda s, p, *_: (s, 0, p))
    spec_kv = pl.BlockSpec((1, length, heads * half), lambda s, p, *_: (s, 0, p))
    return pl.pallas_call(
        functools.partial(attend_back_kernel, block_q, block_k, heads, bool(prior)),
        grid_spec=pltpu.PrefetchScalarGridSpec(
            num_scalar_prefetch=3,
            grid=(seqs, steps),
            in_specs=[
                spec_q, spec_q, spec_q, spec_kv,
                pl.BlockSpec((1, length, heads * half), lambda s, p, *_: (s, 0, p + steps)),
                pl.BlockSpec((1, 1, rows), lambda s, p, *_: (s, 0, 0)),
            ] + [spec_q] * len(prior),
            out_specs=[spec_q, spec_kv, spec_kv],
            scratch_shapes=[
                pltpu.VMEM((heads, length, LANES), BF),
                pltpu.VMEM((heads, length, LANES), BF),
                pltpu.VMEM((heads, length, LANES), F32),
                pltpu.VMEM((heads, length, LANES), F32),
            ],
        ),
        out_shape=[
            jax.ShapeDtypeStruct(q.shape, F32),
            jax.ShapeDtypeStruct((seqs, length, kv_width), BF),
            jax.ShapeDtypeStruct((seqs, length, kv_width), BF),
        ],
        compiler_params=params(),
        cost_estimate=pl.CostEstimate(
            flops=10 * seqs * rows * length * q_width, bytes_accessed=16 * seqs * rows * q_width,
            transcendentals=0,
        ),
        name="attend_back",
    )(*keys, q, d_out, delta, kv, kv, first[:, None, :], *prior)


def hidden_kernel(a_ref, w_ref, x_ref, g_ref, att_ref, hidden_ref, normed_ref):
    attended = a_ref[...].astype(BF)
    att_ref[...] = attended
    hidden = x_ref[...].astype(F32) + mm(attended, w_ref[...])
    hidden_ref[...] = hidden
    inverse = lax.rsqrt(jnp.mean(hidden * hidden, axis=-1, keepdims=True) + epsilon)
    normed_ref[...] = (hidden * inverse * g_ref[...]).astype(BF)


def hidden_call(mixed, w_o, x, g):
    total, width = x.shape
    q_width = mixed.shape[1]
    block = largest_block(total, 256)

    def rows(n):
        return pl.BlockSpec((block, n), lambda i: (i, 0))

    return pl.pallas_call(
        hidden_kernel,
        grid=(total // block,),
        in_specs=[rows(q_width), resident(w_o.shape), rows(width), resident(g.shape)],
        out_specs=[rows(q_width), rows(width), rows(width)],
        out_shape=[
            jax.ShapeDtypeStruct((total, q_width), BF),
            jax.ShapeDtypeStruct((total, width), F32),
            jax.ShapeDtypeStruct((total, width), BF),
        ],
        compiler_params=params(),
        name="hidden",
    )(mixed, w_o, x, g)


def ffn_block(block_t, n_ref, c_ref, wg, wu, wd, out_ref, dn_ref, act_scr, dg_scr, du_scr):
    total = n_ref.shape[0]

    def t_step(i, carry):
        at = pl.ds(pl.multiple_of(i * block_t, block_t), block_t)
        normed = n_ref[at, :]
        gate = mm(normed, wg())
        up = mm(normed, wu())
        d_act = mm(c_ref[at, :], wd(), NT)
        sig = 1.0 / (1.0 + jnp.exp(-gate))
        silu = gate * sig
        act = (silu * up).astype(BF)
        d_gate = (d_act * up * (sig * (1.0 + gate - silu))).astype(BF)
        d_up = (d_act * silu).astype(BF)
        act_scr[at, :] = act
        dg_scr[at, :] = d_gate
        du_scr[at, :] = d_up
        out_ref[at, :] += mm(act, wd())
        dn_ref[at, :] += mm(d_gate, wg(), NT) + mm(d_up, wu(), NT)
        return carry

    lax.fori_loop(0, total // block_t, t_step, 0, unroll=total // block_t)


def down_grad(gd_ref, act_scr, c_ref):
    for c in range(0, act_scr.shape[1], 256):
        gd_ref[c : c + 256, :] = mm(act_scr[:, c : c + 256], c_ref[...], TN).astype(BF)


def ffn_kernel(
    block_t,
    n_ref, c_ref, wg_ref, wu_ref, wd_ref,
    out_ref, dn_ref, gd_ref, gg_ref, gu_ref,
    n_scr, act_scr, dg_scr, du_scr,
):
    @pl.when(pl.program_id(0) == 0)
    def _():
        n_scr[...] = n_ref[...].T
        out_ref[...] = jnp.zeros_like(out_ref)
        dn_ref[...] = jnp.zeros_like(dn_ref)

    ffn_block(
        block_t, n_ref, c_ref, lambda: wg_ref[...], lambda: wu_ref[...], lambda: wd_ref[...],
        out_ref, dn_ref, act_scr, dg_scr, du_scr,
    )

    def d_step(i, carry):
        at = pl.ds(pl.multiple_of(i * 256, 256), 256)
        normed = n_scr[at, :]
        gg_ref[at, :] = mm(normed, dg_scr[...]).astype(BF)
        gu_ref[at, :] = mm(normed, du_scr[...]).astype(BF)
        return carry

    width = n_ref.shape[1]
    lax.fori_loop(0, width // 256, d_step, 0, unroll=width // 256)
    down_grad(gd_ref, act_scr, c_ref)


def ffn_call(normed, grad_low, w_gate, w_up, w_down):
    total, width = normed.shape
    hidden = w_gate.shape[1]
    chunk = largest_block(hidden, 512)
    block_t = largest_block(total, 256)
    cols = pl.BlockSpec((width, chunk), lambda i: (0, i))
    rows = pl.BlockSpec((chunk, width), lambda i: (i, 0))
    return pl.pallas_call(
        functools.partial(ffn_kernel, block_t),
        grid=(hidden // chunk,),
        in_specs=[resident(normed.shape), resident(normed.shape), cols, cols, rows],
        out_specs=[resident(normed.shape), resident(normed.shape), rows, cols, cols],
        out_shape=[
            jax.ShapeDtypeStruct((total, width), F32),
            jax.ShapeDtypeStruct((total, width), F32),
            jax.ShapeDtypeStruct(w_down.shape, BF),
            jax.ShapeDtypeStruct(w_gate.shape, BF),
            jax.ShapeDtypeStruct(w_gate.shape, BF),
        ],
        scratch_shapes=[
            pltpu.VMEM((width, total), BF),
            pltpu.VMEM((total, chunk), BF),
            pltpu.VMEM((total, chunk), BF),
            pltpu.VMEM((total, chunk), BF),
        ],
        compiler_params=params(),
        name="ffn",
    )(normed, grad_low, w_gate, w_up, w_down)


class ColumnGather:
    def __init__(self, me, own, whole, slots, send, recv, keep_sem, load_sems):
        self.me, self.own, self.whole, self.slots = me, own, whole, slots
        self.sems, self.keep_sem, self.load_sems = (send, recv), keep_sem, load_sems

    def cols(self, k, j=None):
        width = self.slots.shape[-1]
        start = k * width if isinstance(k, int) else pl.multiple_of(k * width, width)
        if j is None:
            return pl.ds(start, width)
        half = width // 2
        start = start + j * half
        return pl.ds(start if isinstance(k, int) else pl.multiple_of(start, half), half)

    def keep(self):
        me = self.me
        return pltpu.make_async_copy(
            self.own, self.whole.at[me.z, me.y, me.c, me.x], self.keep_sem.at[0]
        )

    def hop(self, k, j, s):
        me, every = self.me, slice(None)
        whole = self.whole

        def mine(z, y, c, x):
            return whole.at[z, y, c, x, every, self.cols(k, j)]

        if s == 0:
            give = self.own.at[:, self.cols(k, j)]
            return [
                remote(give, mine(me.z, me.y, me.c, me.x), self.sems, (k, j, d - 1), me.peer(z=me.up(d)))
                for d in (1, 2, 3)
            ]
        to_x, to_y = me.peer(x=1 - me.x), me.peer(y=1 - me.y)
        if s == 1:
            give, peer = mine(every, me.y, me.c, me.x), (to_x if j == 0 else to_y)
        elif s == 2 and j == 0:
            give, peer = mine(every, me.y, me.c, every), to_y
        elif s == 2:
            give, peer = mine(every, every, me.c, me.x), to_x
        else:
            give, peer = mine(every, every, me.c, every), me.peer(c=1 - me.c)
        return [remote(give, give, self.sems, (k, j, 2 + s), peer)]

    def load(self, k):
        every = slice(None)
        slot = k % 2 if isinstance(k, int) else lax.rem(k, 2)
        return pltpu.make_async_copy(
            self.whole.at[every, every, every, every, every, self.cols(k)],
            self.slots.at[slot], self.load_sems.at[slot],
        )

    def start(self, k, s):
        for j in (0, 1):
            for copy in self.hop(k, j, s):
                copy.start()

    def wait(self, k, s):
        for j in (0, 1):
            for copy in self.hop(k, j, s):
                copy.wait()

    def open(self):
        self.keep().start()
        for k in range(3):
            self.start(k, 0)
        self.keep().wait()
        for k, s in ((0, 1), (1, 1), (0, 2), (2, 1), (1, 2), (0, 3), (3, 1), (2, 2), (1, 3), (4, 1), (3, 2), (5, 1)):
            self.wait(k, s - 1)
            self.start(k, s)
            if s == 1:
                self.start(k + 3, 0)
        self.fetch(0)

    def fetch(self, k):
        self.wait(k, 3)
        self.load(k).start()

    def ready(self, k):
        self.load(k).wait()

    def advance(self, step, steps):
        for s, early in ((1, 6), (2, 4), (3, 2)):
            k = step + early

            @pl.when(k < steps)
            def _(k=k, s=s):
                self.wait(k, s - 1)
                self.start(k, s)

        @pl.when(step + 9 < steps)
        def _():
            self.start(step + 9, 0)


class GradSums:
    def __init__(self, me, outs, made, r0, r1, r2, r3, send, recv):
        self.me, self.outs, self.made = me, outs, made
        self.r0, self.r1, self.r2, self.r3, self.send, self.recv = r0, r1, r2, r3, send, recv

    def keep(self, step, i, j, grad):
        slot = lax.rem(step, 2)
        grad = grad.astype(BF)
        share = self.made.shape[-2]
        for y, c, x in itertools.product((0, 1), (0, 1), (0, 1)):
            row = ((y * 2 + c) * 2 + x) * share
            one, two = (x, y) if j == 0 else (y, x)
            self.made[slot, j, c, one, two, i] = grad[row : row + share]

    def axes(self, j):
        me = self.me
        along_x = (me.x, me.peer(x=1 - me.x))
        along_y = (me.y, me.peer(y=1 - me.y))
        return (along_x, along_y) if j == 0 else (along_y, along_x)

    def hop(self, k, j, s):
        me = self.me
        sems = (self.send, self.recv)
        r0, r1, r2, r3 = (r.at[k, j] for r in (self.r0, self.r1, self.r2, self.r3))
        (one, to_one), (two, to_two) = self.axes(j)
        if s == 0:
            give = self.made.at[lax.rem(k, 2), j, 1 - me.c]
            return [remote(give, r0, sems, (k, j, 0), me.peer(c=1 - me.c))]
        if s == 1:
            return [remote(r0.at[1 - one], r1, sems, (k, j, 1), to_one)]
        if s == 2:
            return [remote(r1.at[1 - two], r2, sems, (k, j, 2), to_two)]
        return [
            remote(r2.at[me.up(d)], r3.at[d - 1], sems, (k, j, 2 + d), me.peer(z=me.up(d)))
            for d in (1, 2, 3)
        ]

    def settle(self, k, j, s):
        me = self.me
        r0, r1, r2, r3 = (r.at[k, j] for r in (self.r0, self.r1, self.r2, self.r3))
        (one, _), (two, _) = self.axes(j)
        for copy in self.hop(k, j, s):
            copy.wait()
        if s == 0:
            add_into(r0, self.made.at[lax.rem(k, 2), j, me.c])
        elif s == 1:
            add_into(r1, r0.at[one])
        elif s == 2:
            add_into(r2, r1.at[two])
        else:
            width = r2.shape[-1]
            cols = pl.ds(pl.multiple_of(k * width, width), width)
            self.outs[j][:, cols] = (
                r2[me.z].astype(F32) + r3[0].astype(F32) + r3[1].astype(F32) + r3[2].astype(F32)
            )

    def advance(self, step, steps):
        for s, late in ((3, 4), (2, 3), (1, 2), (0, 1)):
            k = step - late

            @pl.when((k >= 0) & (k < steps))
            def _(s=s, k=k):
                for j in (0, 1):
                    self.settle(k, j, s)
                    if s < 3:
                        for copy in self.hop(k, j, s + 1):
                            copy.start()


def feed_kernel(
    block_t, steps, block_m, head,
    n_ref, c_ref, wg_ref, wd_ref, own_up, h_ref, cot_ref, g_ref, w_ref, o_ref, l_ref, ones_ref,
    gd_ref, gg_ref, gu_ref, all_up, out_ref, dh_ref, low_ref, do_ref, de_ref, gain_ref,
    n_scr, act_scr, dg_scr, du_scr, f_scr, dn_scr, slots, made, r0, r1, r2, r3,
    g_send, g_recv, s_send, s_recv, keep_sems, load_sems,
):
    step = pl.program_id(0)
    me = Place()
    gather = ColumnGather(me, own_up, all_up, slots, g_send, g_recv, keep_sems, load_sems)
    sums = GradSums(me, (gg_ref, gu_ref), made, r0, r1, r2, r3, s_send, s_recv)

    @pl.when(step == 0)
    def _():
        greet(me)
        n_scr[...] = n_ref[...].T
        f_scr[...] = jnp.zeros_like(f_scr)
        dn_scr[...] = jnp.zeros_like(dn_scr)
        gather.open()

    @pl.when(step < steps)
    def _():
        gather.ready(step)
        slot = lax.rem(step, 2)
        width, chunk = n_ref.shape[1], wd_ref.shape[0]
        ffn_block(
            block_t, n_ref, c_ref,
            lambda: wg_ref[...],
            lambda: slots[slot].reshape(width, chunk),
            lambda: wd_ref[...],
            f_scr, dn_scr, act_scr, dg_scr, du_scr,
        )

        @pl.when(step + 1 < steps)
        def _():
            gather.fetch(step + 1)

        for i in range(width // 256):
            normed = n_scr[256 * i : 256 * i + 256, :]
            sums.keep(step, i, 0, mm(normed, dg_scr[...]))
            sums.keep(step, i, 1, mm(normed, du_scr[...]))
        down_grad(gd_ref, act_scr, c_ref)

    gather.advance(step, steps)
    sums.advance(step, steps)

    @pl.when(step < steps)
    def _():
        for j in (0, 1):
            for copy in sums.hop(step, j, 0):
                copy.start()

    @pl.when(step == steps)
    def _():
        gain_ref[...] = jnp.zeros_like(gain_ref)

    @pl.when(step >= steps)
    def _():
        at = pl.ds(pl.multiple_of((step - steps) * block_m, block_m), block_m)
        middle_block(
            head, f_scr[at, :], dn_scr[at, :], h_ref, cot_ref, g_ref, w_ref, o_ref, l_ref, ones_ref,
            out_ref, dh_ref, low_ref, do_ref, de_ref, gain_ref,
        )


def feed_call(
    normed, grad_low, w_gate, w_down, own_up, hidden, cotangent, g, w_o, mixed, totals, ones, head,
    collective,
):
    total, width = normed.shape
    share, units = own_up.shape
    q_width = mixed.shape[1]
    chunk = largest_block(units, 512)
    steps = units // chunk
    block_t, block_m = largest_block(total, 256), largest_block(total, 128)
    last = steps - 1
    piece = (share, chunk)

    def after(n):
        return pl.BlockSpec((block_m, n), lambda i: (jnp.maximum(i - steps, 0), 0))

    anywhere = pl.BlockSpec(memory_space=pl.ANY)
    rows = pl.BlockSpec((chunk, width), lambda i: (jnp.minimum(i, last), 0))
    cols = pl.BlockSpec((width, chunk), lambda i: (0, jnp.minimum(i, last)))
    whole = jax.ShapeDtypeStruct((4, 2, 2, 2, share, units), BF)
    outs = pl.pallas_call(
        functools.partial(feed_kernel, block_t, steps, block_m, head),
        grid=(steps + total // block_m,),
        in_specs=[
            resident(normed.shape), resident(normed.shape), cols, rows, anywhere,
            after(width), after(width), resident(g.shape), resident(w_o.shape), after(q_width),
            after(q_width), resident(ones.shape),
        ],
        out_specs=[
            rows, resident((share, units)), resident((share, units)), anywhere,
            after(width), after(width), after(width), after(q_width), after(q_width),
            resident((1, width)),
        ],
        out_shape=[
            jax.ShapeDtypeStruct(w_down.shape, BF),
            jax.ShapeDtypeStruct((share, units), F32),
            jax.ShapeDtypeStruct((share, units), F32),
            whole,
            jax.ShapeDtypeStruct((total, width), BF),
            jax.ShapeDtypeStruct((total, width), F32),
            jax.ShapeDtypeStruct((total, width), BF),
            jax.ShapeDtypeStruct((total, q_width), BF),
            jax.ShapeDtypeStruct((total, q_width), F32),
            jax.ShapeDtypeStruct((1, width), F32),
        ],
        scratch_shapes=[
            pltpu.VMEM((width, total), BF),
            pltpu.VMEM((total, chunk), BF),
            pltpu.VMEM((total, chunk), BF),
            pltpu.VMEM((total, chunk), BF),
            pltpu.VMEM((total, width), F32),
            pltpu.VMEM((total, width), F32),
            pltpu.VMEM((2, 4, 2, 2, 2) + piece, BF),
            pltpu.VMEM((2, 2, 2, 2, 2, 4) + piece, BF),
            pltpu.VMEM((steps, 2, 2, 2, 4) + piece, BF),
            pltpu.VMEM((steps, 2, 2, 4) + piece, BF),
            pltpu.VMEM((steps, 2, 4) + piece, BF),
            pltpu.VMEM((steps, 2, 3) + piece, BF),
        ]
        + [pltpu.SemaphoreType.DMA((steps, 2, 6))] * 4
        + [pltpu.SemaphoreType.DMA((1,)), pltpu.SemaphoreType.DMA((2,))],
        compiler_params=pltpu.CompilerParams(
            vmem_limit_bytes=62 * 2**20, collective_id=collective, has_side_effects=True
        ),
        cost_estimate=pl.CostEstimate(
            flops=18 * total * width * units, bytes_accessed=12 * width * units, transcendentals=0
        ),
        name="feed",
    )(
        normed, grad_low, w_gate, w_down, own_up, hidden, cotangent, g, w_o, mixed, totals, ones
    )
    return outs[:3] + outs[4:]


def middle_block(
    head, ffn, incoming, h_ref, c_ref, g_ref, w_ref, o_ref, l_ref, ones_ref,
    out_ref, dh_ref, low_ref, do_ref, de_ref, gain_ref,
):
    hidden = h_ref[...]
    out_ref[...] = (hidden + ffn).astype(BF)
    inverse = lax.rsqrt(jnp.mean(hidden * hidden, axis=-1, keepdims=True) + epsilon)
    unit = hidden * inverse
    gain_ref[...] += jnp.sum(unit * incoming, axis=0, keepdims=True)
    scaled = incoming * g_ref[...]
    shared = jnp.mean(unit * scaled, axis=-1, keepdims=True)
    d_hidden = c_ref[...] + inverse * (scaled - unit * shared)
    dh_ref[...] = d_hidden
    low = d_hidden.astype(BF)
    low_ref[...] = low
    ones = ones_ref[...]
    wide = ones.shape[0]
    for c in range(0, o_ref.shape[1], wide):
        cols = slice(c, c + wide)
        d_att = mm(low, w_ref[cols, :], NT)
        ratio = 1.0 / l_ref[:, cols]
        do_ref[:, cols] = (d_att * ratio).astype(BF)
        de_ref[:, cols] = head_sum(d_att * o_ref[:, cols], ones) * ratio


def middle_kernel(head, f_ref, dn_ref, *refs):
    gain_ref = refs[-1]

    @pl.when(pl.program_id(0) == 0)
    def _():
        gain_ref[...] = jnp.zeros_like(gain_ref)

    middle_block(head, f_ref[...], dn_ref[...], *refs)


def middle_call(ffn, d_normed, hidden, cotangent, g, w_o, mixed, totals, ones, head):
    total, width = hidden.shape
    q_width = mixed.shape[1]
    block = largest_block(total, 256)

    def rows(n):
        return pl.BlockSpec((block, n), lambda i: (i, 0))

    return pl.pallas_call(
        functools.partial(middle_kernel, head),
        grid=(total // block,),
        in_specs=[
            rows(width), rows(width), rows(width), rows(width), resident(g.shape),
            resident(w_o.shape), rows(q_width), rows(q_width), resident(ones.shape),
        ],
        out_specs=[
            rows(width), rows(width), rows(width), rows(q_width), rows(q_width), resident((1, width)),
        ],
        out_shape=[
            jax.ShapeDtypeStruct((total, width), BF),
            jax.ShapeDtypeStruct((total, width), F32),
            jax.ShapeDtypeStruct((total, width), BF),
            jax.ShapeDtypeStruct((total, q_width), BF),
            jax.ShapeDtypeStruct((total, q_width), F32),
            jax.ShapeDtypeStruct((1, width), F32),
        ],
        compiler_params=params(),
        name="middle",
    )(ffn, d_normed, hidden, cotangent, g, w_o, mixed, totals, ones)


def last_kernel(
    q_width, kv_width, head, scale,
    dq_ref, dk_ref, dv_ref, rawq_ref, rawk_ref, gqk_ref, cos_ref, sin_ref, ones_ref, w_ref, x_ref, g_ref,
    dh_ref, *refs,
):
    got_ref = refs[0] if len(refs) == 6 else None
    d_ref, in_ref, gain_ref, gq_ref, gk_ref = refs[-5:]

    @pl.when(pl.program_id(0) == 0)
    def _():
        gain_ref[...] = jnp.zeros_like(gain_ref)
        gq_ref[...] = jnp.zeros_like(gq_ref)
        gk_ref[...] = jnp.zeros_like(gk_ref)

    ones = ones_ref[...]
    wide = ones.shape[0]
    cos = spread(cos_ref[...], wide)
    sin = spread(sin_ref[...], wide)
    qk = q_width + kv_width
    for c in range(0, qk, wide):
        cols = slice(c, c + wide)
        if c < q_width:
            grad, total, raw = dq_ref[:, cols] * scale, gq_ref, rawq_ref[:, cols]
        else:
            at = slice(c - q_width, c - q_width + wide)
            grad, total, raw = dk_ref[:, at].astype(F32), gk_ref, rawk_ref[:, at]
            if got_ref is not None:
                grad += got_ref[:, at].astype(F32)
        grad = grad * cos + swap_halves(grad * sin, head)
        inv = lax.rsqrt(head_sum(raw * raw, ones) * (1.0 / head) + epsilon)
        unit = raw * inv
        gained = jnp.sum(unit * grad, axis=0, keepdims=True)
        total[...] += sum(gained[:, i : i + LANES] for i in range(0, wide, LANES))
        scaled = grad * gqk_ref[:, cols]
        shared = head_sum(unit * scaled, ones) * (1.0 / head)
        d_ref[:, cols] = (inv * (scaled - unit * shared)).astype(BF)
    d_values = dv_ref[...].astype(F32)
    if got_ref is not None:
        d_values += got_ref[:, kv_width:].astype(F32)
    d_ref[:, qk:] = d_values.astype(BF)
    d_normed = mm(d_ref[...], w_ref[...], NT)
    x = x_ref[...].astype(F32)
    inverse = lax.rsqrt(jnp.mean(x * x, axis=-1, keepdims=True) + epsilon)
    unit = x * inverse
    gain_ref[...] += jnp.sum(unit * d_normed, axis=0, keepdims=True)
    scaled = d_normed * g_ref[...]
    shared = jnp.mean(unit * scaled, axis=-1, keepdims=True)
    in_ref[...] = dh_ref[...] + inverse * (scaled - unit * shared)


def last_call(dq, dk, dv, raw_q, raw_k, gqk, cos, sin, ones, w, x, g, d_hidden, head, got=()):
    total, width = x.shape
    q_width, kv_width = dq.shape[1], dk.shape[1]
    block = largest_block(total, 256)

    def rows(n):
        return pl.BlockSpec((block, n), lambda i: (i, 0))

    return pl.pallas_call(
        functools.partial(last_kernel, q_width, kv_width, head, head ** (-0.5)),
        grid=(total // block,),
        in_specs=[
            rows(q_width), rows(kv_width), rows(kv_width), rows(q_width), rows(kv_width),
            resident(gqk.shape), rows(LANES), rows(LANES), resident(ones.shape),
            resident(w.shape), rows(width), resident(g.shape), rows(width),
        ] + [rows(2 * kv_width)] * len(got),
        out_specs=[
            rows(w.shape[1]), rows(width),
            resident((1, width)), resident((1, LANES)), resident((1, LANES)),
        ],
        out_shape=[
            jax.ShapeDtypeStruct((total, w.shape[1]), BF),
            jax.ShapeDtypeStruct((total, width), F32),
            jax.ShapeDtypeStruct((1, width), F32),
            jax.ShapeDtypeStruct((1, LANES), F32),
            jax.ShapeDtypeStruct((1, LANES), F32),
        ],
        compiler_params=params(),
        name="last",
    )(dq, dk, dv, raw_q, raw_k, gqk, cos, sin, ones, w, x, g, d_hidden, *got)


class Place:
    def __init__(self):
        dp = lax.axis_index("dp")
        self.x = lax.axis_index("ctx")
        self.c = lax.rem(dp, 2)
        self.y = lax.rem(dp // 2, 2)
        self.z = dp // 4

    def peer(self, z=None, y=None, c=None, x=None):
        z = self.z if z is None else z
        y = self.y if y is None else y
        c = self.c if c is None else c
        x = self.x if x is None else x
        return {"dp": (z * 2 + y) * 2 + c, "ctx": x}

    def up(self, d):
        return lax.rem(self.z + d, 4)

    def peers(self):
        return [self.peer(z=self.up(d)) for d in (1, 2, 3)] + [
            self.peer(x=1 - self.x), self.peer(y=1 - self.y), self.peer(c=1 - self.c)
        ]


def greet(place):
    barrier = pltpu.get_barrier_semaphore()
    peers = place.peers()
    for peer in peers:
        pl.semaphore_signal(barrier, inc=1, device_id=peer, device_id_type=pl.DeviceIdType.MESH)
    pl.semaphore_wait(barrier, len(peers))


def remote(src, dst, sems, at, peer):
    send, recv = sems
    return pltpu.make_async_remote_copy(
        src_ref=src, dst_ref=dst, send_sem=send.at[at], recv_sem=recv.at[at],
        device_id=peer, device_id_type=pl.DeviceIdType.MESH,
    )


def gather_kernel(pieces, count, *refs):
    ins, outs = refs[:count], refs[count : 2 * count]
    sems, local = refs[2 * count : 2 * count + 2], refs[2 * count + 2]
    me = Place()
    greet(me)

    def block(p, z, y, c, x):
        array, rows, cols, _ = pieces[p]
        return outs[array].at[z, y, c, x, rows, cols]

    def own(p):
        array, rows, cols, _ = pieces[p]
        return ins[array].at[rows, cols]

    every = slice(None)

    def to_z(p):
        return [
            remote(own(p), block(p, me.z, me.y, me.c, me.x), sems, (p, d - 1), me.peer(z=me.up(d)))
            for d in (1, 2, 3)
        ]

    def keep(p):
        return pltpu.make_async_copy(own(p), block(p, me.z, me.y, me.c, me.x), local.at[p])

    def first(p):
        mine = block(p, every, me.y, me.c, me.x)
        peer = me.peer(x=1 - me.x) if pieces[p][3] else me.peer(y=1 - me.y)
        return [remote(mine, mine, sems, (p, 3), peer)]

    def second(p):
        if pieces[p][3]:
            mine, peer = block(p, every, me.y, me.c, every), me.peer(y=1 - me.y)
        else:
            mine, peer = block(p, every, every, me.c, me.x), me.peer(x=1 - me.x)
        return [remote(mine, mine, sems, (p, 4), peer)]

    def third(p):
        mine = block(p, every, every, me.c, every)
        return [remote(mine, mine, sems, (p, 5), me.peer(c=1 - me.c))]

    n = len(pieces)
    stages = [to_z, first, second, third]
    pair = 2

    def begin(p):
        keep(p).start()
        for copy in to_z(p):
            copy.start()

    for p in range(min(n, AHEAD)):
        begin(p)
    for t in range(0, n + 3 * pair, pair):
        for p in range(t + AHEAD, min(n, t + AHEAD + pair)):
            begin(p)
        for s in (1, 2, 3):
            for p in range(t - (s - 1) * pair, t - (s - 1) * pair + pair):
                if 0 <= p < n:
                    if s == 1:
                        keep(p).wait()
                    for copy in stages[s - 1](p):
                        copy.wait_recv()
                    for copy in stages[s](p):
                        copy.start()
    for p in range(n):
        third(p)[0].wait_recv()
    for p in range(n):
        for stage in stages:
            for copy in stage(p):
                copy.wait_send()


def gather_call(shards, pieces, collective):
    count = len(shards)
    outs = pl.pallas_call(
        functools.partial(gather_kernel, pieces, count),
        in_specs=[pl.BlockSpec(memory_space=pl.ANY)] * count,
        out_specs=[pl.BlockSpec(memory_space=pl.ANY)] * count,
        out_shape=[jax.ShapeDtypeStruct((4, 2, 2, 2) + s.shape, s.dtype) for s in shards],
        scratch_shapes=[
            pltpu.SemaphoreType.DMA((len(pieces), 6)),
            pltpu.SemaphoreType.DMA((len(pieces), 6)),
            pltpu.SemaphoreType.DMA((len(pieces),)),
        ],
        compiler_params=pltpu.CompilerParams(
            collective_id=collective, has_side_effects=True, vmem_limit_bytes=VMEM_LIMIT
        ),
        name="gather",
    )(*shards)
    return [o.reshape(32 * s.shape[0], s.shape[1]) for o, s in zip(outs, shards)]


def add_into(total, more):
    def step(i, carry):
        total[i] = (total[i].astype(F32) + more[i].astype(F32)).astype(total.dtype)
        return carry

    lax.fori_loop(0, total.shape[0], step, 0)


def scatter_kernel(pieces, count, gains, *refs):
    if gains:
        gain_ref, gain_out = refs[count], refs[2 * count + 1]
        sum_scr, got_scr, z_scr, gain_send, gain_recv = refs[-5:]
        refs = refs[:count] + refs[count + 1 : 2 * count + 1] + refs[2 * count + 2 : -5]
    ins, outs = refs[:count], refs[count : 2 * count]
    n = len(pieces)
    shapes, homes = piece_homes(pieces)
    scratch = refs[2 * count : 2 * count + 5 * len(shapes)]
    homes = [
        (scratch[5 * k : 5 * k + 4], i, scratch[5 * k + 4].at[i % OWN], (k, i % OWN)) for k, i in homes
    ]
    sems, local = refs[-3:-1], refs[-1]
    me = Place()
    greet(me)
    every = slice(None)

    def at(p, s):
        return homes[p][0][s].at[homes[p][1]]

    def part(p, c):
        array, rows, cols, _ = pieces[p]
        return ins[array].at[every, every, c, every, rows, cols]

    def load(p):
        return pltpu.make_async_copy(part(p, me.c), homes[p][2], local.at[homes[p][3]])

    def pairs(p):
        return [remote(part(p, 1 - me.c), at(p, 0), sems, (p, 0), me.peer(c=1 - me.c))]

    def first(p):
        if pieces[p][3]:
            give, peer = at(p, 0).at[every, every, 1 - me.x], me.peer(x=1 - me.x)
        else:
            give, peer = at(p, 0).at[every, 1 - me.y], me.peer(y=1 - me.y)
        return [remote(give, at(p, 1), sems, (p, 1), peer)]

    def second(p):
        if pieces[p][3]:
            peer, other = me.peer(y=1 - me.y), 1 - me.y
        else:
            peer, other = me.peer(x=1 - me.x), 1 - me.x
        return [remote(at(p, 1).at[every, other], at(p, 2), sems, (p, 2), peer)]

    def third(p):
        return [
            remote(at(p, 2).at[me.up(d)], at(p, 3).at[d - 1], sems, (p, 2 + d), me.peer(z=me.up(d)))
            for d in (1, 2, 3)
        ]

    stages = [pairs, first, second, third]

    def settle(p, s):
        if s == 0:
            load(p).wait()
            add_into(at(p, 0), homes[p][2])
        elif s == 1:
            kept = at(p, 0).at[every, every, me.x] if pieces[p][3] else at(p, 0).at[every, me.y]
            add_into(at(p, 1), kept)
        elif s == 2:
            add_into(at(p, 2), at(p, 1).at[every, me.y if pieces[p][3] else me.x])
        else:
            array, rows, cols, _ = pieces[p]
            more = at(p, 3)
            outs[array][rows, cols] = (
                at(p, 2)[me.z].astype(F32) + more[0].astype(F32) + more[1].astype(F32) + more[2].astype(F32)
            )

    pair = 2

    def begin(p):
        load(p).start()
        for copy in pairs(p):
            copy.start()

    hops = []
    if gains:
        near = [me.peer(c=1 - me.c), me.peer(x=1 - me.x), me.peer(y=1 - me.y)]
        hops = [
            [remote(sum_scr.at[i], got_scr.at[i], (gain_send, gain_recv), i, peer)]
            for i, peer in enumerate(near)
        ] + [[
            remote(sum_scr.at[3], z_scr.at[me.z], (gain_send, gain_recv), 2 + d, me.peer(z=me.up(d)))
            for d in (1, 2, 3)
        ]]

    def gain_step(i):
        if i == 0:
            sum_scr[0] = gain_ref[...]
        else:
            for copy in hops[i - 1]:
                copy.wait_recv()
            if i < 4:
                sum_scr[i] = sum_scr[i - 1] + got_scr[i - 1]
        if i == 3:
            z_scr[me.z] = sum_scr[3]
        if i < 4:
            for copy in hops[i]:
                copy.start()
        else:
            gain_out[...] = (z_scr[0] + z_scr[1]) + (z_scr[2] + z_scr[3])
            for hop in hops:
                for copy in hop:
                    copy.wait_send()

    for p in range(min(n, AHEAD)):
        begin(p)
    rounds = range(0, n + 3 * pair, pair)
    for t in rounds:
        if gains:
            for i in range(5):
                if i * (len(rounds) - 1) // 4 == t // pair:
                    gain_step(i)
        for s in range(4):
            for p in range(t - s * pair, t - s * pair + pair):
                if 0 <= p < n:
                    for copy in stages[s](p):
                        copy.wait_recv()
                    settle(p, s)
                    if s < 3:
                        for copy in stages[s + 1](p):
                            copy.start()
            if s == 0:
                for p in range(t + AHEAD, min(n, t + AHEAD + pair)):
                    begin(p)
    for p in range(n):
        for stage in stages:
            for copy in stage(p):
                copy.wait_send()


def piece_homes(pieces):
    shapes, homes = [], []
    for _, rows, cols, _ in pieces:
        shape = (rows.stop - rows.start, cols.stop - cols.start)
        if shape not in shapes:
            shapes.append(shape)
        kind = shapes.index(shape)
        homes.append((kind, sum(k == kind for k, _ in homes)))
    return shapes, homes


def scatter_call(grads, pieces, collective, gains=()):
    count = len(grads)
    shards = [(g.shape[0] // 32, g.shape[1]) for g in grads]
    grads = [g.reshape((4, 2, 2, 2) + s) for g, s in zip(grads, shards)]
    shapes, homes = piece_homes(pieces)
    scratch = []
    for kind, shape in enumerate(shapes):
        n = sum(k == kind for k, _ in homes)
        scratch += [
            pltpu.VMEM((n, 4, 2, 2) + shape, BF),
            pltpu.VMEM((n, 4, 2) + shape, BF),
            pltpu.VMEM((n, 4) + shape, BF),
            pltpu.VMEM((n, 3) + shape, BF),
            pltpu.VMEM((OWN, 4, 2, 2) + shape, BF),
        ]
    return pl.pallas_call(
        functools.partial(scatter_kernel, pieces, count, len(gains)),
        in_specs=[pl.BlockSpec(memory_space=pl.ANY)] * count
        + [pl.BlockSpec(memory_space=pltpu.VMEM)] * len(gains),
        out_specs=[pl.BlockSpec(memory_space=pltpu.VMEM)] * (count + len(gains)),
        out_shape=[jax.ShapeDtypeStruct(s, F32) for s in shards]
        + [jax.ShapeDtypeStruct(g.shape, F32) for g in gains],
        scratch_shapes=scratch + [
            pltpu.SemaphoreType.DMA((len(pieces), 6)),
            pltpu.SemaphoreType.DMA((len(pieces), 6)),
            pltpu.SemaphoreType.DMA((len(shapes), OWN)),
        ] + [
            scratch
            for g in gains
            for scratch in (
                pltpu.VMEM((4,) + g.shape, F32),
                pltpu.VMEM((3,) + g.shape, F32),
                pltpu.VMEM((4,) + g.shape, F32),
                pltpu.SemaphoreType.DMA((6,)),
                pltpu.SemaphoreType.DMA((6,)),
            )
        ],
        compiler_params=pltpu.CompilerParams(
            collective_id=collective, has_side_effects=True, vmem_limit_bytes=VMEM_LIMIT
        ),
        name="scatter",
    )(*grads, *gains)


def col_pieces(array, rows, cols, width=512, high=None):
    high = high or rows
    return [
        (array, slice(r, r + high), slice(c, c + width), (c // width) % 2 == 0)
        for r in range(0, rows, high)
        for c in range(0, cols, width)
    ]


def interleave(one, two):
    return [p for pair in zip(one, two) for p in pair]


def per_device(
    tokens, segments, cotangent, w_q, w_k, w_v, w_o, w_gate, w_up, w_down, g_attn, g_q, g_k, g_ffn
):
    seqs, rows, width = tokens.shape
    length = segments.shape[1]
    head = g_q.shape[0]
    q_width, kv_width = w_q.shape[1], w_k.shape[1]
    kv_heads = kv_width // head
    q_heads = q_width // head
    total = seqs * rows
    row_start = lax.axis_index("ctx") * rows
    own_kernels = (lax.axis_size("dp"), lax.axis_size("ctx")) == (16, 2)
    share = w_q.shape[0]

    def fetch(weight):
        return lax.all_gather(weight, AXES, axis=0, tiled=True)

    def send(grad):
        return lax.psum_scatter(grad, AXES, scatter_dimension=0, tiled=True).astype(F32)

    seg_rows = lax.dynamic_slice_in_dim(segments, row_start, rows, 1)
    first = jnp.sum((segments[:, None, :] < seg_rows[:, :, None]).astype(jnp.int32), axis=-1)
    query_pos = row_start + jnp.arange(rows, dtype=jnp.int32)
    positions = (query_pos[None, :] - first).reshape(total)
    frequency = rope_base ** (-jnp.arange(0, head, 2, dtype=F32) / head)
    angles = positions.astype(F32)[:, None] * frequency[None, :]
    cos, sin = jnp.cos(angles), jnp.sin(angles)
    cos = jnp.concatenate([cos] * (2 * LANES // head), axis=1)
    sin = jnp.concatenate([-sin, sin] * (LANES // head), axis=1)
    wide = 2 * LANES
    member = jnp.arange(wide) // head
    ones = (member[:, None] == member[None, :]).astype(BF)
    gains_q = jnp.concatenate([g_q] * q_heads)[None, :]
    gains_k = jnp.concatenate([g_k] * kv_heads)[None, :]
    x = tokens.reshape(total, width)
    cotangent = cotangent.reshape(total, width)

    w_qkv = jnp.concatenate([w_q, w_k, w_v], axis=1)
    w_down, w_gate = fetch(w_down), fetch(w_gate)
    grad_low = cotangent.astype(BF)
    if own_kernels:
        qkv_pieces = col_pieces(0, share, w_qkv.shape[1])
        o_pieces = col_pieces(0, share, w_o.shape[1])
        [w_qkv] = gather_call([w_qkv], qkv_pieces, 0)
    else:
        w_qkv, w_o = fetch(w_qkv), fetch(w_o)
        w_up = fetch(w_up)

    tables = (cos, sin, ones, head)
    normed, kv, raw_k = project_call(
        x, w_qkv, (q_width, 2 * kv_width), kv_width, g_attn[None, :], gains_k, *tables, None, "project_kv"
    )
    kv = kv.reshape(seqs, rows, 2 * kv_width)
    if own_kernels:
        before = lax.ppermute(kv, "ctx", [(0, 1)])
    _, q, raw_q = project_call(
        x, w_qkv, (0, q_width), q_width, g_attn[None, :], gains_q, *tables, head ** (-0.5), "project_q"
    )
    q = q.reshape(seqs, rows, q_width)
    block_q, block_k = min(256, rows), min(256, length)
    at = jnp.arange(0, rows, block_q, dtype=jnp.int32)[None, :]
    lowest = first[:, ::block_q]
    zero = jnp.zeros((1,), jnp.int32)
    if own_kernels:
        own_first = first - row_start
        own_keys = (
            jnp.maximum(lowest - row_start, 0) // block_k,
            jnp.broadcast_to((at + block_q - 1) // block_k + 1, lowest.shape),
            zero,
        )
        far_first = own_first + rows
        far_keys = (
            jnp.clip(lowest - row_start + rows, 0, rows) // block_k,
            jnp.full(lowest.shape, rows // block_k, jnp.int32),
            zero + rows,
        )
        near = attend_call(q, kv, own_first, own_keys, block_q, block_k, last_part=False)
        w_o, _ = lax.optimization_barrier((w_o, near))
        [w_o] = gather_call([w_o], [p[:3] + (True,) for p in o_pieces], 4)
        mixed, totals = attend_call(q, before, far_first, far_keys, block_q, block_k, near)
    else:
        kv = lax.all_gather(kv, "ctx", axis=1, tiled=True)
        all_keys = (
            lowest // block_k,
            jnp.broadcast_to((row_start + at + block_q - 1) // block_k + 1, lowest.shape),
            zero + row_start,
        )
        mixed, totals = attend_call(q, kv, first, all_keys, block_q, block_k)
    mixed, totals = mixed.reshape(total, q_width), totals.reshape(total, q_width)
    attended, hidden, normed_two = hidden_call(mixed, w_o, x, g_ffn[None, :])

    middle_args = (hidden, cotangent, g_ffn[None, :], w_o, mixed, totals, ones, head)
    if own_kernels:
        grad_down, out_gate, out_up, outputs, d_hidden, d_low, d_out, delta, grad_gffn = feed_call(
            normed_two, grad_low, w_gate, w_down, w_up, *middle_args, 2
        )
    else:
        ffn, d_normed_two, grad_down, out_gate, out_up = ffn_call(
            normed_two, grad_low, w_gate, w_up, w_down
        )
        out_gate, out_up = send(out_gate), send(out_up)
        outputs, d_hidden, d_low, d_out, delta, grad_gffn = middle_call(
            ffn, d_normed_two, *middle_args
        )
    out_down = send(grad_down)
    d_out, delta = d_out.reshape(q.shape), delta.reshape(q.shape)
    if own_kernels:
        far_dq, dk, dv = attend_back_call(
            q, d_out, delta, before, far_first, far_keys, block_q, block_k
        )
        got = lax.ppermute(jnp.concatenate([dk, dv], axis=2), "ctx", [(1, 0)])
        dq, dk, dv = attend_back_call(
            q, d_out, delta, kv, own_first, own_keys, block_q, block_k, (far_dq,)
        )
        dk, dv, got = dk.reshape(total, kv_width), dv.reshape(total, kv_width), (got.reshape(total, -1),)
    else:
        dq, dk, dv = attend_back_call(q, d_out, delta, kv, first, all_keys, block_q, block_k)
        dkv = lax.psum_scatter(
            jnp.concatenate([dk, dv], axis=2), "ctx", scatter_dimension=1, tiled=True
        ).reshape(total, 2 * kv_width)
        dk, dv, got = dkv[:, :kv_width], dkv[:, kv_width:], ()
    grad_o = mm(attended, d_low, TN).astype(BF)
    d_qkv, input_grad, grad_gattn, grad_gq, grad_gk = last_call(
        dq.reshape(total, q_width), dk, dv, raw_q, raw_k,
        jnp.concatenate([gains_q, gains_k], axis=1), cos, sin, ones,
        w_qkv, x, g_attn[None, :], d_hidden, head, got,
    )
    grad_qkv = mm(normed, d_qkv, TN).astype(BF)
    if own_kernels:
        flat = jnp.concatenate([grad_gattn, grad_gffn, grad_gq, grad_gk], axis=1).reshape(-1, LANES)
        flat = jnp.pad(flat, ((0, -flat.shape[0] % 8), (0, 0)))
        o_pieces = [(1,) + p[1:] for p in o_pieces]
        out_qkv, out_o, flat = scatter_call([grad_qkv, grad_o], o_pieces + qkv_pieces, 3, (flat,))
        flat = flat.reshape(1, -1)
        grad_gattn, grad_gffn = flat[:, :width], flat[:, width : 2 * width]
        grad_gq = flat[:, 2 * width : 2 * width + LANES]
        grad_gk = flat[:, 2 * width + LANES : 2 * width + 2 * LANES]
    else:
        out_qkv, out_o = send(grad_qkv), send(grad_o)
        grad_gattn, grad_gffn, grad_gq, grad_gk = lax.psum(
            (grad_gattn, grad_gffn, grad_gq, grad_gk), AXES
        )

    def fold(grad):
        return jnp.sum(grad.reshape(LANES // head, head), axis=0)

    return (
        outputs.reshape(tokens.shape),
        input_grad.reshape(tokens.shape),
        out_qkv[:, :q_width],
        out_qkv[:, q_width : q_width + kv_width],
        out_qkv[:, q_width + kv_width :],
        out_o,
        out_gate,
        out_up,
        out_down,
        grad_gattn[0],
        fold(grad_gq),
        fold(grad_gk),
        grad_gffn[0],
    )


def solution(mesh):
    split = P("dp", "ctx", None)
    shard = P(("dp", "ctx"), None)
    in_specs = (split, P("dp", None), split) + (shard,) * 7 + (P(),) * 4
    out_specs = (split, split) + (shard,) * 7 + (P(),) * 4
    return jax.shard_map(
        per_device, mesh=mesh, in_specs=in_specs, out_specs=out_specs, check_vma=False
    )
```

```python
import functools
import itertools

import jax
import jax.numpy as jnp
from jax import lax
from jax.experimental import pallas as pl
from jax.experimental.pallas import tpu as pltpu
from jax.sharding import PartitionSpec as P

epsilon = 1e-05
rope_base = 1000000.0
AXES = ("dp", "ctx")
BF = jnp.bfloat16
F32 = jnp.float32
LANES = 128
VMEM_LIMIT = 56 * 2**20
AHEAD = 4
OWN = 6
NN = (((1,), (0,)), ((), ()))
NT = (((1,), (1,)), ((), ()))
TN = (((0,), (0,)), ((), ()))


def mm(a, b, dims=NN):
    return lax.dot_general(a, b, dims, preferred_element_type=F32)


def params(semantics=None):
    return pltpu.CompilerParams(
        vmem_limit_bytes=VMEM_LIMIT,
        dimension_semantics=semantics,
    )


def resident(shape):
    zeros = (0,) * len(shape)
    return pl.BlockSpec(shape, lambda *_: zeros, pipeline_mode=pl.Buffered(1))


def largest_block(size, most):
    return max(b for b in range(1, min(size, most) + 1) if size % b == 0)


def head_sum(field, ones):
    wide = ones.shape[0]
    high = field.astype(BF)
    low = (field - high.astype(F32)).astype(BF)
    parts = [
        mm(high[:, c : c + wide], ones) + mm(low[:, c : c + wide], ones)
        for c in range(0, field.shape[1], wide)
    ]
    return jnp.concatenate(parts, axis=1)


def swap_halves(field, head):
    half = head // 2
    width = field.shape[1]
    lane = lax.broadcasted_iota(jnp.int32, field.shape, 1)
    return jnp.where(
        lane % head < half,
        pltpu.roll(field, width - half, 1),
        pltpu.roll(field, half, 1),
    )


def spread(table, width):
    return jnp.concatenate([table] * (width // table.shape[1]), axis=1)


def project_kernel(
    rope_width, head, scale,
    x_ref, w_ref, g_ref, gain_ref, cos_ref, sin_ref, ones_ref,
    normed_ref, out_ref, raw_ref,
):
    x = x_ref[...].astype(F32)
    inverse = lax.rsqrt(jnp.mean(x * x, axis=-1, keepdims=True) + epsilon)
    normed = (x * inverse * g_ref[...]).astype(BF)
    normed_ref[...] = normed
    ones = ones_ref[...]
    wide = ones.shape[0]
    cos = spread(cos_ref[...], wide)
    sin = spread(sin_ref[...], wide)
    for c in range(0, rope_width, wide):
        raw = mm(normed, w_ref[:, c : c + wide])
        raw_ref[:, c : c + wide] = raw
        inv = lax.rsqrt(head_sum(raw * raw, ones) * (1.0 / head) + epsilon)
        field = raw * inv * gain_ref[:, c : c + wide]
        turned = (field * cos + swap_halves(field, head) * sin).astype(BF)
        out_ref[:, c : c + wide] = turned if scale is None else turned * jnp.asarray(scale, BF)
    if rope_width < w_ref.shape[1]:
        out_ref[:, rope_width:] = mm(normed, w_ref[:, rope_width:]).astype(BF)


def project_call(x, w, cols, rope_width, g, gains, cos, sin, ones, head, scale, name):
    total, width = x.shape
    block = largest_block(total, 256)
    at, count = cols[0] // cols[1], cols[1]

    def rows(n):
        return pl.BlockSpec((block, n), lambda i: (i, 0))

    return pl.pallas_call(
        functools.partial(project_kernel, rope_width, head, scale),
        grid=(total // block,),
        in_specs=[
            rows(width),
            pl.BlockSpec((width, count), lambda i: (0, at), pipeline_mode=pl.Buffered(1)),
            resident(g.shape), resident(gains.shape),
            rows(LANES), rows(LANES), resident(ones.shape),
        ],
        out_specs=[rows(width), rows(count), rows(rope_width)],
        out_shape=[
            jax.ShapeDtypeStruct((total, width), BF),
            jax.ShapeDtypeStruct((total, count), BF),
            jax.ShapeDtypeStruct((total, rope_width), F32),
        ],
        compiler_params=params(),
        cost_estimate=pl.CostEstimate(
            flops=2 * total * width * count, bytes_accessed=2 * width * count + 10 * total * count,
            transcendentals=0,
        ),
        name=name,
    )(x, w, g, gains, cos, sin, ones)


def pad_head(pair, odd, fill):
    lane = lax.broadcasted_iota(jnp.int32, pair.shape, 1)
    if odd:
        pair = pltpu.roll(pair, LANES // 2, 1)
    return jnp.where(lane < LANES // 2, pair, jnp.asarray(fill, pair.dtype))


def attend_kernel(
    block_q, block_k, heads, more, last_part,
    low_ref, high_ref, start_ref, q_ref, k_ref, v_ref, first_ref, *refs,
):
    prior = refs[:2] if more else ()
    out_ref, total_ref, k_scr, v_scr = refs[len(prior) :]
    s = pl.program_id(0)
    rows = q_ref.shape[1]
    start = start_ref[0]
    half = LANES // 2
    for h in range(heads):
        c = h // 2 * LANES
        k_scr[h] = pad_head(k_ref[0, :, c : c + LANES].astype(F32), h % 2, 0).astype(BF)
        v_scr[h] = pad_head(v_ref[0, :, c : c + LANES].astype(F32), h % 2, 1).astype(BF)
    lane = lax.broadcasted_iota(jnp.int32, (block_q, LANES), 1)
    key_lane = lax.broadcasted_iota(jnp.int32, (2 * block_q, block_k), 1)
    row = lax.broadcasted_iota(jnp.int32, (2 * block_q, 1), 0) % block_q

    def q_step(i, carry):
        at = pl.multiple_of(i * block_q, block_q)
        first = first_ref[0, pl.ds(at, block_q), :]
        first = jnp.concatenate([first, first], axis=0)
        last = row + (start + at)
        queries = []
        for h in range(heads):
            pair = q_ref[0, pl.ds(at, block_q), h * LANES : (h + 1) * LANES].astype(F32)
            queries.append(
                jnp.concatenate([pad_head(pair, 0, 0), pad_head(pair, 1, 0)], axis=0).astype(BF)
            )

        def k_step(j, sums):
            key_at = pl.multiple_of(j * block_k, block_k)
            key = key_lane + key_at
            live = (key >= first) & (key <= last)
            new = []
            for h in range(heads):
                scores = mm(queries[h], k_scr[h, pl.ds(key_at, block_k), :], NT)
                expo = jnp.where(live, jnp.exp(scores), 0.0).astype(BF)
                new.append(sums[h] + mm(expo, v_scr[h, pl.ds(key_at, block_k), :]))
            return tuple(new)

        sums = lax.fori_loop(
            low_ref[s, i], high_ref[s, i], k_step,
            tuple(jnp.zeros((2 * block_q, LANES), F32) for _ in range(heads)),
        )
        for h in range(heads):
            even, odd = sums[h][:block_q], sums[h][block_q:]
            both = jnp.where(lane < half, even, pltpu.roll(odd, half, 1))
            tot = jnp.where(lane < half, pltpu.roll(even, half, 1), odd)
            cols = slice(h * LANES, (h + 1) * LANES)
            if more:
                both += prior[0][0, pl.ds(at, block_q), cols]
                tot += prior[1][0, pl.ds(at, block_q), cols]
            out_ref[0, pl.ds(at, block_q), cols] = both / tot if last_part else both
            total_ref[0, pl.ds(at, block_q), cols] = tot
        return carry

    lax.fori_loop(0, rows // block_q, q_step, 0)


def attend_call(q, kv, first, keys, block_q, block_k, prior=(), last_part=True):
    seqs, rows, q_width = q.shape
    length = kv.shape[1]
    kv_heads = q_width // LANES
    heads = largest_block(kv_heads, 8)
    steps = kv_heads // heads
    half = LANES // 2
    spec_q = pl.BlockSpec((1, rows, heads * LANES), lambda s, p, *_: (s, 0, p))
    return pl.pallas_call(
        functools.partial(attend_kernel, block_q, block_k, heads, bool(prior), last_part),
        grid_spec=pltpu.PrefetchScalarGridSpec(
            num_scalar_prefetch=3,
            grid=(seqs, steps),
            in_specs=[
                spec_q,
                pl.BlockSpec((1, length, heads * half), lambda s, p, *_: (s, 0, p)),
                pl.BlockSpec((1, length, heads * half), lambda s, p, *_: (s, 0, p + steps)),
                pl.BlockSpec((1, rows, 1), lambda s, p, *_: (s, 0, 0)),
            ] + [spec_q] * len(prior),
            out_specs=[spec_q, spec_q],
            scratch_shapes=[
                pltpu.VMEM((heads, length, LANES), BF),
                pltpu.VMEM((heads, length, LANES), BF),
            ],
        ),
        out_shape=[jax.ShapeDtypeStruct(q.shape, F32)] * 2,
        compiler_params=params(),
        cost_estimate=pl.CostEstimate(
            flops=4 * seqs * rows * length * q_width, bytes_accessed=16 * seqs * rows * q_width,
            transcendentals=0,
        ),
        name="attend",
    )(*keys, q, kv, kv, first[:, :, None], *prior)


def attend_back_kernel(
    block_q, block_k, heads, more,
    low_ref, high_ref, start_ref, q_ref, do_ref, de_ref, k_ref, v_ref, first_ref, *refs,
):
    prior_ref = refs[0] if more else None
    dq_ref, dk_ref, dv_ref, k_scr, v_scr, dk_scr, dv_scr = refs[int(more) :]
    s = pl.program_id(0)
    rows = q_ref.shape[1]
    length = k_ref.shape[1]
    start = start_ref[0]
    half = LANES // 2
    for h in range(heads):
        c = h // 2 * LANES
        k_scr[h] = pad_head(k_ref[0, :, c : c + LANES].astype(F32), h % 2, 0).astype(BF)
        v_scr[h] = pad_head(v_ref[0, :, c : c + LANES].astype(F32), h % 2, 1).astype(BF)
    dk_scr[...] = jnp.zeros_like(dk_scr)
    dv_scr[...] = jnp.zeros_like(dv_scr)
    lane = lax.broadcasted_iota(jnp.int32, (block_q, LANES), 1)
    key_row = lax.broadcasted_iota(jnp.int32, (block_k, 2 * block_q), 0)
    column = lax.broadcasted_iota(jnp.int32, (1, 2 * block_q), 1) % block_q

    def tail(pair, odd, delta):
        if odd:
            pair = pltpu.roll(pair, half, 1)
        else:
            delta = pltpu.roll(delta, half, 1)
        part0 = delta.astype(BF).astype(F32)
        part1 = (delta - part0).astype(BF).astype(F32)
        part2 = delta - part0 - part1
        rest = jnp.where(
            lane == half, part0, jnp.where(lane == half + 1, part1, jnp.where(lane == half + 2, part2, 0.0))
        )
        return jnp.where(lane < half, pair, -rest)

    def q_step(i, carry):
        at = pl.multiple_of(i * block_q, block_q)
        first = first_ref[0, :, pl.ds(at, block_q)]
        first = jnp.concatenate([first, first], axis=1)
        last = column + (start + at)
        queries, grads = [], []
        for h in range(heads):
            cols = slice(h * LANES, (h + 1) * LANES)
            pair = q_ref[0, pl.ds(at, block_q), cols].astype(F32)
            queries.append(
                jnp.concatenate([pad_head(pair, 0, 0), pad_head(pair, 1, 0)], axis=0).astype(BF)
            )
            pair = do_ref[0, pl.ds(at, block_q), cols].astype(F32)
            delta = de_ref[0, pl.ds(at, block_q), cols]
            grads.append(
                jnp.concatenate([tail(pair, 0, delta), tail(pair, 1, delta)], axis=0).astype(BF)
            )

        def k_step(j, sums):
            key_at = pl.multiple_of(j * block_k, block_k)
            key = key_row + key_at
            live = (key >= first) & (key <= last)
            new = []
            for h in range(heads):
                k = k_scr[h, pl.ds(key_at, block_k), :]
                v = v_scr[h, pl.ds(key_at, block_k), :]
                scores = mm(k, queries[h], NT)
                expo = jnp.where(live, jnp.exp(scores), 0.0)
                change = mm(v, grads[h], NT)
                d_scores = (expo * change).astype(BF)
                dv_scr[h, pl.ds(key_at, block_k), :] += mm(expo.astype(BF), grads[h])
                dk_scr[h, pl.ds(key_at, block_k), :] += mm(d_scores, queries[h])
                new.append(sums[h] + mm(d_scores, k, TN))
            return tuple(new)

        sums = lax.fori_loop(
            low_ref[s, i], high_ref[s, i], k_step,
            tuple(jnp.zeros((2 * block_q, LANES), F32) for _ in range(heads)),
        )
        for h in range(heads):
            even, odd = sums[h][:block_q], sums[h][block_q:]
            cols = slice(h * LANES, (h + 1) * LANES)
            grad = jnp.where(lane < half, even, pltpu.roll(odd, half, 1))
            if more:
                grad += prior_ref[0, pl.ds(at, block_q), cols]
            dq_ref[0, pl.ds(at, block_q), cols] = grad
        return carry

    lax.fori_loop(0, rows // block_q, q_step, 0)
    wide = lax.broadcasted_iota(jnp.int32, (length, LANES), 1)
    for h in range(0, heads, 2):
        cols = slice(h // 2 * LANES, (h // 2 + 1) * LANES)
        for grad, scr in ((dk_ref, dk_scr), (dv_ref, dv_scr)):
            grad[0, :, cols] = jnp.where(
                wide < half, scr[h], pltpu.roll(scr[h + 1], half, 1)
            ).astype(BF)


def attend_back_call(q, d_out, delta, kv, first, keys, block_q, block_k, prior=()):
    seqs, rows, q_width = q.shape
    length = kv.shape[1]
    kv_width = kv.shape[2] // 2
    kv_heads = q_width // LANES
    heads = largest_block(kv_heads, 8)
    steps = kv_heads // heads
    half = LANES // 2
    spec_q = pl.BlockSpec((1, rows, heads * LANES), lambda s, p, *_: (s, 0, p))
    spec_kv = pl.BlockSpec((1, length, heads * half), lambda s, p, *_: (s, 0, p))
    return pl.pallas_call(
        functools.partial(attend_back_kernel, block_q, block_k, heads, bool(prior)),
        grid_spec=pltpu.PrefetchScalarGridSpec(
            num_scalar_prefetch=3,
            grid=(seqs, steps),
            in_specs=[
                spec_q, spec_q, spec_q, spec_kv,
                pl.BlockSpec((1, length, heads * half), lambda s, p, *_: (s, 0, p + steps)),
                pl.BlockSpec((1, 1, rows), lambda s, p, *_: (s, 0, 0)),
            ] + [spec_q] * len(prior),
            out_specs=[spec_q, spec_kv, spec_kv],
            scratch_shapes=[
                pltpu.VMEM((heads, length, LANES), BF),
                pltpu.VMEM((heads, length, LANES), BF),
                pltpu.VMEM((heads, length, LANES), F32),
                pltpu.VMEM((heads, length, LANES), F32),
            ],
        ),
        out_shape=[
            jax.ShapeDtypeStruct(q.shape, F32),
            jax.ShapeDtypeStruct((seqs, length, kv_width), BF),
            jax.ShapeDtypeStruct((seqs, length, kv_width), BF),
        ],
        compiler_params=params(),
        cost_estimate=pl.CostEstimate(
            flops=10 * seqs * rows * length * q_width, bytes_accessed=16 * seqs * rows * q_width,
            transcendentals=0,
        ),
        name="attend_back",
    )(*keys, q, d_out, delta, kv, kv, first[:, None, :], *prior)


def hidden_kernel(a_ref, w_ref, x_ref, g_ref, att_ref, hidden_ref, normed_ref):
    attended = a_ref[...].astype(BF)
    att_ref[...] = attended
    hidden = x_ref[...].astype(F32) + mm(attended, w_ref[...])
    hidden_ref[...] = hidden
    inverse = lax.rsqrt(jnp.mean(hidden * hidden, axis=-1, keepdims=True) + epsilon)
    normed_ref[...] = (hidden * inverse * g_ref[...]).astype(BF)


def hidden_call(mixed, w_o, x, g):
    total, width = x.shape
    q_width = mixed.shape[1]
    block = largest_block(total, 256)

    def rows(n):
        return pl.BlockSpec((block, n), lambda i: (i, 0))

    return pl.pallas_call(
        hidden_kernel,
        grid=(total // block,),
        in_specs=[rows(q_width), resident(w_o.shape), rows(width), resident(g.shape)],
        out_specs=[rows(q_width), rows(width), rows(width)],
        out_shape=[
            jax.ShapeDtypeStruct((total, q_width), BF),
            jax.ShapeDtypeStruct((total, width), F32),
            jax.ShapeDtypeStruct((total, width), BF),
        ],
        compiler_params=params(),
        name="hidden",
    )(mixed, w_o, x, g)


def ffn_block(block_t, n_ref, c_ref, wg, wu, wd, out_ref, dn_ref, act_scr, dg_scr, du_scr):
    total = n_ref.shape[0]

    def t_step(i, carry):
        at = pl.ds(pl.multiple_of(i * block_t, block_t), block_t)
        normed = n_ref[at, :]
        gate = mm(normed, wg())
        up = mm(normed, wu())
        d_act = mm(c_ref[at, :], wd(), NT)
        sig = 1.0 / (1.0 + jnp.exp(-gate))
        silu = gate * sig
        act = (silu * up).astype(BF)
        d_gate = (d_act * up * (sig * (1.0 + gate - silu))).astype(BF)
        d_up = (d_act * silu).astype(BF)
        act_scr[at, :] = act
        dg_scr[at, :] = d_gate
        du_scr[at, :] = d_up
        out_ref[at, :] += mm(act, wd())
        dn_ref[at, :] += mm(d_gate, wg(), NT) + mm(d_up, wu(), NT)
        return carry

    lax.fori_loop(0, total // block_t, t_step, 0, unroll=total // block_t)


def down_grad(gd_ref, act_scr, c_ref):
    for c in range(0, act_scr.shape[1], 256):
        gd_ref[c : c + 256, :] = mm(act_scr[:, c : c + 256], c_ref[...], TN).astype(BF)


def ffn_kernel(
    block_t,
    n_ref, c_ref, wg_ref, wu_ref, wd_ref,
    out_ref, dn_ref, gd_ref, gg_ref, gu_ref,
    n_scr, act_scr, dg_scr, du_scr,
):
    @pl.when(pl.program_id(0) == 0)
    def _():
        n_scr[...] = n_ref[...].T
        out_ref[...] = jnp.zeros_like(out_ref)
        dn_ref[...] = jnp.zeros_like(dn_ref)

    ffn_block(
        block_t, n_ref, c_ref, lambda: wg_ref[...], lambda: wu_ref[...], lambda: wd_ref[...],
        out_ref, dn_ref, act_scr, dg_scr, du_scr,
    )

    def d_step(i, carry):
        at = pl.ds(pl.multiple_of(i * 256, 256), 256)
        normed = n_scr[at, :]
        gg_ref[at, :] = mm(normed, dg_scr[...]).astype(BF)
        gu_ref[at, :] = mm(normed, du_scr[...]).astype(BF)
        return carry

    width = n_ref.shape[1]
    lax.fori_loop(0, width // 256, d_step, 0, unroll=width // 256)
    down_grad(gd_ref, act_scr, c_ref)


def ffn_call(normed, grad_low, w_gate, w_up, w_down):
    total, width = normed.shape
    hidden = w_gate.shape[1]
    chunk = largest_block(hidden, 512)
    block_t = largest_block(total, 256)
    cols = pl.BlockSpec((width, chunk), lambda i: (0, i))
    rows = pl.BlockSpec((chunk, width), lambda i: (i, 0))
    return pl.pallas_call(
        functools.partial(ffn_kernel, block_t),
        grid=(hidden // chunk,),
        in_specs=[resident(normed.shape), resident(normed.shape), cols, cols, rows],
        out_specs=[resident(normed.shape), resident(normed.shape), rows, cols, cols],
        out_shape=[
            jax.ShapeDtypeStruct((total, width), F32),
            jax.ShapeDtypeStruct((total, width), F32),
            jax.ShapeDtypeStruct(w_down.shape, BF),
            jax.ShapeDtypeStruct(w_gate.shape, BF),
            jax.ShapeDtypeStruct(w_gate.shape, BF),
        ],
        scratch_shapes=[
            pltpu.VMEM((width, total), BF),
            pltpu.VMEM((total, chunk), BF),
            pltpu.VMEM((total, chunk), BF),
            pltpu.VMEM((total, chunk), BF),
        ],
        compiler_params=params(),
        name="ffn",
    )(normed, grad_low, w_gate, w_up, w_down)


class ColumnGather:
    def __init__(self, me, own, whole, slots, send, recv, keep_sem, load_sems):
        self.me, self.own, self.whole, self.slots = me, own, whole, slots
        self.sems, self.keep_sem, self.load_sems = (send, recv), keep_sem, load_sems

    def cols(self, k, j=None):
        width = self.slots.shape[-1]
        start = k * width if isinstance(k, int) else pl.multiple_of(k * width, width)
        if j is None:
            return pl.ds(start, width)
        half = width // 2
        start = start + j * half
        return pl.ds(start if isinstance(k, int) else pl.multiple_of(start, half), half)

    def keep(self):
        me = self.me
        return pltpu.make_async_copy(
            self.own, self.whole.at[me.z, me.y, me.c, me.x], self.keep_sem.at[0]
        )

    def hop(self, k, j, s):
        me, every = self.me, slice(None)
        whole = self.whole

        def mine(z, y, c, x):
            return whole.at[z, y, c, x, every, self.cols(k, j)]

        if s == 0:
            give = self.own.at[:, self.cols(k, j)]
            return [
                remote(give, mine(me.z, me.y, me.c, me.x), self.sems, (k, j, d - 1), me.peer(z=me.up(d)))
                for d in (1, 2, 3)
            ]
        to_x, to_y = me.peer(x=1 - me.x), me.peer(y=1 - me.y)
        if s == 1:
            give, peer = mine(every, me.y, me.c, me.x), (to_x if j == 0 else to_y)
        elif s == 2 and j == 0:
            give, peer = mine(every, me.y, me.c, every), to_y
        elif s == 2:
            give, peer = mine(every, every, me.c, me.x), to_x
        else:
            give, peer = mine(every, every, me.c, every), me.peer(c=1 - me.c)
        return [remote(give, give, self.sems, (k, j, 2 + s), peer)]

    def load(self, k):
        every = slice(None)
        slot = k % 2 if isinstance(k, int) else lax.rem(k, 2)
        return pltpu.make_async_copy(
            self.whole.at[every, every, every, every, every, self.cols(k)],
            self.slots.at[slot], self.load_sems.at[slot],
        )

    def start(self, k, s):
        for j in (0, 1):
            for copy in self.hop(k, j, s):
                copy.start()

    def wait(self, k, s):
        for j in (0, 1):
            for copy in self.hop(k, j, s):
                copy.wait()

    def open(self):
        self.keep().start()
        for k in range(3):
            self.start(k, 0)
        self.keep().wait()
        for k, s in ((0, 1), (1, 1), (0, 2), (2, 1), (1, 2), (0, 3), (3, 1), (2, 2), (1, 3), (4, 1), (3, 2), (5, 1)):
            self.wait(k, s - 1)
            self.start(k, s)
            if s == 1:
                self.start(k + 3, 0)
        self.fetch(0)

    def fetch(self, k):
        self.wait(k, 3)
        self.load(k).start()

    def ready(self, k):
        self.load(k).wait()

    def advance(self, step, steps):
        for s, early in ((1, 6), (2, 4), (3, 2)):
            k = step + early

            @pl.when(k < steps)
            def _(k=k, s=s):
                self.wait(k, s - 1)
                self.start(k, s)

        @pl.when(step + 9 < steps)
        def _():
            self.start(step + 9, 0)


class GradSums:
    def __init__(self, me, outs, made, r0, r1, r2, r3, send, recv):
        self.me, self.outs, self.made = me, outs, made
        self.r0, self.r1, self.r2, self.r3, self.send, self.recv = r0, r1, r2, r3, send, recv

    def keep(self, step, i, j, grad):
        slot = lax.rem(step, 2)
        grad = grad.astype(BF)
        share = self.made.shape[-2]
        for y, c, x in itertools.product((0, 1), (0, 1), (0, 1)):
            row = ((y * 2 + c) * 2 + x) * share
            one, two = (x, y) if j == 0 else (y, x)
            self.made[slot, j, c, one, two, i] = grad[row : row + share]

    def axes(self, j):
        me = self.me
        along_x = (me.x, me.peer(x=1 - me.x))
        along_y = (me.y, me.peer(y=1 - me.y))
        return (along_x, along_y) if j == 0 else (along_y, along_x)

    def hop(self, k, j, s):
        me = self.me
        sems = (self.send, self.recv)
        r0, r1, r2, r3 = (r.at[k, j] for r in (self.r0, self.r1, self.r2, self.r3))
        (one, to_one), (two, to_two) = self.axes(j)
        if s == 0:
            give = self.made.at[lax.rem(k, 2), j, 1 - me.c]
            return [remote(give, r0, sems, (k, j, 0), me.peer(c=1 - me.c))]
        if s == 1:
            return [remote(r0.at[1 - one], r1, sems, (k, j, 1), to_one)]
        if s == 2:
            return [remote(r1.at[1 - two], r2, sems, (k, j, 2), to_two)]
        return [
            remote(r2.at[me.up(d)], r3.at[d - 1], sems, (k, j, 2 + d), me.peer(z=me.up(d)))
            for d in (1, 2, 3)
        ]

    def settle(self, k, j, s):
        me = self.me
        r0, r1, r2, r3 = (r.at[k, j] for r in (self.r0, self.r1, self.r2, self.r3))
        (one, _), (two, _) = self.axes(j)
        for copy in self.hop(k, j, s):
            copy.wait()
        if s == 0:
            add_into(r0, self.made.at[lax.rem(k, 2), j, me.c])
        elif s == 1:
            add_into(r1, r0.at[one])
        elif s == 2:
            add_into(r2, r1.at[two])
        else:
            width = r2.shape[-1]
            cols = pl.ds(pl.multiple_of(k * width, width), width)
            self.outs[j][:, cols] = (
                r2[me.z].astype(F32) + r3[0].astype(F32) + r3[1].astype(F32) + r3[2].astype(F32)
            )

    def advance(self, step, steps):
        for s, late in ((3, 4), (2, 3), (1, 2), (0, 1)):
            k = step - late

            @pl.when((k >= 0) & (k < steps))
            def _(s=s, k=k):
                for j in (0, 1):
                    self.settle(k, j, s)
                    if s < 3:
                        for copy in self.hop(k, j, s + 1):
                            copy.start()


def feed_kernel(
    block_t, steps, block_m, head,
    n_ref, c_ref, wg_ref, wd_ref, own_up, h_ref, cot_ref, g_ref, w_ref, o_ref, l_ref, ones_ref,
    gd_ref, gg_ref, gu_ref, all_up, out_ref, dh_ref, low_ref, do_ref, de_ref, gain_ref,
    n_scr, act_scr, dg_scr, du_scr, f_scr, dn_scr, slots, made, r0, r1, r2, r3,
    g_send, g_recv, s_send, s_recv, keep_sems, load_sems,
):
    step = pl.program_id(0)
    me = Place()
    gather = ColumnGather(me, own_up, all_up, slots, g_send, g_recv, keep_sems, load_sems)
    sums = GradSums(me, (gg_ref, gu_ref), made, r0, r1, r2, r3, s_send, s_recv)

    @pl.when(step == 0)
    def _():
        greet(me)
        n_scr[...] = n_ref[...].T
        f_scr[...] = jnp.zeros_like(f_scr)
        dn_scr[...] = jnp.zeros_like(dn_scr)
        gather.open()

    @pl.when(step < steps)
    def _():
        gather.ready(step)
        slot = lax.rem(step, 2)
        width, chunk = n_ref.shape[1], wd_ref.shape[0]
        ffn_block(
            block_t, n_ref, c_ref,
            lambda: wg_ref[...],
            lambda: slots[slot].reshape(width, chunk),
            lambda: wd_ref[...],
            f_scr, dn_scr, act_scr, dg_scr, du_scr,
        )

        @pl.when(step + 1 < steps)
        def _():
            gather.fetch(step + 1)

        for i in range(width // 256):
            normed = n_scr[256 * i : 256 * i + 256, :]
            sums.keep(step, i, 0, mm(normed, dg_scr[...]))
            sums.keep(step, i, 1, mm(normed, du_scr[...]))
        down_grad(gd_ref, act_scr, c_ref)

    gather.advance(step, steps)
    sums.advance(step, steps)

    @pl.when(step < steps)
    def _():
        for j in (0, 1):
            for copy in sums.hop(step, j, 0):
                copy.start()

    @pl.when(step == steps)
    def _():
        gain_ref[...] = jnp.zeros_like(gain_ref)

    @pl.when(step >= steps)
    def _():
        at = pl.ds(pl.multiple_of((step - steps) * block_m, block_m), block_m)
        middle_block(
            head, f_scr[at, :], dn_scr[at, :], h_ref, cot_ref, g_ref, w_ref, o_ref, l_ref, ones_ref,
            out_ref, dh_ref, low_ref, do_ref, de_ref, gain_ref,
        )


def feed_call(
    normed, grad_low, w_gate, w_down, own_up, hidden, cotangent, g, w_o, mixed, totals, ones, head,
    collective,
):
    total, width = normed.shape
    share, units = own_up.shape
    q_width = mixed.shape[1]
    chunk = largest_block(units, 512)
    steps = units // chunk
    block_t, block_m = largest_block(total, 256), largest_block(total, 128)
    last = steps - 1
    piece = (share, chunk)

    def after(n):
        return pl.BlockSpec((block_m, n), lambda i: (jnp.maximum(i - steps, 0), 0))

    anywhere = pl.BlockSpec(memory_space=pl.ANY)
    rows = pl.BlockSpec((chunk, width), lambda i: (jnp.minimum(i, last), 0))
    cols = pl.BlockSpec((width, chunk), lambda i: (0, jnp.minimum(i, last)))
    whole = jax.ShapeDtypeStruct((4, 2, 2, 2, share, units), BF)
    outs = pl.pallas_call(
        functools.partial(feed_kernel, block_t, steps, block_m, head),
        grid=(steps + total // block_m,),
        in_specs=[
            resident(normed.shape), resident(normed.shape), cols, rows, anywhere,
            after(width), after(width), resident(g.shape), resident(w_o.shape), after(q_width),
            after(q_width), resident(ones.shape),
        ],
        out_specs=[
            rows, resident((share, units)), resident((share, units)), anywhere,
            after(width), after(width), after(width), after(q_width), after(q_width),
            resident((1, width)),
        ],
        out_shape=[
            jax.ShapeDtypeStruct(w_down.shape, BF),
            jax.ShapeDtypeStruct((share, units), F32),
            jax.ShapeDtypeStruct((share, units), F32),
            whole,
            jax.ShapeDtypeStruct((total, width), BF),
            jax.ShapeDtypeStruct((total, width), F32),
            jax.ShapeDtypeStruct((total, width), BF),
            jax.ShapeDtypeStruct((total, q_width), BF),
            jax.ShapeDtypeStruct((total, q_width), F32),
            jax.ShapeDtypeStruct((1, width), F32),
        ],
        scratch_shapes=[
            pltpu.VMEM((width, total), BF),
            pltpu.VMEM((total, chunk), BF),
            pltpu.VMEM((total, chunk), BF),
            pltpu.VMEM((total, chunk), BF),
            pltpu.VMEM((total, width), F32),
            pltpu.VMEM((total, width), F32),
            pltpu.VMEM((2, 4, 2, 2, 2) + piece, BF),
            pltpu.VMEM((2, 2, 2, 2, 2, 4) + piece, BF),
            pltpu.VMEM((steps, 2, 2, 2, 4) + piece, BF),
            pltpu.VMEM((steps, 2, 2, 4) + piece, BF),
            pltpu.VMEM((steps, 2, 4) + piece, BF),
            pltpu.VMEM((steps, 2, 3) + piece, BF),
        ]
        + [pltpu.SemaphoreType.DMA((steps, 2, 6))] * 4
        + [pltpu.SemaphoreType.DMA((1,)), pltpu.SemaphoreType.DMA((2,))],
        compiler_params=pltpu.CompilerParams(
            vmem_limit_bytes=62 * 2**20, collective_id=collective, has_side_effects=True
        ),
        cost_estimate=pl.CostEstimate(
            flops=18 * total * width * units, bytes_accessed=12 * width * units, transcendentals=0
        ),
        name="feed",
    )(
        normed, grad_low, w_gate, w_down, own_up, hidden, cotangent, g, w_o, mixed, totals, ones
    )
    return outs[:3] + outs[4:]


def middle_block(
    head, ffn, incoming, h_ref, c_ref, g_ref, w_ref, o_ref, l_ref, ones_ref,
    out_ref, dh_ref, low_ref, do_ref, de_ref, gain_ref,
):
    hidden = h_ref[...]
    out_ref[...] = (hidden + ffn).astype(BF)
    inverse = lax.rsqrt(jnp.mean(hidden * hidden, axis=-1, keepdims=True) + epsilon)
    unit = hidden * inverse
    gain_ref[...] += jnp.sum(unit * incoming, axis=0, keepdims=True)
    scaled = incoming * g_ref[...]
    shared = jnp.mean(unit * scaled, axis=-1, keepdims=True)
    d_hidden = c_ref[...] + inverse * (scaled - unit * shared)
    dh_ref[...] = d_hidden
    low = d_hidden.astype(BF)
    low_ref[...] = low
    ones = ones_ref[...]
    wide = ones.shape[0]
    for c in range(0, o_ref.shape[1], wide):
        cols = slice(c, c + wide)
        d_att = mm(low, w_ref[cols, :], NT)
        ratio = 1.0 / l_ref[:, cols]
        do_ref[:, cols] = (d_att * ratio).astype(BF)
        de_ref[:, cols] = head_sum(d_att * o_ref[:, cols], ones) * ratio


def middle_kernel(head, f_ref, dn_ref, *refs):
    gain_ref = refs[-1]

    @pl.when(pl.program_id(0) == 0)
    def _():
        gain_ref[...] = jnp.zeros_like(gain_ref)

    middle_block(head, f_ref[...], dn_ref[...], *refs)


def middle_call(ffn, d_normed, hidden, cotangent, g, w_o, mixed, totals, ones, head):
    total, width = hidden.shape
    q_width = mixed.shape[1]
    block = largest_block(total, 256)

    def rows(n):
        return pl.BlockSpec((block, n), lambda i: (i, 0))

    return pl.pallas_call(
        functools.partial(middle_kernel, head),
        grid=(total // block,),
        in_specs=[
            rows(width), rows(width), rows(width), rows(width), resident(g.shape),
            resident(w_o.shape), rows(q_width), rows(q_width), resident(ones.shape),
        ],
        out_specs=[
            rows(width), rows(width), rows(width), rows(q_width), rows(q_width), resident((1, width)),
        ],
        out_shape=[
            jax.ShapeDtypeStruct((total, width), BF),
            jax.ShapeDtypeStruct((total, width), F32),
            jax.ShapeDtypeStruct((total, width), BF),
            jax.ShapeDtypeStruct((total, q_width), BF),
            jax.ShapeDtypeStruct((total, q_width), F32),
            jax.ShapeDtypeStruct((1, width), F32),
        ],
        compiler_params=params(),
        name="middle",
    )(ffn, d_normed, hidden, cotangent, g, w_o, mixed, totals, ones)


def head_back(grad, raw, gains, cos, sin, ones, head):
    grad = grad * cos + swap_halves(grad * sin, head)
    inv = lax.rsqrt(head_sum(raw * raw, ones) * (1.0 / head) + epsilon)
    unit = raw * inv
    gained = jnp.sum(unit * grad, axis=0, keepdims=True)
    scaled = grad * gains
    shared = head_sum(unit * scaled, ones) * (1.0 / head)
    return inv * (scaled - unit * shared), sum(
        gained[:, i : i + LANES] for i in range(0, gained.shape[1], LANES)
    )


def last_q_kernel(
    head, scale, dq_ref, raw_ref, gains_ref, cos_ref, sin_ref, ones_ref, w_ref,
    d_ref, part_ref, gq_ref,
):
    @pl.when(pl.program_id(0) == 0)
    def _():
        gq_ref[...] = jnp.zeros_like(gq_ref)

    ones = ones_ref[...]
    wide = ones.shape[0]
    cos, sin = spread(cos_ref[...], wide), spread(sin_ref[...], wide)
    for c in range(0, dq_ref.shape[1], wide):
        cols = slice(c, c + wide)
        grad, gained = head_back(
            dq_ref[:, cols] * scale, raw_ref[:, cols], gains_ref[:, cols], cos, sin, ones, head
        )
        gq_ref[...] += gained
        d_ref[:, cols] = grad.astype(BF)
    part_ref[...] = mm(d_ref[...], w_ref[...], NT)


def last_kernel(
    kv_width, head,
    dk_ref, dv_ref, raw_ref, gains_ref, cos_ref, sin_ref, ones_ref, w_ref, part_ref, x_ref, g_ref,
    dh_ref, *refs,
):
    got_ref = refs[0] if len(refs) == 5 else None
    d_ref, in_ref, gain_ref, gk_ref = refs[-4:]

    @pl.when(pl.program_id(0) == 0)
    def _():
        gain_ref[...] = jnp.zeros_like(gain_ref)
        gk_ref[...] = jnp.zeros_like(gk_ref)

    ones = ones_ref[...]
    wide = ones.shape[0]
    cos, sin = spread(cos_ref[...], wide), spread(sin_ref[...], wide)
    for c in range(0, kv_width, wide):
        cols = slice(c, c + wide)
        grad = dk_ref[:, cols].astype(F32)
        if got_ref is not None:
            grad += got_ref[:, cols].astype(F32)
        grad, gained = head_back(
            grad, raw_ref[:, cols], gains_ref[:, cols], cos, sin, ones, head
        )
        gk_ref[...] += gained
        d_ref[:, cols] = grad.astype(BF)
    d_values = dv_ref[...].astype(F32)
    if got_ref is not None:
        d_values += got_ref[:, kv_width:].astype(F32)
    d_ref[:, kv_width:] = d_values.astype(BF)
    d_normed = part_ref[...] + mm(d_ref[...], w_ref[...], NT)
    x = x_ref[...].astype(F32)
    inverse = lax.rsqrt(jnp.mean(x * x, axis=-1, keepdims=True) + epsilon)
    unit = x * inverse
    gain_ref[...] += jnp.sum(unit * d_normed, axis=0, keepdims=True)
    scaled = d_normed * g_ref[...]
    shared = jnp.mean(unit * scaled, axis=-1, keepdims=True)
    in_ref[...] = dh_ref[...] + inverse * (scaled - unit * shared)


def row_blocks(total):
    block = largest_block(total, 256)
    return total // block, lambda n: pl.BlockSpec((block, n), lambda i: (i, 0))


def some_cols(w, first, count):
    return pl.BlockSpec(
        (w.shape[0], count), lambda i: (0, first // count), pipeline_mode=pl.Buffered(1)
    )


def last_q_call(dq, raw, gains, cos, sin, ones, w, head):
    total, q_width = dq.shape
    width = w.shape[0]
    blocks, rows = row_blocks(total)
    return pl.pallas_call(
        functools.partial(last_q_kernel, head, head ** (-0.5)),
        grid=(blocks,),
        in_specs=[
            rows(q_width), rows(q_width), resident(gains.shape), rows(LANES), rows(LANES),
            resident(ones.shape), some_cols(w, 0, q_width),
        ],
        out_specs=[rows(q_width), rows(width), resident((1, LANES))],
        out_shape=[
            jax.ShapeDtypeStruct((total, q_width), BF),
            jax.ShapeDtypeStruct((total, width), F32),
            jax.ShapeDtypeStruct((1, LANES), F32),
        ],
        compiler_params=params(),
        name="last_q",
    )(dq, raw, gains, cos, sin, ones, w)


def last_call(dk, dv, raw, gains, cos, sin, ones, w, part, x, g, d_hidden, head, got=()):
    total, width = x.shape
    kv_width = dk.shape[1]
    blocks, rows = row_blocks(total)
    return pl.pallas_call(
        functools.partial(last_kernel, kv_width, head),
        grid=(blocks,),
        in_specs=[
            rows(kv_width), rows(kv_width), rows(kv_width), resident(gains.shape), rows(LANES),
            rows(LANES), resident(ones.shape), some_cols(w, w.shape[1] - 2 * kv_width, 2 * kv_width),
            rows(width), rows(width), resident(g.shape), rows(width),
        ] + [rows(2 * kv_width)] * len(got),
        out_specs=[
            rows(2 * kv_width), rows(width), resident((1, width)), resident((1, LANES)),
        ],
        out_shape=[
            jax.ShapeDtypeStruct((total, 2 * kv_width), BF),
            jax.ShapeDtypeStruct((total, width), F32),
            jax.ShapeDtypeStruct((1, width), F32),
            jax.ShapeDtypeStruct((1, LANES), F32),
        ],
        compiler_params=params(),
        name="last",
    )(dk, dv, raw, gains, cos, sin, ones, w, part, x, g, d_hidden, *got)


class Place:
    def __init__(self):
        dp = lax.axis_index("dp")
        self.x = lax.axis_index("ctx")
        self.c = lax.rem(dp, 2)
        self.y = lax.rem(dp // 2, 2)
        self.z = dp // 4

    def peer(self, z=None, y=None, c=None, x=None):
        z = self.z if z is None else z
        y = self.y if y is None else y
        c = self.c if c is None else c
        x = self.x if x is None else x
        return {"dp": (z * 2 + y) * 2 + c, "ctx": x}

    def up(self, d):
        return lax.rem(self.z + d, 4)

    def peers(self):
        return [self.peer(z=self.up(d)) for d in (1, 2, 3)] + [
            self.peer(x=1 - self.x), self.peer(y=1 - self.y), self.peer(c=1 - self.c)
        ]


def greet(place):
    barrier = pltpu.get_barrier_semaphore()
    peers = place.peers()
    for peer in peers:
        pl.semaphore_signal(barrier, inc=1, device_id=peer, device_id_type=pl.DeviceIdType.MESH)
    pl.semaphore_wait(barrier, len(peers))


def remote(src, dst, sems, at, peer):
    send, recv = sems
    return pltpu.make_async_remote_copy(
        src_ref=src, dst_ref=dst, send_sem=send.at[at], recv_sem=recv.at[at],
        device_id=peer, device_id_type=pl.DeviceIdType.MESH,
    )


def gather_kernel(pieces, count, *refs):
    ins, outs = refs[:count], refs[count : 2 * count]
    sems, local = refs[2 * count : 2 * count + 2], refs[2 * count + 2]
    me = Place()
    greet(me)

    def block(p, z, y, c, x):
        array, rows, cols, _ = pieces[p]
        return outs[array].at[z, y, c, x, rows, cols]

    def own(p):
        array, rows, cols, _ = pieces[p]
        return ins[array].at[rows, cols]

    every = slice(None)

    def to_z(p):
        return [
            remote(own(p), block(p, me.z, me.y, me.c, me.x), sems, (p, d - 1), me.peer(z=me.up(d)))
            for d in (1, 2, 3)
        ]

    def keep(p):
        return pltpu.make_async_copy(own(p), block(p, me.z, me.y, me.c, me.x), local.at[p])

    def first(p):
        mine = block(p, every, me.y, me.c, me.x)
        peer = me.peer(x=1 - me.x) if pieces[p][3] else me.peer(y=1 - me.y)
        return [remote(mine, mine, sems, (p, 3), peer)]

    def second(p):
        if pieces[p][3]:
            mine, peer = block(p, every, me.y, me.c, every), me.peer(y=1 - me.y)
        else:
            mine, peer = block(p, every, every, me.c, me.x), me.peer(x=1 - me.x)
        return [remote(mine, mine, sems, (p, 4), peer)]

    def third(p):
        mine = block(p, every, every, me.c, every)
        return [remote(mine, mine, sems, (p, 5), me.peer(c=1 - me.c))]

    n = len(pieces)
    stages = [to_z, first, second, third]
    pair = 2

    def begin(p):
        keep(p).start()
        for copy in to_z(p):
            copy.start()

    for p in range(min(n, AHEAD)):
        begin(p)
    for t in range(0, n + 3 * pair, pair):
        for p in range(t + AHEAD, min(n, t + AHEAD + pair)):
            begin(p)
        for s in (1, 2, 3):
            for p in range(t - (s - 1) * pair, t - (s - 1) * pair + pair):
                if 0 <= p < n:
                    if s == 1:
                        keep(p).wait()
                    for copy in stages[s - 1](p):
                        copy.wait_recv()
                    for copy in stages[s](p):
                        copy.start()
    for p in range(n):
        third(p)[0].wait_recv()
    for p in range(n):
        for stage in stages:
            for copy in stage(p):
                copy.wait_send()


def gather_call(shards, pieces, collective):
    count = len(shards)
    outs = pl.pallas_call(
        functools.partial(gather_kernel, pieces, count),
        in_specs=[pl.BlockSpec(memory_space=pl.ANY)] * count,
        out_specs=[pl.BlockSpec(memory_space=pl.ANY)] * count,
        out_shape=[jax.ShapeDtypeStruct((4, 2, 2, 2) + s.shape, s.dtype) for s in shards],
        scratch_shapes=[
            pltpu.SemaphoreType.DMA((len(pieces), 6)),
            pltpu.SemaphoreType.DMA((len(pieces), 6)),
            pltpu.SemaphoreType.DMA((len(pieces),)),
        ],
        compiler_params=pltpu.CompilerParams(
            collective_id=collective, has_side_effects=True, vmem_limit_bytes=VMEM_LIMIT
        ),
        name="gather",
    )(*shards)
    return [o.reshape(32 * s.shape[0], s.shape[1]) for o, s in zip(outs, shards)]


def add_into(total, more):
    def step(i, carry):
        total[i] = (total[i].astype(F32) + more[i].astype(F32)).astype(total.dtype)
        return carry

    lax.fori_loop(0, total.shape[0], step, 0)


def scatter_kernel(pieces, count, gains, *refs):
    if gains:
        gain_ref, gain_out = refs[count], refs[2 * count + 1]
        sum_scr, got_scr, z_scr, gain_send, gain_recv = refs[-5:]
        refs = refs[:count] + refs[count + 1 : 2 * count + 1] + refs[2 * count + 2 : -5]
    ins, outs = refs[:count], refs[count : 2 * count]
    n = len(pieces)
    shapes, homes = piece_homes(pieces)
    scratch = refs[2 * count : 2 * count + 5 * len(shapes)]
    homes = [
        (scratch[5 * k : 5 * k + 4], i, scratch[5 * k + 4].at[i % OWN], (k, i % OWN)) for k, i in homes
    ]
    sems, local = refs[-3:-1], refs[-1]
    me = Place()
    greet(me)
    every = slice(None)

    def at(p, s):
        return homes[p][0][s].at[homes[p][1]]

    def part(p, c):
        array, rows, cols, _ = pieces[p]
        return ins[array].at[every, every, c, every, rows, cols]

    def load(p):
        return pltpu.make_async_copy(part(p, me.c), homes[p][2], local.at[homes[p][3]])

    def pairs(p):
        return [remote(part(p, 1 - me.c), at(p, 0), sems, (p, 0), me.peer(c=1 - me.c))]

    def first(p):
        if pieces[p][3]:
            give, peer = at(p, 0).at[every, every, 1 - me.x], me.peer(x=1 - me.x)
        else:
            give, peer = at(p, 0).at[every, 1 - me.y], me.peer(y=1 - me.y)
        return [remote(give, at(p, 1), sems, (p, 1), peer)]

    def second(p):
        if pieces[p][3]:
            peer, other = me.peer(y=1 - me.y), 1 - me.y
        else:
            peer, other = me.peer(x=1 - me.x), 1 - me.x
        return [remote(at(p, 1).at[every, other], at(p, 2), sems, (p, 2), peer)]

    def third(p):
        return [
            remote(at(p, 2).at[me.up(d)], at(p, 3).at[d - 1], sems, (p, 2 + d), me.peer(z=me.up(d)))
            for d in (1, 2, 3)
        ]

    stages = [pairs, first, second, third]

    def settle(p, s):
        if s == 0:
            load(p).wait()
            add_into(at(p, 0), homes[p][2])
        elif s == 1:
            kept = at(p, 0).at[every, every, me.x] if pieces[p][3] else at(p, 0).at[every, me.y]
            add_into(at(p, 1), kept)
        elif s == 2:
            add_into(at(p, 2), at(p, 1).at[every, me.y if pieces[p][3] else me.x])
        else:
            array, rows, cols, _ = pieces[p]
            more = at(p, 3)
            outs[array][rows, cols] = (
                at(p, 2)[me.z].astype(F32) + more[0].astype(F32) + more[1].astype(F32) + more[2].astype(F32)
            )

    pair = 2

    def begin(p):
        load(p).start()
        for copy in pairs(p):
            copy.start()

    hops = []
    if gains:
        near = [me.peer(c=1 - me.c), me.peer(x=1 - me.x), me.peer(y=1 - me.y)]
        hops = [
            [remote(sum_scr.at[i], got_scr.at[i], (gain_send, gain_recv), i, peer)]
            for i, peer in enumerate(near)
        ] + [[
            remote(sum_scr.at[3], z_scr.at[me.z], (gain_send, gain_recv), 2 + d, me.peer(z=me.up(d)))
            for d in (1, 2, 3)
        ]]

    def gain_step(i):
        if i == 0:
            sum_scr[0] = gain_ref[...]
        else:
            for copy in hops[i - 1]:
                copy.wait_recv()
            if i < 4:
                sum_scr[i] = sum_scr[i - 1] + got_scr[i - 1]
        if i == 3:
            z_scr[me.z] = sum_scr[3]
        if i < 4:
            for copy in hops[i]:
                copy.start()
        else:
            gain_out[...] = (z_scr[0] + z_scr[1]) + (z_scr[2] + z_scr[3])
            for hop in hops:
                for copy in hop:
                    copy.wait_send()

    for p in range(min(n, AHEAD)):
        begin(p)
    rounds = range(0, n + 3 * pair, pair)
    for t in rounds:
        if gains:
            for i in range(5):
                if i * (len(rounds) - 1) // 4 == t // pair:
                    gain_step(i)
        for s in range(4):
            for p in range(t - s * pair, t - s * pair + pair):
                if 0 <= p < n:
                    for copy in stages[s](p):
                        copy.wait_recv()
                    settle(p, s)
                    if s < 3:
                        for copy in stages[s + 1](p):
                            copy.start()
            if s == 0:
                for p in range(t + AHEAD, min(n, t + AHEAD + pair)):
                    begin(p)
    for p in range(n):
        for stage in stages:
            for copy in stage(p):
                copy.wait_send()


def piece_homes(pieces):
    shapes, homes = [], []
    for _, rows, cols, _ in pieces:
        shape = (rows.stop - rows.start, cols.stop - cols.start)
        if shape not in shapes:
            shapes.append(shape)
        kind = shapes.index(shape)
        homes.append((kind, sum(k == kind for k, _ in homes)))
    return shapes, homes


def scatter_call(grads, pieces, collective, gains=()):
    count = len(grads)
    shards = [(g.shape[0] // 32, g.shape[1]) for g in grads]
    grads = [g.reshape((4, 2, 2, 2) + s) for g, s in zip(grads, shards)]
    shapes, homes = piece_homes(pieces)
    scratch = []
    for kind, shape in enumerate(shapes):
        n = sum(k == kind for k, _ in homes)
        scratch += [
            pltpu.VMEM((n, 4, 2, 2) + shape, BF),
            pltpu.VMEM((n, 4, 2) + shape, BF),
            pltpu.VMEM((n, 4) + shape, BF),
            pltpu.VMEM((n, 3) + shape, BF),
            pltpu.VMEM((OWN, 4, 2, 2) + shape, BF),
        ]
    return pl.pallas_call(
        functools.partial(scatter_kernel, pieces, count, len(gains)),
        in_specs=[pl.BlockSpec(memory_space=pl.ANY)] * count
        + [pl.BlockSpec(memory_space=pltpu.VMEM)] * len(gains),
        out_specs=[pl.BlockSpec(memory_space=pltpu.VMEM)] * (count + len(gains)),
        out_shape=[jax.ShapeDtypeStruct(s, F32) for s in shards]
        + [jax.ShapeDtypeStruct(g.shape, F32) for g in gains],
        scratch_shapes=scratch + [
            pltpu.SemaphoreType.DMA((len(pieces), 6)),
            pltpu.SemaphoreType.DMA((len(pieces), 6)),
            pltpu.SemaphoreType.DMA((len(shapes), OWN)),
        ] + [
            scratch
            for g in gains
            for scratch in (
                pltpu.VMEM((4,) + g.shape, F32),
                pltpu.VMEM((3,) + g.shape, F32),
                pltpu.VMEM((4,) + g.shape, F32),
                pltpu.SemaphoreType.DMA((6,)),
                pltpu.SemaphoreType.DMA((6,)),
            )
        ],
        compiler_params=pltpu.CompilerParams(
            collective_id=collective, has_side_effects=True, vmem_limit_bytes=VMEM_LIMIT
        ),
        name="scatter",
    )(*grads, *gains)


def col_pieces(array, rows, cols, width=512, high=None):
    high = high or rows
    return [
        (array, slice(r, r + high), slice(c, c + width), (c // width) % 2 == 0)
        for r in range(0, rows, high)
        for c in range(0, cols, width)
    ]


def interleave(one, two):
    return [p for pair in zip(one, two) for p in pair]


def per_device(
    tokens, segments, cotangent, w_q, w_k, w_v, w_o, w_gate, w_up, w_down, g_attn, g_q, g_k, g_ffn
):
    seqs, rows, width = tokens.shape
    length = segments.shape[1]
    head = g_q.shape[0]
    q_width, kv_width = w_q.shape[1], w_k.shape[1]
    kv_heads = kv_width // head
    q_heads = q_width // head
    total = seqs * rows
    row_start = lax.axis_index("ctx") * rows
    own_kernels = (lax.axis_size("dp"), lax.axis_size("ctx")) == (16, 2)
    share = w_q.shape[0]

    def fetch(weight):
        return lax.all_gather(weight, AXES, axis=0, tiled=True)

    def send(grad):
        return lax.psum_scatter(grad, AXES, scatter_dimension=0, tiled=True).astype(F32)

    seg_rows = lax.dynamic_slice_in_dim(segments, row_start, rows, 1)
    first = jnp.sum((segments[:, None, :] < seg_rows[:, :, None]).astype(jnp.int32), axis=-1)
    query_pos = row_start + jnp.arange(rows, dtype=jnp.int32)
    positions = (query_pos[None, :] - first).reshape(total)
    frequency = rope_base ** (-jnp.arange(0, head, 2, dtype=F32) / head)
    angles = positions.astype(F32)[:, None] * frequency[None, :]
    cos, sin = jnp.cos(angles), jnp.sin(angles)
    cos = jnp.concatenate([cos] * (2 * LANES // head), axis=1)
    sin = jnp.concatenate([-sin, sin] * (LANES // head), axis=1)
    wide = 2 * LANES
    member = jnp.arange(wide) // head
    ones = (member[:, None] == member[None, :]).astype(BF)
    gains_q = jnp.concatenate([g_q] * q_heads)[None, :]
    gains_k = jnp.concatenate([g_k] * kv_heads)[None, :]
    x = tokens.reshape(total, width)
    cotangent = cotangent.reshape(total, width)

    w_qkv = jnp.concatenate([w_q, w_k, w_v], axis=1)
    w_down, w_gate = fetch(w_down), fetch(w_gate)
    grad_low = cotangent.astype(BF)
    if own_kernels:
        qkv_pieces = col_pieces(0, share, w_qkv.shape[1])
        o_pieces = col_pieces(0, share, w_o.shape[1])
        [w_qkv] = gather_call([w_qkv], qkv_pieces, 0)
    else:
        w_qkv, w_o = fetch(w_qkv), fetch(w_o)
        w_up = fetch(w_up)

    tables = (cos, sin, ones, head)
    normed, kv, raw_k = project_call(
        x, w_qkv, (q_width, 2 * kv_width), kv_width, g_attn[None, :], gains_k, *tables, None, "project_kv"
    )
    kv = kv.reshape(seqs, rows, 2 * kv_width)
    if own_kernels:
        before = lax.ppermute(kv, "ctx", [(0, 1)])
    _, q, raw_q = project_call(
        x, w_qkv, (0, q_width), q_width, g_attn[None, :], gains_q, *tables, head ** (-0.5), "project_q"
    )
    q = q.reshape(seqs, rows, q_width)
    block_q, block_k = min(256, rows), min(256, length)
    at = jnp.arange(0, rows, block_q, dtype=jnp.int32)[None, :]
    lowest = first[:, ::block_q]
    zero = jnp.zeros((1,), jnp.int32)
    if own_kernels:
        own_first = first - row_start
        own_keys = (
            jnp.maximum(lowest - row_start, 0) // block_k,
            jnp.broadcast_to((at + block_q - 1) // block_k + 1, lowest.shape),
            zero,
        )
        far_first = own_first + rows
        far_keys = (
            jnp.clip(lowest - row_start + rows, 0, rows) // block_k,
            jnp.full(lowest.shape, rows // block_k, jnp.int32),
            zero + rows,
        )
        near = attend_call(q, kv, own_first, own_keys, block_q, block_k, last_part=False)
        w_o, _ = lax.optimization_barrier((w_o, near))
        [w_o] = gather_call([w_o], [p[:3] + (True,) for p in o_pieces], 4)
        mixed, totals = attend_call(q, before, far_first, far_keys, block_q, block_k, near)
    else:
        kv = lax.all_gather(kv, "ctx", axis=1, tiled=True)
        all_keys = (
            lowest // block_k,
            jnp.broadcast_to((row_start + at + block_q - 1) // block_k + 1, lowest.shape),
            zero + row_start,
        )
        mixed, totals = attend_call(q, kv, first, all_keys, block_q, block_k)
    mixed, totals = mixed.reshape(total, q_width), totals.reshape(total, q_width)
    attended, hidden, normed_two = hidden_call(mixed, w_o, x, g_ffn[None, :])

    middle_args = (hidden, cotangent, g_ffn[None, :], w_o, mixed, totals, ones, head)
    if own_kernels:
        grad_down, out_gate, out_up, outputs, d_hidden, d_low, d_out, delta, grad_gffn = feed_call(
            normed_two, grad_low, w_gate, w_down, w_up, *middle_args, 2
        )
    else:
        ffn, d_normed_two, grad_down, out_gate, out_up = ffn_call(
            normed_two, grad_low, w_gate, w_up, w_down
        )
        out_gate, out_up = send(out_gate), send(out_up)
        outputs, d_hidden, d_low, d_out, delta, grad_gffn = middle_call(
            ffn, d_normed_two, *middle_args
        )
    out_down = send(grad_down)
    d_out, delta = d_out.reshape(q.shape), delta.reshape(q.shape)
    if own_kernels:
        far_dq, dk, dv = attend_back_call(
            q, d_out, delta, before, far_first, far_keys, block_q, block_k
        )
        got = lax.ppermute(jnp.concatenate([dk, dv], axis=2), "ctx", [(1, 0)])
        dq, dk, dv = attend_back_call(
            q, d_out, delta, kv, own_first, own_keys, block_q, block_k, (far_dq,)
        )
        dk, dv, got = dk.reshape(total, kv_width), dv.reshape(total, kv_width), (got.reshape(total, -1),)
    else:
        dq, dk, dv = attend_back_call(q, d_out, delta, kv, first, all_keys, block_q, block_k)
        dkv = lax.psum_scatter(
            jnp.concatenate([dk, dv], axis=2), "ctx", scatter_dimension=1, tiled=True
        ).reshape(total, 2 * kv_width)
        dk, dv, got = dkv[:, :kv_width], dkv[:, kv_width:], ()
    grad_o = mm(attended, d_low, TN).astype(BF)
    d_q, part, grad_gq = last_q_call(
        dq.reshape(total, q_width), raw_q, gains_q, cos, sin, ones, w_qkv, head
    )
    grad_q = mm(normed, d_q, TN).astype(BF)
    if own_kernels:
        got, grad_q, part, grad_o = lax.optimization_barrier((got, grad_q, part, grad_o))
    d_kv, input_grad, grad_gattn, grad_gk = last_call(
        dk, dv, raw_k, gains_k, cos, sin, ones, w_qkv, part, x, g_attn[None, :], d_hidden, head, got
    )
    grad_kv = mm(normed, d_kv, TN).astype(BF)
    if own_kernels:
        flat = jnp.concatenate([grad_gattn, grad_gffn, grad_gq, grad_gk], axis=1).reshape(-1, LANES)
        flat = jnp.pad(flat, ((0, -flat.shape[0] % 8), (0, 0)))
        last_pieces = [
            (array,) + p[1:] for array, width_of in enumerate((width, q_width, 2 * kv_width))
            for p in col_pieces(array, share, width_of)
        ]
        out_o, out_q, out_kv, flat = scatter_call([grad_o, grad_q, grad_kv], last_pieces, 3, (flat,))
        flat = flat.reshape(1, -1)
        grad_gattn, grad_gffn = flat[:, :width], flat[:, width : 2 * width]
        grad_gq = flat[:, 2 * width : 2 * width + LANES]
        grad_gk = flat[:, 2 * width + LANES : 2 * width + 2 * LANES]
    else:
        out_q, out_kv, out_o = send(grad_q), send(grad_kv), send(grad_o)
        grad_gattn, grad_gffn, grad_gq, grad_gk = lax.psum(
            (grad_gattn, grad_gffn, grad_gq, grad_gk), AXES
        )

    def fold(grad):
        return jnp.sum(grad.reshape(LANES // head, head), axis=0)

    return (
        outputs.reshape(tokens.shape),
        input_grad.reshape(tokens.shape),
        out_q,
        out_kv[:, :kv_width],
        out_kv[:, kv_width:],
        out_o,
        out_gate,
        out_up,
        out_down,
        grad_gattn[0],
        fold(grad_gq),
        fold(grad_gk),
        grad_gffn[0],
    )


def solution(mesh):
    split = P("dp", "ctx", None)
    shard = P(("dp", "ctx"), None)
    in_specs = (split, P("dp", None), split) + (shard,) * 7 + (P(),) * 4
    out_specs = (split, split) + (shard,) * 7 + (P(),) * 4
    return jax.shard_map(
        per_device, mesh=mesh, in_specs=in_specs, out_specs=out_specs, check_vma=False
    )
```

```python
import functools
import itertools

import jax
import jax.numpy as jnp
from jax import lax
from jax.experimental import pallas as pl
from jax.experimental.pallas import tpu as pltpu
from jax.sharding import PartitionSpec as P

epsilon = 1e-05
rope_base = 1000000.0
AXES = ("dp", "ctx")
BF = jnp.bfloat16
F32 = jnp.float32
LANES = 128
VMEM_LIMIT = 56 * 2**20
AHEAD = 4
OWN = 6
NN = (((1,), (0,)), ((), ()))
NT = (((1,), (1,)), ((), ()))
TN = (((0,), (0,)), ((), ()))


def mm(a, b, dims=NN):
    return lax.dot_general(a, b, dims, preferred_element_type=F32)


def params(semantics=None):
    return pltpu.CompilerParams(
        vmem_limit_bytes=VMEM_LIMIT,
        dimension_semantics=semantics,
    )


def resident(shape):
    zeros = (0,) * len(shape)
    return pl.BlockSpec(shape, lambda *_: zeros, pipeline_mode=pl.Buffered(1))


def largest_block(size, most):
    return max(b for b in range(1, min(size, most) + 1) if size % b == 0)


def head_sum(field, ones):
    wide = ones.shape[0]
    high = field.astype(BF)
    low = (field - high.astype(F32)).astype(BF)
    parts = [
        mm(high[:, c : c + wide], ones) + mm(low[:, c : c + wide], ones)
        for c in range(0, field.shape[1], wide)
    ]
    return jnp.concatenate(parts, axis=1)


def swap_halves(field, head):
    half = head // 2
    width = field.shape[1]
    lane = lax.broadcasted_iota(jnp.int32, field.shape, 1)
    return jnp.where(
        lane % head < half,
        pltpu.roll(field, width - half, 1),
        pltpu.roll(field, half, 1),
    )


def spread(table, width):
    return jnp.concatenate([table] * (width // table.shape[1]), axis=1)


def project_kernel(
    rope_width, head, scale,
    x_ref, w_ref, g_ref, gain_ref, cos_ref, sin_ref, ones_ref,
    normed_ref, out_ref, raw_ref,
):
    x = x_ref[...].astype(F32)
    inverse = lax.rsqrt(jnp.mean(x * x, axis=-1, keepdims=True) + epsilon)
    normed = (x * inverse * g_ref[...]).astype(BF)
    normed_ref[...] = normed
    ones = ones_ref[...]
    wide = ones.shape[0]
    cos = spread(cos_ref[...], wide)
    sin = spread(sin_ref[...], wide)
    for c in range(0, rope_width, wide):
        raw = mm(normed, w_ref[:, c : c + wide])
        raw_ref[:, c : c + wide] = raw
        inv = lax.rsqrt(head_sum(raw * raw, ones) * (1.0 / head) + epsilon)
        field = raw * inv * gain_ref[:, c : c + wide]
        turned = (field * cos + swap_halves(field, head) * sin).astype(BF)
        out_ref[:, c : c + wide] = turned if scale is None else turned * jnp.asarray(scale, BF)
    if rope_width < w_ref.shape[1]:
        out_ref[:, rope_width:] = mm(normed, w_ref[:, rope_width:]).astype(BF)


def project_call(x, w, cols, rope_width, g, gains, cos, sin, ones, head, scale, name):
    total, width = x.shape
    block = largest_block(total, 256)
    at, count = cols[0] // cols[1], cols[1]

    def rows(n):
        return pl.BlockSpec((block, n), lambda i: (i, 0))

    return pl.pallas_call(
        functools.partial(project_kernel, rope_width, head, scale),
        grid=(total // block,),
        in_specs=[
            rows(width),
            pl.BlockSpec((width, count), lambda i: (0, at), pipeline_mode=pl.Buffered(1)),
            resident(g.shape), resident(gains.shape),
            rows(LANES), rows(LANES), resident(ones.shape),
        ],
        out_specs=[rows(width), rows(count), rows(rope_width)],
        out_shape=[
            jax.ShapeDtypeStruct((total, width), BF),
            jax.ShapeDtypeStruct((total, count), BF),
            jax.ShapeDtypeStruct((total, rope_width), F32),
        ],
        compiler_params=params(),
        cost_estimate=pl.CostEstimate(
            flops=2 * total * width * count, bytes_accessed=2 * width * count + 10 * total * count,
            transcendentals=0,
        ),
        name=name,
    )(x, w, g, gains, cos, sin, ones)


def pad_head(pair, odd, fill):
    lane = lax.broadcasted_iota(jnp.int32, pair.shape, 1)
    if odd:
        pair = pltpu.roll(pair, LANES // 2, 1)
    return jnp.where(lane < LANES // 2, pair, jnp.asarray(fill, pair.dtype))


def attend_kernel(
    block_q, block_k, heads, more, last_part,
    low_ref, high_ref, start_ref, q_ref, k_ref, v_ref, first_ref, *refs,
):
    prior = refs[:2] if more else ()
    out_ref, total_ref, k_scr, v_scr = refs[len(prior) :]
    s = pl.program_id(0)
    rows = q_ref.shape[1]
    start = start_ref[0]
    half = LANES // 2
    for h in range(heads):
        c = h // 2 * LANES
        k_scr[h] = pad_head(k_ref[0, :, c : c + LANES].astype(F32), h % 2, 0).astype(BF)
        v_scr[h] = pad_head(v_ref[0, :, c : c + LANES].astype(F32), h % 2, 1).astype(BF)
    lane = lax.broadcasted_iota(jnp.int32, (block_q, LANES), 1)
    key_lane = lax.broadcasted_iota(jnp.int32, (2 * block_q, block_k), 1)
    row = lax.broadcasted_iota(jnp.int32, (2 * block_q, 1), 0) % block_q

    def q_step(i, carry):
        at = pl.multiple_of(i * block_q, block_q)
        first = first_ref[0, pl.ds(at, block_q), :]
        first = jnp.concatenate([first, first], axis=0)
        last = row + (start + at)
        queries = []
        for h in range(heads):
            pair = q_ref[0, pl.ds(at, block_q), h * LANES : (h + 1) * LANES].astype(F32)
            queries.append(
                jnp.concatenate([pad_head(pair, 0, 0), pad_head(pair, 1, 0)], axis=0).astype(BF)
            )

        def k_step(j, sums):
            key_at = pl.multiple_of(j * block_k, block_k)
            key = key_lane + key_at
            live = (key >= first) & (key <= last)
            new = []
            for h in range(heads):
                scores = mm(queries[h], k_scr[h, pl.ds(key_at, block_k), :], NT)
                expo = jnp.where(live, jnp.exp(scores), 0.0).astype(BF)
                new.append(sums[h] + mm(expo, v_scr[h, pl.ds(key_at, block_k), :]))
            return tuple(new)

        sums = lax.fori_loop(
            low_ref[s, i], high_ref[s, i], k_step,
            tuple(jnp.zeros((2 * block_q, LANES), F32) for _ in range(heads)),
        )
        for h in range(heads):
            even, odd = sums[h][:block_q], sums[h][block_q:]
            both = jnp.where(lane < half, even, pltpu.roll(odd, half, 1))
            tot = jnp.where(lane < half, pltpu.roll(even, half, 1), odd)
            cols = slice(h * LANES, (h + 1) * LANES)
            if more:
                both += prior[0][0, pl.ds(at, block_q), cols]
                tot += prior[1][0, pl.ds(at, block_q), cols]
            out_ref[0, pl.ds(at, block_q), cols] = both / tot if last_part else both
            total_ref[0, pl.ds(at, block_q), cols] = tot
        return carry

    lax.fori_loop(0, rows // block_q, q_step, 0)


def attend_call(q, kv, first, keys, block_q, block_k, prior=(), last_part=True):
    seqs, rows, q_width = q.shape
    length = kv.shape[1]
    kv_heads = q_width // LANES
    heads = largest_block(kv_heads, 8)
    steps = kv_heads // heads
    half = LANES // 2
    spec_q = pl.BlockSpec((1, rows, heads * LANES), lambda s, p, *_: (s, 0, p))
    return pl.pallas_call(
        functools.partial(attend_kernel, block_q, block_k, heads, bool(prior), last_part),
        grid_spec=pltpu.PrefetchScalarGridSpec(
            num_scalar_prefetch=3,
            grid=(seqs, steps),
            in_specs=[
                spec_q,
                pl.BlockSpec((1, length, heads * half), lambda s, p, *_: (s, 0, p)),
                pl.BlockSpec((1, length, heads * half), lambda s, p, *_: (s, 0, p + steps)),
                pl.BlockSpec((1, rows, 1), lambda s, p, *_: (s, 0, 0)),
            ] + [spec_q] * len(prior),
            out_specs=[spec_q, spec_q],
            scratch_shapes=[
                pltpu.VMEM((heads, length, LANES), BF),
                pltpu.VMEM((heads, length, LANES), BF),
            ],
        ),
        out_shape=[jax.ShapeDtypeStruct(q.shape, F32)] * 2,
        compiler_params=params(),
        cost_estimate=pl.CostEstimate(
            flops=4 * seqs * rows * length * q_width, bytes_accessed=16 * seqs * rows * q_width,
            transcendentals=0,
        ),
        name="attend",
    )(*keys, q, kv, kv, first[:, :, None], *prior)


def attend_back_kernel(
    block_q, block_k, heads, more,
    low_ref, high_ref, start_ref, q_ref, do_ref, de_ref, k_ref, v_ref, first_ref, *refs,
):
    prior_ref = refs[0] if more else None
    dq_ref, dk_ref, dv_ref, k_scr, v_scr, dk_scr, dv_scr = refs[int(more) :]
    s = pl.program_id(0)
    rows = q_ref.shape[1]
    length = k_ref.shape[1]
    start = start_ref[0]
    half = LANES // 2
    for h in range(heads):
        c = h // 2 * LANES
        k_scr[h] = pad_head(k_ref[0, :, c : c + LANES].astype(F32), h % 2, 0).astype(BF)
        v_scr[h] = pad_head(v_ref[0, :, c : c + LANES].astype(F32), h % 2, 1).astype(BF)
    dk_scr[...] = jnp.zeros_like(dk_scr)
    dv_scr[...] = jnp.zeros_like(dv_scr)
    lane = lax.broadcasted_iota(jnp.int32, (block_q, LANES), 1)
    key_row = lax.broadcasted_iota(jnp.int32, (block_k, 2 * block_q), 0)
    column = lax.broadcasted_iota(jnp.int32, (1, 2 * block_q), 1) % block_q

    def tail(pair, odd, delta):
        if odd:
            pair = pltpu.roll(pair, half, 1)
        else:
            delta = pltpu.roll(delta, half, 1)
        part0 = delta.astype(BF).astype(F32)
        part1 = (delta - part0).astype(BF).astype(F32)
        part2 = delta - part0 - part1
        rest = jnp.where(
            lane == half, part0, jnp.where(lane == half + 1, part1, jnp.where(lane == half + 2, part2, 0.0))
        )
        return jnp.where(lane < half, pair, -rest)

    def q_step(i, carry):
        at = pl.multiple_of(i * block_q, block_q)
        first = first_ref[0, :, pl.ds(at, block_q)]
        first = jnp.concatenate([first, first], axis=1)
        last = column + (start + at)
        queries, grads = [], []
        for h in range(heads):
            cols = slice(h * LANES, (h + 1) * LANES)
            pair = q_ref[0, pl.ds(at, block_q), cols].astype(F32)
            queries.append(
                jnp.concatenate([pad_head(pair, 0, 0), pad_head(pair, 1, 0)], axis=0).astype(BF)
            )
            pair = do_ref[0, pl.ds(at, block_q), cols].astype(F32)
            delta = de_ref[0, pl.ds(at, block_q), cols]
            grads.append(
                jnp.concatenate([tail(pair, 0, delta), tail(pair, 1, delta)], axis=0).astype(BF)
            )

        def k_step(j, sums):
            key_at = pl.multiple_of(j * block_k, block_k)
            key = key_row + key_at
            live = (key >= first) & (key <= last)
            new = []
            for h in range(heads):
                k = k_scr[h, pl.ds(key_at, block_k), :]
                v = v_scr[h, pl.ds(key_at, block_k), :]
                scores = mm(k, queries[h], NT)
                expo = jnp.where(live, jnp.exp(scores), 0.0)
                change = mm(v, grads[h], NT)
                d_scores = (expo * change).astype(BF)
                dv_scr[h, pl.ds(key_at, block_k), :] += mm(expo.astype(BF), grads[h])
                dk_scr[h, pl.ds(key_at, block_k), :] += mm(d_scores, queries[h])
                new.append(sums[h] + mm(d_scores, k, TN))
            return tuple(new)

        sums = lax.fori_loop(
            low_ref[s, i], high_ref[s, i], k_step,
            tuple(jnp.zeros((2 * block_q, LANES), F32) for _ in range(heads)),
        )
        for h in range(heads):
            even, odd = sums[h][:block_q], sums[h][block_q:]
            cols = slice(h * LANES, (h + 1) * LANES)
            grad = jnp.where(lane < half, even, pltpu.roll(odd, half, 1))
            if more:
                grad += prior_ref[0, pl.ds(at, block_q), cols]
            dq_ref[0, pl.ds(at, block_q), cols] = grad
        return carry

    lax.fori_loop(0, rows // block_q, q_step, 0)
    wide = lax.broadcasted_iota(jnp.int32, (length, LANES), 1)
    for h in range(0, heads, 2):
        cols = slice(h // 2 * LANES, (h // 2 + 1) * LANES)
        for grad, scr in ((dk_ref, dk_scr), (dv_ref, dv_scr)):
            grad[0, :, cols] = jnp.where(
                wide < half, scr[h], pltpu.roll(scr[h + 1], half, 1)
            ).astype(BF)


def attend_back_call(q, d_out, delta, kv, first, keys, block_q, block_k, prior=()):
    seqs, rows, q_width = q.shape
    length = kv.shape[1]
    kv_width = kv.shape[2] // 2
    kv_heads = q_width // LANES
    heads = largest_block(kv_heads, 8)
    steps = kv_heads // heads
    half = LANES // 2
    spec_q = pl.BlockSpec((1, rows, heads * LANES), lambda s, p, *_: (s, 0, p))
    spec_kv = pl.BlockSpec((1, length, heads * half), lambda s, p, *_: (s, 0, p))
    return pl.pallas_call(
        functools.partial(attend_back_kernel, block_q, block_k, heads, bool(prior)),
        grid_spec=pltpu.PrefetchScalarGridSpec(
            num_scalar_prefetch=3,
            grid=(seqs, steps),
            in_specs=[
                spec_q, spec_q, spec_q, spec_kv,
                pl.BlockSpec((1, length, heads * half), lambda s, p, *_: (s, 0, p + steps)),
                pl.BlockSpec((1, 1, rows), lambda s, p, *_: (s, 0, 0)),
            ] + [spec_q] * len(prior),
            out_specs=[spec_q, spec_kv, spec_kv],
            scratch_shapes=[
                pltpu.VMEM((heads, length, LANES), BF),
                pltpu.VMEM((heads, length, LANES), BF),
                pltpu.VMEM((heads, length, LANES), F32),
                pltpu.VMEM((heads, length, LANES), F32),
            ],
        ),
        out_shape=[
            jax.ShapeDtypeStruct(q.shape, F32),
            jax.ShapeDtypeStruct((seqs, length, kv_width), BF),
            jax.ShapeDtypeStruct((seqs, length, kv_width), BF),
        ],
        compiler_params=params(),
        cost_estimate=pl.CostEstimate(
            flops=10 * seqs * rows * length * q_width, bytes_accessed=16 * seqs * rows * q_width,
            transcendentals=0,
        ),
        name="attend_back",
    )(*keys, q, d_out, delta, kv, kv, first[:, None, :], *prior)


def hidden_kernel(a_ref, w_ref, x_ref, g_ref, att_ref, hidden_ref, normed_ref):
    attended = a_ref[...].astype(BF)
    att_ref[...] = attended
    hidden = x_ref[...].astype(F32) + mm(attended, w_ref[...])
    hidden_ref[...] = hidden
    inverse = lax.rsqrt(jnp.mean(hidden * hidden, axis=-1, keepdims=True) + epsilon)
    normed_ref[...] = (hidden * inverse * g_ref[...]).astype(BF)


def hidden_call(mixed, w_o, x, g):
    total, width = x.shape
    q_width = mixed.shape[1]
    block = largest_block(total, 256)

    def rows(n):
        return pl.BlockSpec((block, n), lambda i: (i, 0))

    return pl.pallas_call(
        hidden_kernel,
        grid=(total // block,),
        in_specs=[rows(q_width), resident(w_o.shape), rows(width), resident(g.shape)],
        out_specs=[rows(q_width), rows(width), rows(width)],
        out_shape=[
            jax.ShapeDtypeStruct((total, q_width), BF),
            jax.ShapeDtypeStruct((total, width), F32),
            jax.ShapeDtypeStruct((total, width), BF),
        ],
        compiler_params=params(),
        name="hidden",
    )(mixed, w_o, x, g)


def ffn_block(block_t, n_ref, c_ref, wg, wu, wd, out_ref, dn_ref, act_scr, dg_scr, du_scr):
    total = n_ref.shape[0]

    def t_step(i, carry):
        at = pl.ds(pl.multiple_of(i * block_t, block_t), block_t)
        normed = n_ref[at, :]
        gate = mm(normed, wg())
        up = mm(normed, wu())
        d_act = mm(c_ref[at, :], wd(), NT)
        sig = 1.0 / (1.0 + jnp.exp(-gate))
        silu = gate * sig
        act = (silu * up).astype(BF)
        d_gate = (d_act * up * (sig * (1.0 + gate - silu))).astype(BF)
        d_up = (d_act * silu).astype(BF)
        act_scr[at, :] = act
        dg_scr[at, :] = d_gate
        du_scr[at, :] = d_up
        out_ref[at, :] += mm(act, wd())
        dn_ref[at, :] += mm(d_gate, wg(), NT) + mm(d_up, wu(), NT)
        return carry

    lax.fori_loop(0, total // block_t, t_step, 0, unroll=total // block_t)


def down_grad(gd_ref, act_scr, c_ref):
    for c in range(0, act_scr.shape[1], 256):
        gd_ref[c : c + 256, :] = mm(act_scr[:, c : c + 256], c_ref[...], TN).astype(BF)


def ffn_kernel(
    block_t,
    n_ref, c_ref, wg_ref, wu_ref, wd_ref,
    out_ref, dn_ref, gd_ref, gg_ref, gu_ref,
    n_scr, act_scr, dg_scr, du_scr,
):
    @pl.when(pl.program_id(0) == 0)
    def _():
        n_scr[...] = n_ref[...].T
        out_ref[...] = jnp.zeros_like(out_ref)
        dn_ref[...] = jnp.zeros_like(dn_ref)

    ffn_block(
        block_t, n_ref, c_ref, lambda: wg_ref[...], lambda: wu_ref[...], lambda: wd_ref[...],
        out_ref, dn_ref, act_scr, dg_scr, du_scr,
    )

    def d_step(i, carry):
        at = pl.ds(pl.multiple_of(i * 256, 256), 256)
        normed = n_scr[at, :]
        gg_ref[at, :] = mm(normed, dg_scr[...]).astype(BF)
        gu_ref[at, :] = mm(normed, du_scr[...]).astype(BF)
        return carry

    width = n_ref.shape[1]
    lax.fori_loop(0, width // 256, d_step, 0, unroll=width // 256)
    down_grad(gd_ref, act_scr, c_ref)


def ffn_call(normed, grad_low, w_gate, w_up, w_down):
    total, width = normed.shape
    hidden = w_gate.shape[1]
    chunk = largest_block(hidden, 512)
    block_t = largest_block(total, 256)
    cols = pl.BlockSpec((width, chunk), lambda i: (0, i))
    rows = pl.BlockSpec((chunk, width), lambda i: (i, 0))
    return pl.pallas_call(
        functools.partial(ffn_kernel, block_t),
        grid=(hidden // chunk,),
        in_specs=[resident(normed.shape), resident(normed.shape), cols, cols, rows],
        out_specs=[resident(normed.shape), resident(normed.shape), rows, cols, cols],
        out_shape=[
            jax.ShapeDtypeStruct((total, width), F32),
            jax.ShapeDtypeStruct((total, width), F32),
            jax.ShapeDtypeStruct(w_down.shape, BF),
            jax.ShapeDtypeStruct(w_gate.shape, BF),
            jax.ShapeDtypeStruct(w_gate.shape, BF),
        ],
        scratch_shapes=[
            pltpu.VMEM((width, total), BF),
            pltpu.VMEM((total, chunk), BF),
            pltpu.VMEM((total, chunk), BF),
            pltpu.VMEM((total, chunk), BF),
        ],
        compiler_params=params(),
        name="ffn",
    )(normed, grad_low, w_gate, w_up, w_down)


class ColumnGather:
    def __init__(self, me, own, whole, slots, send, recv, keep_sem, load_sems):
        self.me, self.own, self.whole, self.slots = me, own, whole, slots
        self.sems, self.keep_sem, self.load_sems = (send, recv), keep_sem, load_sems

    def cols(self, k, j=None):
        width = self.slots.shape[-1]
        start = k * width if isinstance(k, int) else pl.multiple_of(k * width, width)
        if j is None:
            return pl.ds(start, width)
        half = width // 2
        start = start + j * half
        return pl.ds(start if isinstance(k, int) else pl.multiple_of(start, half), half)

    def keep(self):
        me = self.me
        return pltpu.make_async_copy(
            self.own, self.whole.at[me.z, me.y, me.c, me.x], self.keep_sem.at[0]
        )

    def hop(self, k, j, s):
        me, every = self.me, slice(None)
        whole = self.whole

        def mine(z, y, c, x):
            return whole.at[z, y, c, x, every, self.cols(k, j)]

        if s == 0:
            give = self.own.at[:, self.cols(k, j)]
            return [
                remote(give, mine(me.z, me.y, me.c, me.x), self.sems, (k, j, d - 1), me.peer(z=me.up(d)))
                for d in (1, 2, 3)
            ]
        to_x, to_y = me.peer(x=1 - me.x), me.peer(y=1 - me.y)
        if s == 1:
            give, peer = mine(every, me.y, me.c, me.x), (to_x if j == 0 else to_y)
        elif s == 2 and j == 0:
            give, peer = mine(every, me.y, me.c, every), to_y
        elif s == 2:
            give, peer = mine(every, every, me.c, me.x), to_x
        else:
            give, peer = mine(every, every, me.c, every), me.peer(c=1 - me.c)
        return [remote(give, give, self.sems, (k, j, 2 + s), peer)]

    def load(self, k):
        every = slice(None)
        slot = k % 2 if isinstance(k, int) else lax.rem(k, 2)
        return pltpu.make_async_copy(
            self.whole.at[every, every, every, every, every, self.cols(k)],
            self.slots.at[slot], self.load_sems.at[slot],
        )

    def start(self, k, s):
        for j in (0, 1):
            for copy in self.hop(k, j, s):
                copy.start()

    def wait(self, k, s):
        for j in (0, 1):
            for copy in self.hop(k, j, s):
                copy.wait()

    def open(self):
        self.keep().start()
        for k in range(3):
            self.start(k, 0)
        self.keep().wait()
        for k, s in ((0, 1), (1, 1), (0, 2), (2, 1), (1, 2), (0, 3), (3, 1), (2, 2), (1, 3), (4, 1), (3, 2), (5, 1)):
            self.wait(k, s - 1)
            self.start(k, s)
            if s == 1:
                self.start(k + 3, 0)
        self.fetch(0)

    def fetch(self, k):
        self.wait(k, 3)
        self.load(k).start()

    def ready(self, k):
        self.load(k).wait()

    def advance(self, step, steps):
        for s, early in ((1, 6), (2, 4), (3, 2)):
            k = step + early

            @pl.when(k < steps)
            def _(k=k, s=s):
                self.wait(k, s - 1)
                self.start(k, s)

        @pl.when(step + 9 < steps)
        def _():
            self.start(step + 9, 0)


class GradSums:
    def __init__(self, me, outs, made, r0, r1, r2, r3, send, recv):
        self.me, self.outs, self.made = me, outs, made
        self.r0, self.r1, self.r2, self.r3, self.send, self.recv = r0, r1, r2, r3, send, recv

    def keep(self, step, i, j, grad):
        slot = lax.rem(step, 2)
        grad = grad.astype(BF)
        share = self.made.shape[-2]
        for y, c, x in itertools.product((0, 1), (0, 1), (0, 1)):
            row = ((y * 2 + c) * 2 + x) * share
            one, two = (x, y) if j == 0 else (y, x)
            self.made[slot, j, c, one, two, i] = grad[row : row + share]

    def axes(self, j):
        me = self.me
        along_x = (me.x, me.peer(x=1 - me.x))
        along_y = (me.y, me.peer(y=1 - me.y))
        return (along_x, along_y) if j == 0 else (along_y, along_x)

    def hop(self, k, j, s):
        me = self.me
        sems = (self.send, self.recv)
        r0, r1, r2, r3 = (r.at[k, j] for r in (self.r0, self.r1, self.r2, self.r3))
        (one, to_one), (two, to_two) = self.axes(j)
        if s == 0:
            give = self.made.at[lax.rem(k, 2), j, 1 - me.c]
            return [remote(give, r0, sems, (k, j, 0), me.peer(c=1 - me.c))]
        if s == 1:
            return [remote(r0.at[1 - one], r1, sems, (k, j, 1), to_one)]
        if s == 2:
            return [remote(r1.at[1 - two], r2, sems, (k, j, 2), to_two)]
        return [
            remote(r2.at[me.up(d)], r3.at[d - 1], sems, (k, j, 2 + d), me.peer(z=me.up(d)))
            for d in (1, 2, 3)
        ]

    def settle(self, k, j, s):
        me = self.me
        r0, r1, r2, r3 = (r.at[k, j] for r in (self.r0, self.r1, self.r2, self.r3))
        (one, _), (two, _) = self.axes(j)
        for copy in self.hop(k, j, s):
            copy.wait()
        if s == 0:
            add_into(r0, self.made.at[lax.rem(k, 2), j, me.c])
        elif s == 1:
            add_into(r1, r0.at[one])
        elif s == 2:
            add_into(r2, r1.at[two])
        else:
            width = r2.shape[-1]
            cols = pl.ds(pl.multiple_of(k * width, width), width)
            self.outs[j][:, cols] = (
                r2[me.z].astype(F32) + r3[0].astype(F32) + r3[1].astype(F32) + r3[2].astype(F32)
            )

    def advance(self, step, steps):
        for s, late in ((3, 4), (2, 3), (1, 2), (0, 1)):
            k = step - late

            @pl.when((k >= 0) & (k < steps))
            def _(s=s, k=k):
                for j in (0, 1):
                    self.settle(k, j, s)
                    if s < 3:
                        for copy in self.hop(k, j, s + 1):
                            copy.start()


def feed_kernel(
    block_t, steps, block_m, head,
    n_ref, c_ref, wg_ref, wd_ref, own_up, h_ref, cot_ref, g_ref, w_ref, o_ref, l_ref, ones_ref,
    gd_ref, gg_ref, gu_ref, all_up, out_ref, dh_ref, low_ref, do_ref, de_ref, gain_ref,
    n_scr, act_scr, dg_scr, du_scr, f_scr, dn_scr, slots, made, r0, r1, r2, r3,
    g_send, g_recv, s_send, s_recv, keep_sems, load_sems,
):
    step = pl.program_id(0)
    me = Place()
    gather = ColumnGather(me, own_up, all_up, slots, g_send, g_recv, keep_sems, load_sems)
    sums = GradSums(me, (gg_ref, gu_ref), made, r0, r1, r2, r3, s_send, s_recv)

    @pl.when(step == 0)
    def _():
        greet(me)
        n_scr[...] = n_ref[...].T
        f_scr[...] = jnp.zeros_like(f_scr)
        dn_scr[...] = jnp.zeros_like(dn_scr)
        gather.open()

    @pl.when(step < steps)
    def _():
        gather.ready(step)
        slot = lax.rem(step, 2)
        width, chunk = n_ref.shape[1], wd_ref.shape[0]
        ffn_block(
            block_t, n_ref, c_ref,
            lambda: wg_ref[...],
            lambda: slots[slot].reshape(width, chunk),
            lambda: wd_ref[...],
            f_scr, dn_scr, act_scr, dg_scr, du_scr,
        )

        @pl.when(step + 1 < steps)
        def _():
            gather.fetch(step + 1)

        for i in range(width // 256):
            normed = n_scr[256 * i : 256 * i + 256, :]
            sums.keep(step, i, 0, mm(normed, dg_scr[...]))
            sums.keep(step, i, 1, mm(normed, du_scr[...]))
        down_grad(gd_ref, act_scr, c_ref)

    gather.advance(step, steps)
    sums.advance(step, steps)

    @pl.when(step < steps)
    def _():
        for j in (0, 1):
            for copy in sums.hop(step, j, 0):
                copy.start()

    @pl.when(step == steps)
    def _():
        gain_ref[...] = jnp.zeros_like(gain_ref)

    @pl.when(step >= steps)
    def _():
        at = pl.ds(pl.multiple_of((step - steps) * block_m, block_m), block_m)
        middle_block(
            head, f_scr[at, :], dn_scr[at, :], h_ref, cot_ref, g_ref, w_ref, o_ref, l_ref, ones_ref,
            out_ref, dh_ref, low_ref, do_ref, de_ref, gain_ref,
        )


def feed_call(
    normed, grad_low, w_gate, w_down, own_up, hidden, cotangent, g, w_o, mixed, totals, ones, head,
    collective,
):
    total, width = normed.shape
    share, units = own_up.shape
    q_width = mixed.shape[1]
    chunk = largest_block(units, 512)
    steps = units // chunk
    block_t, block_m = largest_block(total, 256), largest_block(total, 128)
    last = steps - 1
    piece = (share, chunk)

    def after(n):
        return pl.BlockSpec((block_m, n), lambda i: (jnp.maximum(i - steps, 0), 0))

    anywhere = pl.BlockSpec(memory_space=pl.ANY)
    rows = pl.BlockSpec((chunk, width), lambda i: (jnp.minimum(i, last), 0))
    cols = pl.BlockSpec((width, chunk), lambda i: (0, jnp.minimum(i, last)))
    whole = jax.ShapeDtypeStruct((4, 2, 2, 2, share, units), BF)
    outs = pl.pallas_call(
        functools.partial(feed_kernel, block_t, steps, block_m, head),
        grid=(steps + total // block_m,),
        in_specs=[
            resident(normed.shape), resident(normed.shape), cols, rows, anywhere,
            after(width), after(width), resident(g.shape), resident(w_o.shape), after(q_width),
            after(q_width), resident(ones.shape),
        ],
        out_specs=[
            rows, resident((share, units)), resident((share, units)), anywhere,
            after(width), after(width), after(width), after(q_width), after(q_width),
            resident((1, width)),
        ],
        out_shape=[
            jax.ShapeDtypeStruct(w_down.shape, BF),
            jax.ShapeDtypeStruct((share, units), F32),
            jax.ShapeDtypeStruct((share, units), F32),
            whole,
            jax.ShapeDtypeStruct((total, width), BF),
            jax.ShapeDtypeStruct((total, width), F32),
            jax.ShapeDtypeStruct((total, width), BF),
            jax.ShapeDtypeStruct((total, q_width), BF),
            jax.ShapeDtypeStruct((total, q_width), F32),
            jax.ShapeDtypeStruct((1, width), F32),
        ],
        scratch_shapes=[
            pltpu.VMEM((width, total), BF),
            pltpu.VMEM((total, chunk), BF),
            pltpu.VMEM((total, chunk), BF),
            pltpu.VMEM((total, chunk), BF),
            pltpu.VMEM((total, width), F32),
            pltpu.VMEM((total, width), F32),
            pltpu.VMEM((2, 4, 2, 2, 2) + piece, BF),
            pltpu.VMEM((2, 2, 2, 2, 2, 4) + piece, BF),
            pltpu.VMEM((steps, 2, 2, 2, 4) + piece, BF),
            pltpu.VMEM((steps, 2, 2, 4) + piece, BF),
            pltpu.VMEM((steps, 2, 4) + piece, BF),
            pltpu.VMEM((steps, 2, 3) + piece, BF),
        ]
        + [pltpu.SemaphoreType.DMA((steps, 2, 6))] * 4
        + [pltpu.SemaphoreType.DMA((1,)), pltpu.SemaphoreType.DMA((2,))],
        compiler_params=pltpu.CompilerParams(
            vmem_limit_bytes=62 * 2**20, collective_id=collective, has_side_effects=True
        ),
        cost_estimate=pl.CostEstimate(
            flops=18 * total * width * units, bytes_accessed=12 * width * units, transcendentals=0
        ),
        name="feed",
    )(
        normed, grad_low, w_gate, w_down, own_up, hidden, cotangent, g, w_o, mixed, totals, ones
    )
    return outs[:3] + outs[4:]


def middle_block(
    head, ffn, incoming, h_ref, c_ref, g_ref, w_ref, o_ref, l_ref, ones_ref,
    out_ref, dh_ref, low_ref, do_ref, de_ref, gain_ref,
):
    hidden = h_ref[...]
    out_ref[...] = (hidden + ffn).astype(BF)
    inverse = lax.rsqrt(jnp.mean(hidden * hidden, axis=-1, keepdims=True) + epsilon)
    unit = hidden * inverse
    gain_ref[...] += jnp.sum(unit * incoming, axis=0, keepdims=True)
    scaled = incoming * g_ref[...]
    shared = jnp.mean(unit * scaled, axis=-1, keepdims=True)
    d_hidden = c_ref[...] + inverse * (scaled - unit * shared)
    dh_ref[...] = d_hidden
    low = d_hidden.astype(BF)
    low_ref[...] = low
    ones = ones_ref[...]
    wide = ones.shape[0]
    for c in range(0, o_ref.shape[1], wide):
        cols = slice(c, c + wide)
        d_att = mm(low, w_ref[cols, :], NT)
        ratio = 1.0 / l_ref[:, cols]
        do_ref[:, cols] = (d_att * ratio).astype(BF)
        de_ref[:, cols] = head_sum(d_att * o_ref[:, cols], ones) * ratio


def middle_kernel(head, f_ref, dn_ref, *refs):
    gain_ref = refs[-1]

    @pl.when(pl.program_id(0) == 0)
    def _():
        gain_ref[...] = jnp.zeros_like(gain_ref)

    middle_block(head, f_ref[...], dn_ref[...], *refs)


def middle_call(ffn, d_normed, hidden, cotangent, g, w_o, mixed, totals, ones, head):
    total, width = hidden.shape
    q_width = mixed.shape[1]
    block = largest_block(total, 256)

    def rows(n):
        return pl.BlockSpec((block, n), lambda i: (i, 0))

    return pl.pallas_call(
        functools.partial(middle_kernel, head),
        grid=(total // block,),
        in_specs=[
            rows(width), rows(width), rows(width), rows(width), resident(g.shape),
            resident(w_o.shape), rows(q_width), rows(q_width), resident(ones.shape),
        ],
        out_specs=[
            rows(width), rows(width), rows(width), rows(q_width), rows(q_width), resident((1, width)),
        ],
        out_shape=[
            jax.ShapeDtypeStruct((total, width), BF),
            jax.ShapeDtypeStruct((total, width), F32),
            jax.ShapeDtypeStruct((total, width), BF),
            jax.ShapeDtypeStruct((total, q_width), BF),
            jax.ShapeDtypeStruct((total, q_width), F32),
            jax.ShapeDtypeStruct((1, width), F32),
        ],
        compiler_params=params(),
        name="middle",
    )(ffn, d_normed, hidden, cotangent, g, w_o, mixed, totals, ones)


def head_back(grad, raw, gains, cos, sin, ones, head):
    grad = grad * cos + swap_halves(grad * sin, head)
    inv = lax.rsqrt(head_sum(raw * raw, ones) * (1.0 / head) + epsilon)
    unit = raw * inv
    gained = jnp.sum(unit * grad, axis=0, keepdims=True)
    scaled = grad * gains
    shared = head_sum(unit * scaled, ones) * (1.0 / head)
    return inv * (scaled - unit * shared), sum(
        gained[:, i : i + LANES] for i in range(0, gained.shape[1], LANES)
    )


def last_q_kernel(
    head, scale, dq_ref, raw_ref, gains_ref, cos_ref, sin_ref, ones_ref, w_ref,
    d_ref, part_ref, gq_ref,
):
    @pl.when(pl.program_id(0) == 0)
    def _():
        gq_ref[...] = jnp.zeros_like(gq_ref)

    ones = ones_ref[...]
    wide = ones.shape[0]
    cos, sin = spread(cos_ref[...], wide), spread(sin_ref[...], wide)
    for c in range(0, dq_ref.shape[1], wide):
        cols = slice(c, c + wide)
        grad, gained = head_back(
            dq_ref[:, cols] * scale, raw_ref[:, cols], gains_ref[:, cols], cos, sin, ones, head
        )
        gq_ref[...] += gained
        d_ref[:, cols] = grad.astype(BF)
    part_ref[...] = mm(d_ref[...], w_ref[...], NT)


def last_kernel(
    kv_width, head,
    dk_ref, dv_ref, raw_ref, gains_ref, cos_ref, sin_ref, ones_ref, w_ref, part_ref, x_ref, g_ref,
    dh_ref, *refs,
):
    got_ref = refs[0] if len(refs) == 5 else None
    d_ref, in_ref, gain_ref, gk_ref = refs[-4:]

    @pl.when(pl.program_id(0) == 0)
    def _():
        gain_ref[...] = jnp.zeros_like(gain_ref)
        gk_ref[...] = jnp.zeros_like(gk_ref)

    ones = ones_ref[...]
    wide = ones.shape[0]
    cos, sin = spread(cos_ref[...], wide), spread(sin_ref[...], wide)
    for c in range(0, kv_width, wide):
        cols = slice(c, c + wide)
        grad = dk_ref[:, cols].astype(F32)
        if got_ref is not None:
            grad += got_ref[:, cols].astype(F32)
        grad, gained = head_back(
            grad, raw_ref[:, cols], gains_ref[:, cols], cos, sin, ones, head
        )
        gk_ref[...] += gained
        d_ref[:, cols] = grad.astype(BF)
    d_values = dv_ref[...].astype(F32)
    if got_ref is not None:
        d_values += got_ref[:, kv_width:].astype(F32)
    d_ref[:, kv_width:] = d_values.astype(BF)
    d_normed = part_ref[...] + mm(d_ref[...], w_ref[...], NT)
    x = x_ref[...].astype(F32)
    inverse = lax.rsqrt(jnp.mean(x * x, axis=-1, keepdims=True) + epsilon)
    unit = x * inverse
    gain_ref[...] += jnp.sum(unit * d_normed, axis=0, keepdims=True)
    scaled = d_normed * g_ref[...]
    shared = jnp.mean(unit * scaled, axis=-1, keepdims=True)
    in_ref[...] = dh_ref[...] + inverse * (scaled - unit * shared)


def row_blocks(total):
    block = largest_block(total, 256)
    return total // block, lambda n: pl.BlockSpec((block, n), lambda i: (i, 0))


def some_cols(w, first, count):
    return pl.BlockSpec(
        (w.shape[0], count), lambda i: (0, first // count), pipeline_mode=pl.Buffered(1)
    )


def last_q_call(dq, raw, gains, cos, sin, ones, w, head):
    total, q_width = dq.shape
    width = w.shape[0]
    blocks, rows = row_blocks(total)
    return pl.pallas_call(
        functools.partial(last_q_kernel, head, head ** (-0.5)),
        grid=(blocks,),
        in_specs=[
            rows(q_width), rows(q_width), resident(gains.shape), rows(LANES), rows(LANES),
            resident(ones.shape), some_cols(w, 0, q_width),
        ],
        out_specs=[rows(q_width), rows(width), resident((1, LANES))],
        out_shape=[
            jax.ShapeDtypeStruct((total, q_width), BF),
            jax.ShapeDtypeStruct((total, width), F32),
            jax.ShapeDtypeStruct((1, LANES), F32),
        ],
        compiler_params=params(),
        name="last_q",
    )(dq, raw, gains, cos, sin, ones, w)


def last_call(dk, dv, raw, gains, cos, sin, ones, w, part, x, g, d_hidden, head, got=()):
    total, width = x.shape
    kv_width = dk.shape[1]
    blocks, rows = row_blocks(total)
    return pl.pallas_call(
        functools.partial(last_kernel, kv_width, head),
        grid=(blocks,),
        in_specs=[
            rows(kv_width), rows(kv_width), rows(kv_width), resident(gains.shape), rows(LANES),
            rows(LANES), resident(ones.shape), some_cols(w, w.shape[1] - 2 * kv_width, 2 * kv_width),
            rows(width), rows(width), resident(g.shape), rows(width),
        ] + [rows(2 * kv_width)] * len(got),
        out_specs=[
            rows(2 * kv_width), rows(width), resident((1, width)), resident((1, LANES)),
        ],
        out_shape=[
            jax.ShapeDtypeStruct((total, 2 * kv_width), BF),
            jax.ShapeDtypeStruct((total, width), F32),
            jax.ShapeDtypeStruct((1, width), F32),
            jax.ShapeDtypeStruct((1, LANES), F32),
        ],
        compiler_params=params(),
        name="last",
    )(dk, dv, raw, gains, cos, sin, ones, w, part, x, g, d_hidden, *got)


class Place:
    def __init__(self):
        dp = lax.axis_index("dp")
        self.x = lax.axis_index("ctx")
        self.c = lax.rem(dp, 2)
        self.y = lax.rem(dp // 2, 2)
        self.z = dp // 4

    def peer(self, z=None, y=None, c=None, x=None):
        z = self.z if z is None else z
        y = self.y if y is None else y
        c = self.c if c is None else c
        x = self.x if x is None else x
        return {"dp": (z * 2 + y) * 2 + c, "ctx": x}

    def up(self, d):
        return lax.rem(self.z + d, 4)

    def peers(self):
        return [self.peer(z=self.up(d)) for d in (1, 2, 3)] + [
            self.peer(x=1 - self.x), self.peer(y=1 - self.y), self.peer(c=1 - self.c)
        ]


def greet(place):
    barrier = pltpu.get_barrier_semaphore()
    peers = place.peers()
    for peer in peers:
        pl.semaphore_signal(barrier, inc=1, device_id=peer, device_id_type=pl.DeviceIdType.MESH)
    pl.semaphore_wait(barrier, len(peers))


def remote(src, dst, sems, at, peer):
    send, recv = sems
    return pltpu.make_async_remote_copy(
        src_ref=src, dst_ref=dst, send_sem=send.at[at], recv_sem=recv.at[at],
        device_id=peer, device_id_type=pl.DeviceIdType.MESH,
    )


def gather_kernel(pieces, count, *refs):
    ins, outs = refs[:count], refs[count : 2 * count]
    sems, local = refs[2 * count : 2 * count + 2], refs[2 * count + 2]
    me = Place()
    greet(me)

    def block(p, z, y, c, x):
        array, rows, cols, _ = pieces[p]
        return outs[array].at[z, y, c, x, rows, cols]

    def own(p):
        array, rows, cols, _ = pieces[p]
        return ins[array].at[rows, cols]

    every = slice(None)

    def to_z(p):
        return [
            remote(own(p), block(p, me.z, me.y, me.c, me.x), sems, (p, d - 1), me.peer(z=me.up(d)))
            for d in (1, 2, 3)
        ]

    def keep(p):
        return pltpu.make_async_copy(own(p), block(p, me.z, me.y, me.c, me.x), local.at[p])

    def first(p):
        mine = block(p, every, me.y, me.c, me.x)
        peer = me.peer(x=1 - me.x) if pieces[p][3] else me.peer(y=1 - me.y)
        return [remote(mine, mine, sems, (p, 3), peer)]

    def second(p):
        if pieces[p][3]:
            mine, peer = block(p, every, me.y, me.c, every), me.peer(y=1 - me.y)
        else:
            mine, peer = block(p, every, every, me.c, me.x), me.peer(x=1 - me.x)
        return [remote(mine, mine, sems, (p, 4), peer)]

    def third(p):
        mine = block(p, every, every, me.c, every)
        return [remote(mine, mine, sems, (p, 5), me.peer(c=1 - me.c))]

    n = len(pieces)
    stages = [to_z, first, second, third]
    pair = 2

    def begin(p):
        keep(p).start()
        for copy in to_z(p):
            copy.start()

    for p in range(min(n, AHEAD)):
        begin(p)
    for t in range(0, n + 3 * pair, pair):
        for p in range(t + AHEAD, min(n, t + AHEAD + pair)):
            begin(p)
        for s in (1, 2, 3):
            for p in range(t - (s - 1) * pair, t - (s - 1) * pair + pair):
                if 0 <= p < n:
                    if s == 1:
                        keep(p).wait()
                    for copy in stages[s - 1](p):
                        copy.wait_recv()
                    for copy in stages[s](p):
                        copy.start()
    for p in range(n):
        third(p)[0].wait_recv()
    for p in range(n):
        for stage in stages:
            for copy in stage(p):
                copy.wait_send()


def gather_call(shards, pieces, collective):
    count = len(shards)
    outs = pl.pallas_call(
        functools.partial(gather_kernel, pieces, count),
        in_specs=[pl.BlockSpec(memory_space=pl.ANY)] * count,
        out_specs=[pl.BlockSpec(memory_space=pl.ANY)] * count,
        out_shape=[jax.ShapeDtypeStruct((4, 2, 2, 2) + s.shape, s.dtype) for s in shards],
        scratch_shapes=[
            pltpu.SemaphoreType.DMA((len(pieces), 6)),
            pltpu.SemaphoreType.DMA((len(pieces), 6)),
            pltpu.SemaphoreType.DMA((len(pieces),)),
        ],
        compiler_params=pltpu.CompilerParams(
            collective_id=collective, has_side_effects=True, vmem_limit_bytes=VMEM_LIMIT
        ),
        name="gather",
    )(*shards)
    return [o.reshape(32 * s.shape[0], s.shape[1]) for o, s in zip(outs, shards)]


def add_into(total, more):
    def step(i, carry):
        total[i] = (total[i].astype(F32) + more[i].astype(F32)).astype(total.dtype)
        return carry

    lax.fori_loop(0, total.shape[0], step, 0)


def scatter_kernel(pieces, count, gains, *refs):
    if gains:
        gain_ref, gain_out = refs[count], refs[2 * count + 1]
        sum_scr, got_scr, z_scr, gain_send, gain_recv = refs[-5:]
        refs = refs[:count] + refs[count + 1 : 2 * count + 1] + refs[2 * count + 2 : -5]
    ins, outs = refs[:count], refs[count : 2 * count]
    n = len(pieces)
    shapes, homes = piece_homes(pieces)
    scratch = refs[2 * count : 2 * count + 5 * len(shapes)]
    homes = [
        (scratch[5 * k : 5 * k + 4], i, scratch[5 * k + 4].at[i % OWN], (k, i % OWN)) for k, i in homes
    ]
    sems, local = refs[-3:-1], refs[-1]
    me = Place()
    greet(me)
    every = slice(None)

    def at(p, s):
        return homes[p][0][s].at[homes[p][1]]

    def part(p, c):
        array, rows, cols, _ = pieces[p]
        return ins[array].at[every, every, c, every, rows, cols]

    def load(p):
        return pltpu.make_async_copy(part(p, me.c), homes[p][2], local.at[homes[p][3]])

    def pairs(p):
        return [remote(part(p, 1 - me.c), at(p, 0), sems, (p, 0), me.peer(c=1 - me.c))]

    def first(p):
        if pieces[p][3]:
            give, peer = at(p, 0).at[every, every, 1 - me.x], me.peer(x=1 - me.x)
        else:
            give, peer = at(p, 0).at[every, 1 - me.y], me.peer(y=1 - me.y)
        return [remote(give, at(p, 1), sems, (p, 1), peer)]

    def second(p):
        if pieces[p][3]:
            peer, other = me.peer(y=1 - me.y), 1 - me.y
        else:
            peer, other = me.peer(x=1 - me.x), 1 - me.x
        return [remote(at(p, 1).at[every, other], at(p, 2), sems, (p, 2), peer)]

    def third(p):
        return [
            remote(at(p, 2).at[me.up(d)], at(p, 3).at[d - 1], sems, (p, 2 + d), me.peer(z=me.up(d)))
            for d in (1, 2, 3)
        ]

    stages = [pairs, first, second, third]

    def settle(p, s):
        if s == 0:
            load(p).wait()
            add_into(at(p, 0), homes[p][2])
        elif s == 1:
            kept = at(p, 0).at[every, every, me.x] if pieces[p][3] else at(p, 0).at[every, me.y]
            add_into(at(p, 1), kept)
        elif s == 2:
            add_into(at(p, 2), at(p, 1).at[every, me.y if pieces[p][3] else me.x])
        else:
            array, rows, cols, _ = pieces[p]
            more = at(p, 3)
            outs[array][rows, cols] = (
                at(p, 2)[me.z].astype(F32) + more[0].astype(F32) + more[1].astype(F32) + more[2].astype(F32)
            )

    pair = 2

    def begin(p):
        load(p).start()
        for copy in pairs(p):
            copy.start()

    hops = []
    if gains:
        near = [me.peer(c=1 - me.c), me.peer(x=1 - me.x), me.peer(y=1 - me.y)]
        hops = [
            [remote(sum_scr.at[i], got_scr.at[i], (gain_send, gain_recv), i, peer)]
            for i, peer in enumerate(near)
        ] + [[
            remote(sum_scr.at[3], z_scr.at[me.z], (gain_send, gain_recv), 2 + d, me.peer(z=me.up(d)))
            for d in (1, 2, 3)
        ]]

    def gain_step(i):
        if i == 0:
            sum_scr[0] = gain_ref[...]
        else:
            for copy in hops[i - 1]:
                copy.wait_recv()
            if i < 4:
                sum_scr[i] = sum_scr[i - 1] + got_scr[i - 1]
        if i == 3:
            z_scr[me.z] = sum_scr[3]
        if i < 4:
            for copy in hops[i]:
                copy.start()
        else:
            gain_out[...] = (z_scr[0] + z_scr[1]) + (z_scr[2] + z_scr[3])
            for hop in hops:
                for copy in hop:
                    copy.wait_send()

    for p in range(min(n, AHEAD)):
        begin(p)
    rounds = range(0, n + 3 * pair, pair)
    for t in rounds:
        if gains:
            for i in range(5):
                if i * (len(rounds) - 1) // 4 == t // pair:
                    gain_step(i)
        for s in range(4):
            for p in range(t - s * pair, t - s * pair + pair):
                if 0 <= p < n:
                    for copy in stages[s](p):
                        copy.wait_recv()
                    settle(p, s)
                    if s < 3:
                        for copy in stages[s + 1](p):
                            copy.start()
            if s == 0:
                for p in range(t + AHEAD, min(n, t + AHEAD + pair)):
                    begin(p)
    for p in range(n):
        for stage in stages:
            for copy in stage(p):
                copy.wait_send()


def piece_homes(pieces):
    shapes, homes = [], []
    for _, rows, cols, _ in pieces:
        shape = (rows.stop - rows.start, cols.stop - cols.start)
        if shape not in shapes:
            shapes.append(shape)
        kind = shapes.index(shape)
        homes.append((kind, sum(k == kind for k, _ in homes)))
    return shapes, homes


def scatter_call(grads, pieces, collective, gains=()):
    count = len(grads)
    shards = [(g.shape[0] // 32, g.shape[1]) for g in grads]
    grads = [g.reshape((4, 2, 2, 2) + s) for g, s in zip(grads, shards)]
    shapes, homes = piece_homes(pieces)
    scratch = []
    for kind, shape in enumerate(shapes):
        n = sum(k == kind for k, _ in homes)
        scratch += [
            pltpu.VMEM((n, 4, 2, 2) + shape, BF),
            pltpu.VMEM((n, 4, 2) + shape, BF),
            pltpu.VMEM((n, 4) + shape, BF),
            pltpu.VMEM((n, 3) + shape, BF),
            pltpu.VMEM((OWN, 4, 2, 2) + shape, BF),
        ]
    return pl.pallas_call(
        functools.partial(scatter_kernel, pieces, count, len(gains)),
        in_specs=[pl.BlockSpec(memory_space=pl.ANY)] * count
        + [pl.BlockSpec(memory_space=pltpu.VMEM)] * len(gains),
        out_specs=[pl.BlockSpec(memory_space=pltpu.VMEM)] * (count + len(gains)),
        out_shape=[jax.ShapeDtypeStruct(s, F32) for s in shards]
        + [jax.ShapeDtypeStruct(g.shape, F32) for g in gains],
        scratch_shapes=scratch + [
            pltpu.SemaphoreType.DMA((len(pieces), 6)),
            pltpu.SemaphoreType.DMA((len(pieces), 6)),
            pltpu.SemaphoreType.DMA((len(shapes), OWN)),
        ] + [
            scratch
            for g in gains
            for scratch in (
                pltpu.VMEM((4,) + g.shape, F32),
                pltpu.VMEM((3,) + g.shape, F32),
                pltpu.VMEM((4,) + g.shape, F32),
                pltpu.SemaphoreType.DMA((6,)),
                pltpu.SemaphoreType.DMA((6,)),
            )
        ],
        compiler_params=pltpu.CompilerParams(
            collective_id=collective, has_side_effects=True, vmem_limit_bytes=VMEM_LIMIT
        ),
        name="scatter",
    )(*grads, *gains)


def col_pieces(array, rows, cols, width=256, high=None):
    high = high or rows
    return [
        (array, slice(r, r + high), slice(c, c + width), (c // width) % 2 == 0)
        for r in range(0, rows, high)
        for c in range(0, cols, width)
    ]


def interleave(one, two):
    return [p for pair in zip(one, two) for p in pair]


def per_device(
    tokens, segments, cotangent, w_q, w_k, w_v, w_o, w_gate, w_up, w_down, g_attn, g_q, g_k, g_ffn
):
    seqs, rows, width = tokens.shape
    length = segments.shape[1]
    head = g_q.shape[0]
    q_width, kv_width = w_q.shape[1], w_k.shape[1]
    kv_heads = kv_width // head
    q_heads = q_width // head
    total = seqs * rows
    row_start = lax.axis_index("ctx") * rows
    own_kernels = (lax.axis_size("dp"), lax.axis_size("ctx")) == (16, 2)
    share = w_q.shape[0]

    def fetch(weight):
        return lax.all_gather(weight, AXES, axis=0, tiled=True)

    def send(grad):
        return lax.psum_scatter(grad, AXES, scatter_dimension=0, tiled=True).astype(F32)

    seg_rows = lax.dynamic_slice_in_dim(segments, row_start, rows, 1)
    first = jnp.sum((segments[:, None, :] < seg_rows[:, :, None]).astype(jnp.int32), axis=-1)
    query_pos = row_start + jnp.arange(rows, dtype=jnp.int32)
    positions = (query_pos[None, :] - first).reshape(total)
    frequency = rope_base ** (-jnp.arange(0, head, 2, dtype=F32) / head)
    angles = positions.astype(F32)[:, None] * frequency[None, :]
    cos, sin = jnp.cos(angles), jnp.sin(angles)
    cos = jnp.concatenate([cos] * (2 * LANES // head), axis=1)
    sin = jnp.concatenate([-sin, sin] * (LANES // head), axis=1)
    wide = 2 * LANES
    member = jnp.arange(wide) // head
    ones = (member[:, None] == member[None, :]).astype(BF)
    gains_q = jnp.concatenate([g_q] * q_heads)[None, :]
    gains_k = jnp.concatenate([g_k] * kv_heads)[None, :]
    x = tokens.reshape(total, width)
    cotangent = cotangent.reshape(total, width)

    w_qkv = jnp.concatenate([w_q, w_k, w_v], axis=1)
    w_down, w_gate = fetch(w_down), fetch(w_gate)
    grad_low = cotangent.astype(BF)
    if own_kernels:
        qkv_pieces = col_pieces(0, share, w_qkv.shape[1])
        o_pieces = col_pieces(0, share, w_o.shape[1])
        [w_qkv] = gather_call([w_qkv], qkv_pieces, 0)
    else:
        w_qkv, w_o = fetch(w_qkv), fetch(w_o)
        w_up = fetch(w_up)

    tables = (cos, sin, ones, head)
    normed, kv, raw_k = project_call(
        x, w_qkv, (q_width, 2 * kv_width), kv_width, g_attn[None, :], gains_k, *tables, None, "project_kv"
    )
    kv = kv.reshape(seqs, rows, 2 * kv_width)
    if own_kernels:
        before = lax.ppermute(kv, "ctx", [(0, 1)])
    _, q, raw_q = project_call(
        x, w_qkv, (0, q_width), q_width, g_attn[None, :], gains_q, *tables, head ** (-0.5), "project_q"
    )
    q = q.reshape(seqs, rows, q_width)
    block_q, block_k = min(256, rows), min(256, length)
    at = jnp.arange(0, rows, block_q, dtype=jnp.int32)[None, :]
    lowest = first[:, ::block_q]
    zero = jnp.zeros((1,), jnp.int32)
    if own_kernels:
        own_first = first - row_start
        own_keys = (
            jnp.maximum(lowest - row_start, 0) // block_k,
            jnp.broadcast_to((at + block_q - 1) // block_k + 1, lowest.shape),
            zero,
        )
        far_first = own_first + rows
        far_keys = (
            jnp.clip(lowest - row_start + rows, 0, rows) // block_k,
            jnp.full(lowest.shape, rows // block_k, jnp.int32),
            zero + rows,
        )
        near = attend_call(q, kv, own_first, own_keys, block_q, block_k, last_part=False)
        w_o, _ = lax.optimization_barrier((w_o, near))
        [w_o] = gather_call([w_o], [p[:3] + (True,) for p in o_pieces], 4)
        mixed, totals = attend_call(q, before, far_first, far_keys, block_q, block_k, near)
    else:
        kv = lax.all_gather(kv, "ctx", axis=1, tiled=True)
        all_keys = (
            lowest // block_k,
            jnp.broadcast_to((row_start + at + block_q - 1) // block_k + 1, lowest.shape),
            zero + row_start,
        )
        mixed, totals = attend_call(q, kv, first, all_keys, block_q, block_k)
    mixed, totals = mixed.reshape(total, q_width), totals.reshape(total, q_width)
    attended, hidden, normed_two = hidden_call(mixed, w_o, x, g_ffn[None, :])

    middle_args = (hidden, cotangent, g_ffn[None, :], w_o, mixed, totals, ones, head)
    if own_kernels:
        grad_down, out_gate, out_up, outputs, d_hidden, d_low, d_out, delta, grad_gffn = feed_call(
            normed_two, grad_low, w_gate, w_down, w_up, *middle_args, 2
        )
    else:
        ffn, d_normed_two, grad_down, out_gate, out_up = ffn_call(
            normed_two, grad_low, w_gate, w_up, w_down
        )
        out_gate, out_up = send(out_gate), send(out_up)
        outputs, d_hidden, d_low, d_out, delta, grad_gffn = middle_call(
            ffn, d_normed_two, *middle_args
        )
    out_down = send(grad_down)
    d_out, delta = d_out.reshape(q.shape), delta.reshape(q.shape)
    if own_kernels:
        far_dq, dk, dv = attend_back_call(
            q, d_out, delta, before, far_first, far_keys, block_q, block_k
        )
        got = lax.ppermute(jnp.concatenate([dk, dv], axis=2), "ctx", [(1, 0)])
        dq, dk, dv = attend_back_call(
            q, d_out, delta, kv, own_first, own_keys, block_q, block_k, (far_dq,)
        )
        dk, dv, got = dk.reshape(total, kv_width), dv.reshape(total, kv_width), (got.reshape(total, -1),)
    else:
        dq, dk, dv = attend_back_call(q, d_out, delta, kv, first, all_keys, block_q, block_k)
        dkv = lax.psum_scatter(
            jnp.concatenate([dk, dv], axis=2), "ctx", scatter_dimension=1, tiled=True
        ).reshape(total, 2 * kv_width)
        dk, dv, got = dkv[:, :kv_width], dkv[:, kv_width:], ()
    grad_o = mm(attended, d_low, TN).astype(BF)
    d_q, part, grad_gq = last_q_call(
        dq.reshape(total, q_width), raw_q, gains_q, cos, sin, ones, w_qkv, head
    )
    grad_q = mm(normed, d_q, TN).astype(BF)
    if own_kernels:
        got, grad_q, part, grad_o = lax.optimization_barrier((got, grad_q, part, grad_o))
    d_kv, input_grad, grad_gattn, grad_gk = last_call(
        dk, dv, raw_k, gains_k, cos, sin, ones, w_qkv, part, x, g_attn[None, :], d_hidden, head, got
    )
    grad_kv = mm(normed, d_kv, TN).astype(BF)
    if own_kernels:
        flat = jnp.concatenate([grad_gattn, grad_gffn, grad_gq, grad_gk], axis=1).reshape(-1, LANES)
        flat = jnp.pad(flat, ((0, -flat.shape[0] % 8), (0, 0)))
        last_pieces = [
            (array,) + p[1:] for array, width_of in enumerate((width, q_width, 2 * kv_width))
            for p in col_pieces(array, share, width_of)
        ]
        out_o, out_q, out_kv, flat = scatter_call([grad_o, grad_q, grad_kv], last_pieces, 3, (flat,))
        flat = flat.reshape(1, -1)
        grad_gattn, grad_gffn = flat[:, :width], flat[:, width : 2 * width]
        grad_gq = flat[:, 2 * width : 2 * width + LANES]
        grad_gk = flat[:, 2 * width + LANES : 2 * width + 2 * LANES]
    else:
        out_q, out_kv, out_o = send(grad_q), send(grad_kv), send(grad_o)
        grad_gattn, grad_gffn, grad_gq, grad_gk = lax.psum(
            (grad_gattn, grad_gffn, grad_gq, grad_gk), AXES
        )

    def fold(grad):
        return jnp.sum(grad.reshape(LANES // head, head), axis=0)

    return (
        outputs.reshape(tokens.shape),
        input_grad.reshape(tokens.shape),
        out_q,
        out_kv[:, :kv_width],
        out_kv[:, kv_width:],
        out_o,
        out_gate,
        out_up,
        out_down,
        grad_gattn[0],
        fold(grad_gq),
        fold(grad_gk),
        grad_gffn[0],
    )


def solution(mesh):
    split = P("dp", "ctx", None)
    shard = P(("dp", "ctx"), None)
    in_specs = (split, P("dp", None), split) + (shard,) * 7 + (P(),) * 4
    out_specs = (split, split) + (shard,) * 7 + (P(),) * 4
    return jax.shard_map(
        per_device, mesh=mesh, in_specs=in_specs, out_specs=out_specs, check_vma=False
    )
```
